512 devices in a mesh: gx: 16 (over z), gy: 4 (over x), gz: 8 (over y, core).
Axes of the slice: x: 4, y: 4, z: 16, core: 2. Of those that a mesh axis runs over, the one named last changes fastest.
Arguments:
- right_side: float32 [256, 128, 1024], P('gx', 'gy', 'gz'), may hold values from -24 to 24
- conductivity: float32 [256, 128, 1024], P('gx', 'gy', 'gz'), may hold values from 0.1 to 10
Outputs:
- solution: float32 [256, 128, 1024], P('gx', 'gy', 'gz')
- residual: float32 [256, 128, 1024], P('gx', 'gy', 'gz')
The draws below stay inside these ranges and needn't reach their ends.
All inputs are finite; a program needn't handle non-finite values.
Results may differ from the reference program's by a relative error of at most 0.0004.
Values sent between devices are 32-bit elements; how exact they have to be, the bound alone decides.
No kernel may reach another device: no remote copies, remote signals or barrier semaphores. Data moves between devices by JAX's collectives and lax.ppermute only.
A program may use at most 128 MiB of HBM per device.

```python
import math
import jax
import jax.numpy as jnp
from jax import lax

LEVELS = 4
CYCLES = 2
CSWEEPS = 6
NX = 256
NY = 128
NZ = 1024


def draw_right_side(key, part):
    rough = 4.0 * jax.random.normal(key, (NX, NY, NZ), jnp.float32)
    return jnp.clip(rough, -24.0, 24.0)


def shard_levels(key, shape, cuts, low, largest):
    def one(position, shards_of):
        steps = jax.random.uniform(jax.random.fold_in(jax.random.fold_in(key, 6), position), (shards_of,), jnp.float32, low / len(cuts), largest / len(cuts))
        return jnp.repeat(jnp.exp(steps), shape[position] // shards_of).reshape((-1,) + (1,) * (len(shape) - position - 1))

    level = one(*cuts[0])
    for cut in cuts[1:]:
        level = level * one(*cut)
    return level


def setup_inputs(seed: int = 0) -> dict:
    arg_keys = jax.random.split(jax.random.key(seed), 3)
    right_side = draw_right_side(jax.random.fold_in(arg_keys[2], 71), 0)
    conductivity = jnp.clip(jnp.exp(math.log(10.0) - 4.6051702 * jax.random.uniform(arg_keys[1], (NX, NY, NZ), jnp.float32) ** shard_levels(arg_keys[1], (NX, NY, NZ), ((0, 16), (1, 4), (2, 8)), -0.2, 0.2)), 0.1, 10.0)
    return dict(right_side=right_side, conductivity=conductivity)


absorption = 0.01
relaxation = 0.8


def six_views(padded):
    return [padded[2:, 1:-1, 1:-1], padded[:-2, 1:-1, 1:-1],
            padded[1:-1, 2:, 1:-1], padded[1:-1, :-2, 1:-1],
            padded[1:-1, 1:-1, 2:], padded[1:-1, 1:-1, :-2]]


def operator_parts(field, padded, kpadded, factor):
    center = kpadded[1:-1, 1:-1, 1:-1]
    total = None
    weight_sum = None
    for kother, fother in zip(six_views(kpadded), six_views(padded)):
        weight = 0.5 * (center + kother)
        term = weight * (field - fother)
        total = term if total is None else total + term
        weight_sum = weight if weight_sum is None else weight_sum + weight
    return factor * total + absorption * field, factor * weight_sum + absorption


def diagonal_only(kpadded, factor):
    center = kpadded[1:-1, 1:-1, 1:-1]
    weight_sum = None
    for kother in six_views(kpadded):
        weight = 0.5 * (center + kother)
        weight_sum = weight if weight_sum is None else weight_sum + weight
    return factor * weight_sum + absorption


def coarsen(values):
    values = 0.5 * (values[0::2] + values[1::2])
    values = 0.5 * (values[:, 0::2] + values[:, 1::2])
    return 0.5 * (values[:, :, 0::2] + values[:, :, 1::2])


def restrict_dim(padded, along):
    count = padded.shape[along] - 2
    first = lax.slice_in_dim(padded, 0, count, 2, along)
    second = lax.slice_in_dim(padded, 1, count + 1, 2, along)
    third = lax.slice_in_dim(padded, 2, count + 2, 2, along)
    fourth = lax.slice_in_dim(padded, 3, count + 2, 2, along)
    return (first + 3.0 * second + 3.0 * third + fourth) * 0.125


def prolong_dim(padded, along):
    count = padded.shape[along] - 2
    middle = lax.slice_in_dim(padded, 1, count + 1, 1, along)
    lower = lax.slice_in_dim(padded, 0, count, 1, along)
    upper = lax.slice_in_dim(padded, 2, count + 2, 1, along)
    even = (3.0 * middle + lower) * 0.25
    odd = (3.0 * middle + upper) * 0.25
    both = jnp.stack([even, odd], axis=along + 1)
    shape = list(middle.shape)
    shape[along] = 2 * count
    return both.reshape(shape)


def reference(right_side, conductivity):
    coefficient_pads = []
    values = conductivity
    for level in range(LEVELS + 1):
        coefficient_pads.append(jnp.pad(values, 1))
        if level < LEVELS:
            values = coarsen(values)

    def sweep(field, source, level):
        image, diagonal = operator_parts(field, jnp.pad(field, 1), coefficient_pads[level], 0.25 ** level)
        return field + relaxation * (source - image) / diagonal

    def first_sweep(source, level):
        return relaxation * source / diagonal_only(coefficient_pads[level], 0.25 ** level)

    def restrict(residual_field):
        result = restrict_dim(jnp.pad(residual_field, 1), 0)
        result = restrict_dim(result, 1)
        return restrict_dim(result, 2)

    def prolong(coarse_field):
        result = prolong_dim(jnp.pad(coarse_field, 1), 0)
        result = prolong_dim(result, 1)
        return prolong_dim(result, 2)

    def cycle(level, source, field):
        if field is None:
            field = first_sweep(source, level)
        else:
            field = sweep(field, source, level)
        image, diagonal = operator_parts(field, jnp.pad(field, 1), coefficient_pads[level], 0.25 ** level)
        coarse_source = restrict(source - image)
        if level + 1 == LEVELS:
            correction = first_sweep(coarse_source, LEVELS)
            for turn in range(CSWEEPS - 1):
                correction = sweep(correction, coarse_source, LEVELS)
        else:
            correction = cycle(level + 1, coarse_source, None)
        field = field + prolong(correction)
        return sweep(field, source, level)

    solution = cycle(0, right_side, None)
    for turn in range(CYCLES - 1):
        solution = cycle(0, right_side, solution)
    image, diagonal = operator_parts(solution, jnp.pad(solution, 1), coefficient_pads[0], 1.0)
    return solution, right_side - image
```

```python
import jax
import jax.numpy as jnp
from jax import lax
from jax.sharding import PartitionSpec as P

LEVELS = 4
CSWEEPS = 6
absorption = 0.01
relaxation = 0.8
AXES = ("gx", "gy", "gz")
HI = lax.Precision.HIGHEST


def neighbours(last, initial, axis):
    count = lax.axis_size(axis)
    if axis == "gz":
        up = [(i, (i + 1) % count) for i in range(count)]
    else:
        up = [(i, i + 1) for i in range(count - 1)]
    down = [(j, i) for i, j in up]
    before = lax.ppermute(last, axis, up)
    after = lax.ppermute(initial, axis, down)
    if axis == "gz":
        at = lax.axis_index(axis)
        before = jnp.where(at == 0, 0.0, before)
        after = jnp.where(at == count - 1, 0.0, after)
    return before, after


def exchange(fields, width):
    for axis, dim in (("gz", 2), ("gy", 1), ("gx", 0)):
        along = 2 if dim == 2 else 0
        size = fields[0].shape[dim]
        last = [lax.slice_in_dim(f, size - width, size, axis=dim) for f in fields]
        initial = [lax.slice_in_dim(f, 0, width, axis=dim) for f in fields]
        before, after = neighbours(
            jnp.concatenate(last, along), jnp.concatenate(initial, along), axis
        )
        before = jnp.split(before, len(fields), along)
        after = jnp.split(after, len(fields), along)
        fields = [
            jnp.concatenate([b, f, a], dim) for b, f, a in zip(before, fields, after)
        ]
    return fields


def crop(values, width):
    if width == 0:
        return values
    return values[width:-width, width:-width, width:-width]


def inside(block, width):
    mask = None
    for dim, axis in enumerate(AXES):
        at = lax.axis_index(axis) * block[dim] - width
        cells = at + jnp.arange(block[dim] + 2 * width)
        one = (cells >= 0) & (cells < lax.axis_size(axis) * block[dim])
        one = one.astype(jnp.float32).reshape([-1 if d == dim else 1 for d in range(3)])
        mask = one if mask is None else mask * one
    return mask


def six_views(padded):
    return [
        padded[2:, 1:-1, 1:-1],
        padded[:-2, 1:-1, 1:-1],
        padded[1:-1, 2:, 1:-1],
        padded[1:-1, :-2, 1:-1],
        padded[1:-1, 1:-1, 2:],
        padded[1:-1, 1:-1, :-2],
    ]


def image(padded, kpadded, factor):
    center, field = kpadded[1:-1, 1:-1, 1:-1], padded[1:-1, 1:-1, 1:-1]
    total = None
    for kother, fother in zip(six_views(kpadded), six_views(padded)):
        term = 0.5 * (center + kother) * (field - fother)
        total = term if total is None else total + term
    return factor * total + absorption * field


def step_of(kpadded, factor):
    center = kpadded[1:-1, 1:-1, 1:-1]
    total = None
    for kother in six_views(kpadded):
        weight = 0.5 * (center + kother)
        total = weight if total is None else total + weight
    return relaxation / (factor * total + absorption)


def restriction(count):
    fine = jnp.arange(count + 2)[:, None] - 2 * jnp.arange(count // 2)[None, :]
    outer = (fine == 0) | (fine == 3)
    inner = (fine == 1) | (fine == 2)
    return jnp.where(outer, 0.125, jnp.where(inner, 0.375, 0.0)).astype(jnp.float32)


def halving(count):
    fine = jnp.arange(count)[:, None] // 2 == jnp.arange(count // 2)[None, :]
    return jnp.where(fine, 0.5, 0.0).astype(jnp.float32)


def prolongation(count):
    fine = jnp.arange(2 * count - 2)[None, :]
    coarse = jnp.arange(count)[:, None]
    near = coarse == (fine + 1) // 2
    far = coarse == fine // 2 + (fine + 1) % 2
    return jnp.where(near, 0.75, jnp.where(far, 0.25, 0.0)).astype(jnp.float32)


def coarsen(values):
    values = 0.5 * (values[0::2] + values[1::2])
    values = 0.5 * (values[:, 0::2] + values[:, 1::2])
    return jnp.dot(values, halving(values.shape[2]), precision=HI)


def restrict_dim(padded, along):
    count = padded.shape[along] - 2
    first = lax.slice_in_dim(padded, 0, count, 2, along)
    second = lax.slice_in_dim(padded, 1, count + 1, 2, along)
    third = lax.slice_in_dim(padded, 2, count + 2, 2, along)
    fourth = lax.slice_in_dim(padded, 3, count + 2, 2, along)
    return (first + 3.0 * second + 3.0 * third + fourth) * 0.125


def restrict(padded):
    result = restrict_dim(restrict_dim(padded, 0), 1)
    return jnp.dot(result, restriction(padded.shape[2] - 2), precision=HI)


def prolong_dim(values, along):
    count = values.shape[along]
    lower = lax.slice_in_dim(values, 0, count - 1, 1, along)
    upper = lax.slice_in_dim(values, 1, count, 1, along)
    both = [(3.0 * lower + upper) * 0.25, (3.0 * upper + lower) * 0.25]
    shape = list(values.shape)
    shape[along] = 2 * count - 2
    return jnp.stack(both, axis=along + 1).reshape(shape)


def prolong(values):
    result = jnp.dot(values, prolongation(values.shape[2]), precision=HI)
    return prolong_dim(prolong_dim(result, 0), 1)


def gathered(fields):
    block = fields[0].shape
    count = len(fields)
    piece = jnp.stack([f.reshape(-1) for f in fields])
    nx, ny, nz = (lax.axis_size(axis) for axis in AXES)
    piece = lax.all_to_all(jnp.broadcast_to(piece[None], (nx,) + piece.shape), "gx", 0, 0)
    piece = lax.all_gather(piece, "gy")
    piece = lax.all_gather(piece, "gz")
    piece = piece.reshape((nz, ny, nx, count) + block)
    piece = piece.transpose(3, 2, 4, 1, 5, 0, 6)
    return list(piece.reshape(count, nx * block[0], ny * block[1], nz * block[2]))


def body(right_side, conductivity):
    blocks = [tuple(n >> level for n in right_side.shape) for level in range(LEVELS + 1)]
    factors = [0.25**level for level in range(LEVELS + 1)]
    ring = lambda values: jnp.pad(values, 1)

    source0, k0 = exchange([right_side, conductivity], 5)
    source0 = crop(source0, 1)
    k = [k0]
    step = [step_of(k0, 1.0) * inside(blocks[0], 4)]
    coarse_k = coarsen(crop(k0, 1))
    k3 = None

    def down(level, field, source, width):
        trimmed = crop(field, width - 2)
        kk = crop(k[level], (k[level].shape[0] - blocks[level][0]) // 2 - 2)
        residual = crop(source, width - 1) - image(trimmed, kk, factors[level])
        return restrict(residual * inside(blocks[level], 1))

    def smooth(level, field, source, width):
        kk = crop(k[level], (k[level].shape[0] - blocks[level][0]) // 2 - width)
        ss = crop(step[level], (step[level].shape[0] - blocks[level][0]) // 2 - width + 1)
        return crop(field, 1) + (source - image(field, kk, factors[level])) * ss

    def coarsest(source3):
        kp3, kp4 = k[3], k[4]
        field = source3 * step[3]
        residual = source3 - image(ring(field), kp3, factors[3])
        source4 = restrict(ring(residual))
        error = source4 * step[4]
        for turn in range(CSWEEPS - 1):
            error = error + (source4 - image(ring(error), kp4, factors[4])) * step[4]
        field = field + crop(prolong(ring(error)), 1)
        return field + (source3 - image(ring(field), kp3, factors[3])) * step[3]

    def window(values, width):
        values = jnp.pad(values, width)
        starts = [lax.axis_index(a) * b for a, b in zip(AXES, blocks[3])]
        return lax.dynamic_slice(values, starts, [b + 2 * width for b in blocks[3]])

    def up(level, field, error, source, width):
        finer = prolong(error)
        have = (finer.shape[0] - blocks[level][0]) // 2
        field = (field + crop(finer, have - width)) * inside(blocks[level], width)
        return smooth(level, field, crop(source, 1), width)

    def cycle(first, field, halo):
        source = [crop(source0, 4 - halo)]
        fields = [field]
        nonlocal coarse_k
        w = 4 if first else 3
        for level in (0, 1):
            g = down(level, fields[level], source[level], halo if level == 0 else w)
            if first:
                kk = coarse_k
                st = step_of(crop(kk, 0), factors[level + 1])
                g, kk, st = exchange([g, crop(kk, 2), crop(st, 1)], 4)
                k.append(kk)
                step.append(st)
                coarse_k = coarsen(kk)
            else:
                (g,) = exchange([g], 3)
            source.append(g)
            fields.append(g * crop(step[level + 1], 4 - w))
        g = down(2, fields[2], source[2], w)
        if first:
            g, whole = gathered([g, crop(coarse_k, 2)])
            k.append(ring(whole))
            k.append(ring(coarsen(whole)))
            step.append(step_of(k[3], factors[3]))
            step.append(step_of(k[4], factors[4]))
        else:
            (g,) = gathered([g])
        error = window(coarsest(g), 3 if first else 2)
        error = up(2, fields[2], error, source[2], w)
        error = up(1, fields[1], error, source[1], w)
        return up(0, fields[0], error, source[0], halo)

    field = source0 * step[0]
    field = cycle(True, field, 4)
    field = smooth(0, field, crop(source0, 2), 3)
    field = cycle(False, field, 2)
    residual = right_side - image(field, crop(k0, 4), 1.0)
    return crop(field, 1), residual


def solution(mesh):
    placed = P("gx", "gy", "gz")
    return jax.shard_map(
        body, mesh=mesh, in_specs=(placed, placed), out_specs=(placed, placed), check_vma=False
    )
```

```python
import functools

import jax
import jax.numpy as jnp
import numpy as np
from jax import lax
from jax.experimental import pallas as pl
from jax.experimental.pallas import tpu as pltpu
from jax.sharding import PartitionSpec as P

LEVELS = 4
CSWEEPS = 6
absorption = 0.01
relaxation = 0.8
F32 = jnp.float32


def coords(n, b):
    at = np.arange(n)
    return np.where(at < (n + b) // 2, at, at - n)


def restriction(coarse, fine):
    gap = fine[None, :] - 2 * coarse[:, None]
    outer, inner = (gap == -1) | (gap == 2), (gap == 0) | (gap == 1)
    return np.where(outer, 0.125, np.where(inner, 0.375, 0.0)).astype(np.float32)


def halving(coarse, fine):
    return np.where(fine[None, :] // 2 == coarse[:, None], 0.5, 0.0).astype(np.float32)


def prolongation(fine, coarse):
    near = fine[:, None] // 2 == coarse[None, :]
    far = fine[:, None] // 2 + 2 * (fine[:, None] % 2) - 1 == coarse[None, :]
    return np.where(near, 0.75, np.where(far, 0.25, 0.0)).astype(np.float32)


def dot(a, b):
    return lax.dot_general(
        a, b, (((1,), (0,)), ((), ())),
        precision=lax.Precision.HIGHEST, preferred_element_type=F32,
    )


def planes(lo, hi, step, carry=0, unroll=1):
    whole = (hi - lo) // unroll

    def body(turn, carry):
        for j in range(unroll):
            carry = step(lo + turn * unroll + j, carry)
        return carry

    if whole > 1:
        carry = lax.fori_loop(0, whole, body, carry)
    elif whole == 1:
        carry = body(0, carry)
    for i in range(lo + whole * unroll, hi):
        carry = step(i, carry)
    return carry


class Open:
    def above(self, v, dim):
        return pltpu.roll(v, v.shape[dim] - 1, dim)

    def below(self, v, dim):
        return pltpu.roll(v, 1, dim)

    def closed(self, k):
        return None


class Closed(Open):
    def __init__(self, shape, counts):
        self.last, self.first = [], []
        for dim in range(2):
            at = lax.broadcasted_iota(jnp.int32, shape, dim)
            self.last.append(jnp.where(at == counts[dim] - 1, 0.0, 1.0))
            self.first.append(jnp.where(at == 0, 0.0, 1.0))

    def above(self, v, dim):
        return super().above(v, dim) * self.last[dim]

    def below(self, v, dim):
        return super().below(v, dim) * self.first[dim]

    def closed(self, k):
        return k * ((1.0 - self.first[0]) + (1.0 - self.first[1]))


def weigh(k, wx, wy, wz, lo, hi, factor, shifts, d=None, mask=None, b=None, unroll=1):
    half = 0.5 * factor
    first = half * (k[lo - 1] + k[lo])
    wx[lo - 1] = first

    def step(i, below):
        here = k[i]
        x = half * (here + k[i + 1])
        y = half * (here + shifts.above(here, 0))
        z = half * (here + shifts.above(here, 1))
        wx[i], wy[i], wz[i] = x, y, z
        ends = shifts.closed(half * here)
        if ends is not None:
            b[i] = ends
        if d is not None:
            total = (x + below) + (y + shifts.below(y, 0)) + (z + shifts.below(z, 1))
            if ends is not None:
                total = total + ends
            d[i] = mask(here, relaxation / (total + absorption))
        return x

    planes(lo, hi, step, first, unroll)


def image(v, wx, wy, wz, lo, hi, use, shifts, b=None, unroll=1):
    def step(i, below):
        here = v[i]
        x = wx[i] * (here - v[i + 1])
        y = wy[i] * (here - shifts.above(here, 0))
        z = wz[i] * (here - shifts.above(here, 1))
        total = (x - below) + (y - shifts.below(y, 0)) + (z - shifts.below(z, 1))
        if b is not None:
            total = total + b[i] * here
        use(i, here, total + absorption * here)
        return x

    planes(lo, hi, step, wx[lo - 1] * (v[lo - 1] - v[lo]), unroll)


def smooth(v, f, d, w, lo, hi, shifts, b=None, unroll=1):
    def use(i, here, im):
        v[i] = here + d[i] * (f[i] - im)

    image(v, *w, lo, hi, use, shifts, b, unroll)


def residual_of(v, f, r, w, lo, hi, shifts, mask=None, b=None, unroll=1):
    def use(i, here, im):
        value = f[i] - im
        r[i] = value if mask is None else jnp.where(mask[i] > 0.0, value, 0.0)

    image(v, *w, lo, hi, use, shifts, b, unroll)


def restrict_x(r, offset, count, rows):
    for i in range(count):
        at = 2 * i + offset
        outer, inner = r[at - 1] + r[at + 2], r[at] + r[at + 1]
        rows(i, 0.125 * outer + 0.375 * inner)


def restrict(r, offset, count, ry, rz, held):
    size = ry.shape[0]

    def rows(i, plane):
        held[i * size : (i + 1) * size, :] = dot(ry[...], plane)

    restrict_x(r, offset, count, rows)
    return dot(held[: count * size, :], rz[...])


def halve(k, offset, lo, hi, cy, cz, put):
    for i in range(lo, hi):
        plane = 0.5 * (k[2 * i + offset] + k[2 * i + 1 + offset])
        put(i, dot(dot(cy[...], plane), cz[...]))


def prolong(e, first, count, py, pz, finer, use):
    rows, fine = e.shape[1], py.shape[0]
    spread = dot(e[pl.ds(first, count)].reshape(count * rows, e.shape[2]), pz)
    for i in range(count):
        finer[i] = dot(py, spread[i * rows : (i + 1) * rows])

    def step(i, carry):
        below, here, above = finer[i - 1], finer[i], finer[i + 1]
        use(2 * (i - 1), 0.75 * here + 0.25 * below)
        use(2 * (i - 1) + 1, 0.75 * here + 0.25 * above)
        return carry

    planes(1, count - 1, step)


def inside(k, value):
    return jnp.where(k > 0.0, value, 0.0)


def down0(f, k, ry, rz, cy, cz, wx, wy, wz, d, g1, k1, d1, v, r, held, kc, wc):
    shifts = Open()
    weigh(k, wx, wy, wz, 1, 25, 1.0, shifts, d, inside)

    def start(i, carry):
        v[i] = f[i] * d[i]
        return carry

    planes(1, 25, start)
    residual_of(v, f, r, (wx, wy, wz), 4, 22, shifts, k)
    g1[...] = restrict(r, 5, 8, ry, rz, held).reshape(g1.shape)

    def put(i, value):
        kc[i + 1] = value

    halve(k, 5, -1, 9, cy, cz, put)
    coarse(kc, wc, k1, d1, 8, 0.25, shifts)


def coarse(kc, wc, kn, dn, count, factor, shifts):
    rows = kn.shape[1]
    dd = wc.at[3]
    weigh(kc, wc.at[0], wc.at[1], wc.at[2], 1, count + 1, factor, shifts, dd, lambda k, value: value)
    for i in range(count):
        kn[i] = kc[i + 1, :rows]
        dn[i] = dd[i + 1, :rows]


def start_level(g, k, d, v, w, factor):
    count, shifts = g.shape[0], Open()
    weigh(k, *w, 1, count - 1, factor, shifts, unroll=2)

    def start(i, carry):
        v[i] = g[i] * d[i]
        return carry

    planes(0, count, start, unroll=4)


def down(level, first, *refs):
    factor, shifts = 0.25**level, Open()
    block = 16 >> level
    g, k, d = refs[:3]
    if first:
        ry, rz, cy, cz, gn, kn, dn, v, r, held, w, kc, wc = refs[3:]
    else:
        ry, rz, gn, v, r, held, w = refs[3:]
    w = tuple(w.at[i] for i in range(3))
    start_level(g, k, d, v, w, factor)
    residual_of(v, g, r, w, 3, block + 5, shifts, d, unroll=2)
    gn[...] = restrict(r, 4, block // 2, ry, rz, held).reshape(gn.shape)
    if first:

        def put(i, value):
            kc[i + 1] = value

        halve(k, 4, -1, block // 2 + 1, cy, cz, put)
        coarse(kc, wc, kn, dn, block // 2, factor * 0.25, shifts)


def down2(first, *refs):
    g, k, d, ry, rz = refs[:5]
    if first:
        cy, cz = refs[5:7]
    gn, v, r, held, w = refs[-5:]
    w = tuple(w.at[i] for i in range(3))
    start_level(g, k, d, v, w, 0.25**2)
    residual_of(v, g, r, w, 3, 9, Open(), d, unroll=2)

    def rows(i, plane):
        held[i] = dot(ry[i], plane)

    restrict_x(r, 4, 2, rows)
    gn[0] = dot(held[0] + held[1], rz[...])
    if first:
        part = [dot(cy[i], 0.5 * (k[2 * i + 4] + k[2 * i + 5])) for i in range(2)]
        gn[1] = dot(part[0] + part[1], cz[...])


def repack(s, out):
    for field in range(s.shape[1]):
        total = s[0, field]
        for i in range(1, s.shape[0]):
            total = total + pltpu.roll(s[i, field], 16 * i, 1)
        for i in range(out.shape[0]):
            out[i, field] = total


def bottom(s, k3, scratch, mats):
    g3, v3, r3, w3, d3, b3, k4, g4, v4, w4, d4, b4, held, fine4 = scratch
    ry3, rz3, cy3, cz3, py3, pz3 = mats[:6]
    ny, nx = s.shape[:2]
    n3, n4 = 2 * nx, nx
    rows, lanes = g3.shape[1], g3.shape[2]
    for ref in (v3, r3, k4, v4):
        ref[...] = jnp.zeros(ref.shape, F32)
    for j in range(ny):
        for i in range(nx):
            for x in range(2):
                g3[2 * i + x + 3, 4 * j : 4 * j + 4] = s[j, i, 0, 4 * x : 4 * x + 4]
                if s.shape[2] == 2:
                    k3[2 * i + x + 3, 4 * j : 4 * j + 4] = s[j, i, 1, 4 * x : 4 * x + 4]
    if s.shape[2] == 2:
        for i in (0, 1, 2, n3 + 3, n3 + 4, n3 + 5):
            k3[i] = jnp.zeros((rows, lanes), F32)

    def put(i, value):
        k4[i + 1] = value

    halve(k3, 3, 0, n4, cy3, cz3, put)
    used = mats[6]
    shifts3 = Closed((rows, lanes), (rows, used))
    shifts4 = Closed((k4.shape[1], lanes), (k4.shape[1], used // 2))
    w3 = tuple(w3.at[i] for i in range(3))
    w4 = tuple(w4.at[i] for i in range(3))
    weigh(k3, *w3, 3, n3 + 3, 0.25**3, shifts3, d3, inside, b3, unroll=4)
    weigh(k4, *w4, 1, n4 + 1, 0.25**4, shifts4, d4, inside, b4, unroll=4)

    def start3(i, carry):
        v3[i] = g3[i] * d3[i]
        return carry

    planes(3, n3 + 3, start3, unroll=4)
    residual_of(v3, g3, r3, w3, 3, n3 + 3, shifts3, b=b3, unroll=4)
    g4[...] = restrict(r3, 3, n4, ry3, rz3, held).reshape(g4.shape)

    def start4(i, carry):
        v4[i + 1] = g4[i] * d4[i + 1]
        return carry

    planes(0, n4, start4, unroll=4)

    def turn(j, carry):
        def use(i, here, im):
            v4[i] = here + d4[i] * (g4[i - 1] - im)

        image(v4, *w4, 1, n4 + 1, use, shifts4, b4, unroll=n4)
        return carry

    lax.fori_loop(0, CSWEEPS - 1, turn, 0)

    def use(i, value):
        v3[i + 3] = v3[i + 3] + value

    prolong(v4, 0, n4 + 2, py3[...], pz3[...], fine4, use)
    smooth(v3, g3, d3, w3, 3, n3 + 3, shifts3, b3, unroll=4)
    return v3


def spread_matrix(shape, dim_fine, coarse_start, block_fine):
    fine = lax.broadcasted_iota(jnp.int32, shape, dim_fine)
    size = shape[dim_fine]
    fine = jnp.where(fine < (size + block_fine) // 2, fine, fine - size)
    whole = lax.broadcasted_iota(jnp.int32, shape, 1 - dim_fine)
    near = (fine >> 1) + coarse_start
    far = near + 2 * (fine & 1) - 1
    return jnp.where(whole == near, 0.75, jnp.where(whole == far, 0.25, 0.0))


def upward(index, e3, g2, k2, d2, g1, k1, d1, scratch, mats):
    v2, w2, v1, w1, fine2, fine1 = scratch
    py1, pz1 = mats
    shifts = Open()
    w2 = tuple(w2.at[i] for i in range(3))
    w1 = tuple(w1.at[i] for i in range(3))
    start_level(g2, k2, d2, v2, w2, 0.25**2)
    start_level(g1, k1, d1, v1, w1, 0.25)

    def use2(i, value):
        v2[i] = jnp.where(d2[i] > 0.0, v2[i] + value, 0.0)

    py2 = spread_matrix((g2.shape[1], e3.shape[1]), 0, index[1] * 4, 8)
    pz2 = spread_matrix((e3.shape[2], g2.shape[2]), 1, index[2] * 16, 32)
    prolong(e3, index[0] * 2, 8, py2, pz2, fine2, use2)
    smooth(v2, g2, d2, w2, 1, 11, shifts, unroll=2)

    def use1(i, value):
        v1[i] = jnp.where(d1[i] > 0.0, v1[i] + value, 0.0)

    prolong(v2, 1, 10, py1[...], pz1[...], fine1, use1)
    smooth(v1, g1, d1, w1, 1, 15, shifts, unroll=2)
    return v1


BOTTOM = 14
UP = 6


def middle(used, index, s, g2, k2, d2, g1, k1, d1, f, wx, wy, wz, d, k, *refs):
    m3, (py1, pz1, py0, pz0, ry, rz) = refs[:6] + (used,), refs[6:12]
    v, gn, k3 = refs[12:15]
    low, mid, (fine0, r, held0) = refs[15 : 15 + BOTTOM], refs[15 + BOTTOM : 15 + BOTTOM + UP], refs[15 + BOTTOM + UP :]
    e3 = bottom(s, k3, low, m3)
    e1 = upward(index, e3, g2, k2, d2, g1, k1, d1, mid, (py1, pz1))
    w, shifts = (wx, wy, wz), Open()

    def use(i, value):
        v[i + 1] = inside(k[i + 1], f[i + 1] * d[i + 1] + value)

    prolong(e1, 1, 14, py0[...], pz0[...], fine0, use)
    smooth(v, f, d, w, 2, 24, shifts)
    smooth(v, f, d, w, 3, 23, shifts)
    residual_of(v, f, r, w, 4, 22, shifts, k)
    gn[...] = restrict(r, 5, 8, ry, rz, held0).reshape(gn.shape)


def final(used, index, s, g2, k2, d2, g1, k1, d1, f, wx, wy, wz, d, k, *refs):
    m3, (py1, pz1, py0, pz0) = refs[:6] + (used,), refs[6:10]
    k3, v0, solution_, residual_ = refs[10:14]
    low, mid, (fine0, v) = refs[14 : 14 + BOTTOM], refs[14 + BOTTOM : 14 + BOTTOM + UP], refs[14 + BOTTOM + UP :]
    e3 = bottom(s, k3, low, m3)
    e1 = upward(index, e3, g2, k2, d2, g1, k1, d1, mid, (py1, pz1))
    w, shifts = (wx, wy, wz), Open()

    def use(i, value):
        v[i + 3] = inside(k[i + 3], v0[i + 3] + value)

    prolong(e1, 2, 12, py0[...], pz0[...], fine0, use)
    smooth(v, f, d, w, 4, 22, shifts)

    def out(i, here, im):
        solution_[i - 5] = here[:32, :128]
        residual_[i - 5] = (f[i] - im)[:32, :128]

    image(v, *w, 5, 21, out, shifts)


def call(kernel, outs, scratch, *args, name, scalars=0):
    vmem = pl.BlockSpec(memory_space=pltpu.VMEM)
    smem = pl.BlockSpec(memory_space=pltpu.SMEM)
    return pl.pallas_call(
        kernel,
        out_shape=[jax.ShapeDtypeStruct(o, F32) for o in outs],
        in_specs=[smem] * scalars + [vmem] * (len(args) - scalars),
        out_specs=[vmem] * len(outs),
        scratch_shapes=[pltpu.VMEM(s, F32) for s in scratch],
        compiler_params=pltpu.CompilerParams(vmem_limit_bytes=48 << 20),
        name=name,
    )(*args)


def neighbours(last, initial, axis):
    count = lax.axis_size(axis)
    if axis == "gz":
        up = [(i, (i + 1) % count) for i in range(count)]
    else:
        up = [(i, i + 1) for i in range(count - 1)]
    down = [(j, i) for i, j in up]
    before = lax.ppermute(last, axis, up)
    after = lax.ppermute(initial, axis, down)
    if axis == "gz":
        at = lax.axis_index(axis)
        before = jnp.where(at == 0, 0.0, before)
        after = jnp.where(at == count - 1, 0.0, after)
    return before, after


def exchange(fields, block, sizes, width):
    count = len(fields)
    for axis, dim in (("gz", 2), ("gy", 1), ("gx", 0)):
        along = 2 if dim == 2 else 0
        size = block[dim]
        last = [lax.slice_in_dim(f, size - width, size, axis=dim) for f in fields]
        initial = [lax.slice_in_dim(f, 0, width, axis=dim) for f in fields]
        before, after = neighbours(
            jnp.concatenate(last, along), jnp.concatenate(initial, along), axis
        )
        before = jnp.split(before, count, along)
        after = jnp.split(after, count, along)
        if dim == 0:
            fields = [jnp.concatenate([b, f, a], 0) for b, f, a in zip(before, fields, after)]
            continue
        own = [lax.slice_in_dim(f, 0, size, axis=dim) for f in fields]
        gap = list(own[0].shape)
        gap[dim] = sizes[dim - 1] - size - 2 * width
        parts = [[jnp.zeros(gap, F32)] if gap[dim] else []] * count
        fields = [
            jnp.concatenate([f, a] + z + [b], dim)
            for b, f, a, z in zip(before, own, after, parts)
        ]
    return fields


def gathered(piece):
    count = piece.shape[0]
    nx = lax.axis_size("gx")
    pieces = lax.all_gather(piece, "gz")
    (pieces,) = call(repack, [(nx, count, 8, 128)], [], pieces, name="repack")
    pieces = lax.all_to_all(pieces, "gx", 0, 0)
    return lax.all_gather(pieces, "gy")


def body(right_side, conductivity):
    nx, ny, nz = (lax.axis_size(axis) for axis in ("gx", "gy", "gz"))
    index = jnp.stack([lax.axis_index(axis) for axis in ("gx", "gy", "gz")]).astype(jnp.int32)
    y0, z0 = coords(48, 32), coords(256, 128)
    y1, z1 = coords(24, 16), coords(128, 64)
    y2, z2 = coords(16, 8), coords(128, 32)
    far = np.full(128, -1000)

    def ends(count):
        at = far.copy()
        at[:count] = np.arange(count)
        return at

    ry0, rz0 = restriction(np.arange(16), y0), restriction(ends(64), z0).T
    cy0, cz0 = halving(y1, y0), halving(z1, z0).T
    ry1, rz1 = restriction(np.arange(8), y1), restriction(ends(32), z1).T
    cy1, cz1 = halving(y2, y1), halving(z2, z1).T

    def both(matrix):
        zero = np.zeros_like(matrix)
        return np.stack([np.concatenate([matrix, zero]), np.concatenate([zero, matrix])])

    ry2, rz2 = both(restriction(np.arange(4), y2)), restriction(ends(16), z2).T
    cy2, cz2 = both(halving(np.arange(4), y2)), halving(ends(16), z2).T
    py0, pz0 = prolongation(y0, y1), prolongation(z0, z1).T
    py1, pz1 = prolongation(y1, y2), prolongation(z1, z2).T
    rows3, rows4, lanes3 = np.arange(4 * ny), np.arange(2 * ny), ends(16 * nz)
    lanes4 = np.where(ends(8 * nz) < 0, -5000, ends(8 * nz))
    ry3, rz3 = restriction(rows4, rows3), restriction(lanes4, lanes3).T
    cy3, cz3 = halving(rows4, rows3), halving(lanes4, lanes3).T
    py3, pz3 = prolongation(rows3, rows4), prolongation(lanes3, lanes4).T
    m3 = (ry3, rz3, cy3, cz3, py3, pz3)

    wide, l1, l2 = (26, 48, 256), (16, 24, 128), (12, 16, 128)
    n3, n4 = (2 * nx + 6, 4 * ny, 128), (nx + 2, 2 * ny, 128)
    low = [
        n3, n3, n3, (3,) + n3, n3, n3,
        n4, (nx, 2 * ny, 128), n4, (3,) + n4, n4, n4,
        (nx * 2 * ny, 128), (nx + 2, 4 * ny, 128),
    ]
    mid = [l2, (3,) + l2, l1, (3,) + l1, (8, 16, 128), (10, 24, 128)]

    f, k = exchange([right_side, conductivity], (16, 32, 128), (48, 256), 5)
    b1, b2 = (8, 16, 128), (4, 8, 128)
    wx, wy, wz, d, g1, k1, d1 = call(
        down0, [wide] * 4 + [b1] * 3,
        [wide, wide, (128, 256), (10, 24, 128), (4, 10, 24, 128)],
        f, k, ry0, rz0, cy0, cz0, name="down0",
    )
    g1, k1, d1 = exchange([g1, k1, d1], (8, 16, 64), (24, 128), 4)
    inner1 = [l1, l1, (32, 128), (3,) + l1]
    g2, k2, d2 = call(
        functools.partial(down, 1, True), [b2] * 3,
        inner1 + [(6, 16, 128), (4, 6, 16, 128)],
        g1, k1, d1, ry1, rz1, cy1, cz1, name="down1",
    )
    g2, k2, d2 = exchange([g2, k2, d2], (4, 8, 32), (16, 128), 4)
    inner2 = [l2, l2, (2, 8, 128), (3,) + l2]
    (piece,) = call(
        functools.partial(down2, True), [(2, 8, 128)], inner2,
        g2, k2, d2, ry2, rz2, cy2, cz2, name="down2",
    )
    s = gathered(piece)
    fields = (f, wx, wy, wz, d, k)
    v, g1b, k3 = call(
        functools.partial(middle, 16 * nz), [wide, b1, n3],
        low + mid + [(14, 48, 256), wide, (128, 256)],
        index, s, g2, k2, d2, g1, k1, d1, *fields, *m3, py1, pz1, py0, pz0, ry0, rz0,
        name="middle", scalars=1,
    )
    (g1,) = exchange([g1b], (8, 16, 64), (24, 128), 4)
    (g2b,) = call(
        functools.partial(down, 1, False), [b2], inner1, g1, k1, d1, ry1, rz1, name="again1"
    )
    (g2,) = exchange([g2b], (4, 8, 32), (16, 128), 4)
    (piece,) = call(
        functools.partial(down2, False), [(1, 8, 128)], inner2, g2, k2, d2, ry2, rz2, name="again2"
    )
    s = gathered(piece)
    return tuple(call(
        functools.partial(final, 16 * nz), [(16, 32, 128)] * 2,
        low + mid + [(12, 48, 256), wide],
        index, s, g2, k2, d2, g1, k1, d1, *fields, *m3, py1, pz1, py0, pz0, k3, v,
        name="final", scalars=1,
    ))


def solution(mesh):
    placed = P("gx", "gy", "gz")
    return jax.shard_map(
        body, mesh=mesh, in_specs=(placed, placed), out_specs=(placed, placed), check_vma=False
    )
```

```python
import functools

import jax
import jax.numpy as jnp
import numpy as np
from jax import lax
from jax.experimental import pallas as pl
from jax.experimental.pallas import tpu as pltpu
from jax.sharding import PartitionSpec as P

LEVELS = 4
CSWEEPS = 6
absorption = 0.01
relaxation = 0.8
F32 = jnp.float32


def coords(n, b):
    at = np.arange(n)
    return np.where(at < (n + b) // 2, at, at - n)


def restriction(coarse, fine):
    gap = fine[None, :] - 2 * coarse[:, None]
    outer, inner = (gap == -1) | (gap == 2), (gap == 0) | (gap == 1)
    return np.where(outer, 0.125, np.where(inner, 0.375, 0.0)).astype(np.float32)


def halving(coarse, fine):
    return np.where(fine[None, :] // 2 == coarse[:, None], 0.5, 0.0).astype(np.float32)


def prolongation(fine, coarse):
    near = fine[:, None] // 2 == coarse[None, :]
    far = fine[:, None] // 2 + 2 * (fine[:, None] % 2) - 1 == coarse[None, :]
    return np.where(near, 0.75, np.where(far, 0.25, 0.0)).astype(np.float32)


def dot(a, b):
    return lax.dot_general(
        a, b, (((1,), (0,)), ((), ())),
        precision=lax.Precision.HIGHEST, preferred_element_type=F32,
    )


def planes(lo, hi, step, carry=0, unroll=1):
    whole = (hi - lo) // unroll
    if whole > 1:
        carry = lax.fori_loop(0, whole, lambda t, c: step(lo + t * unroll, unroll, c), carry)
    elif whole == 1:
        carry = step(lo, unroll, carry)
    rest = (hi - lo) % unroll
    return step(hi - rest, rest, carry) if rest else carry


class Open:
    def above(self, v, dim):
        return pltpu.roll(v, v.shape[dim] - 1, dim)

    def below(self, v, dim):
        return pltpu.roll(v, 1, dim)

    def closed(self, k):
        return None


class Closed(Open):
    def __init__(self, shape, counts):
        self.last, self.first = [], []
        for dim in range(2):
            at = lax.broadcasted_iota(jnp.int32, shape, dim)
            self.last.append(jnp.where(at == counts[dim] - 1, 0.0, 1.0))
            self.first.append(jnp.where(at == 0, 0.0, 1.0))

    def above(self, v, dim):
        return super().above(v, dim) * self.last[dim]

    def below(self, v, dim):
        return super().below(v, dim) * self.first[dim]

    def closed(self, k):
        return k * ((1.0 - self.first[0]) + (1.0 - self.first[1]))


def weigh(k, wx, wy, wz, lo, hi, factor, shifts, d=None, mask=None, b=None, unroll=1):
    half = 0.5 * factor
    first = half * (k[lo - 1] + k[lo])
    wx[lo - 1] = first

    def step(i, n, below):
        here = [k[i + j] for j in range(n + 1)]
        outs = []
        for j in range(n):
            x = half * (here[j] + here[j + 1])
            y = half * (here[j] + shifts.above(here[j], 0))
            z = half * (here[j] + shifts.above(here[j], 1))
            ends, value = shifts.closed(half * here[j]), None
            if d is not None:
                value = (x + below) + (y + shifts.below(y, 0)) + (z + shifts.below(z, 1))
                if ends is not None:
                    value = value + ends
                value = relaxation / (value + absorption)
                if mask is not None:
                    value = mask(here[j], value)
            outs.append((x, y, z, ends, value))
            below = x
        for j, (x, y, z, ends, value) in enumerate(outs):
            wx[i + j], wy[i + j], wz[i + j] = x, y, z
            if ends is not None:
                b[i + j] = ends
            if value is not None:
                d[i + j] = value
        return below

    planes(lo, hi, step, first, unroll)


def image(v, wx, wy, wz, lo, hi, use, put, shifts, b=None, unroll=1):
    def step(i, n, below):
        here = [v[i + j] for j in range(n + 1)]
        outs = []
        for j in range(n):
            x = wx[i + j] * (here[j] - here[j + 1])
            y = wy[i + j] * (here[j] - shifts.above(here[j], 0))
            z = wz[i + j] * (here[j] - shifts.above(here[j], 1))
            total = (x - below) + (y - shifts.below(y, 0)) + (z - shifts.below(z, 1))
            if b is not None:
                total = total + b[i + j] * here[j]
            outs.append(use(i + j, here[j], total + absorption * here[j]))
            below = x
        for j, value in enumerate(outs):
            put(i + j, value)
        return below

    planes(lo, hi, step, wx[lo - 1] * (v[lo - 1] - v[lo]), unroll)


def into(ref, by=0):
    def put(i, value):
        ref[i + by] = value

    return put


def smooth(v, f, d, w, lo, hi, shifts, b=None, unroll=1, by=0):
    def use(i, here, im):
        return here + d[i] * (f[i + by] - im)

    image(v, *w, lo, hi, use, into(v), shifts, b, unroll)


def residual_of(v, f, r, w, lo, hi, shifts, mask=None, b=None, unroll=1):
    def use(i, here, im):
        value = f[i] - im
        return value if mask is None else jnp.where(mask[i] > 0.0, value, 0.0)

    image(v, *w, lo, hi, use, into(r), shifts, b, unroll)


def first_sweep(g, d, v, lo, hi, unroll, by=0):
    def step(i, n, carry):
        values = [g[i + j + by] * d[i + j] for j in range(n)]
        for j, value in enumerate(values):
            v[i + j] = value
        return carry

    planes(lo, hi, step, unroll=unroll)


def restrict(r, offset, lo, hi, ry, rz, held):
    size = ry.shape[0]
    for i in range(lo, hi):
        at = 2 * i + offset
        plane = 0.125 * (r[at - 1] + r[at + 2]) + 0.375 * (r[at] + r[at + 1])
        held[(i - lo) * size : (i - lo + 1) * size, :] = dot(ry[...], plane)
    return dot(held[: (hi - lo) * size, :], rz[...])


def halve(k, offset, lo, hi, cy, cz, held):
    size = cy.shape[0]
    for i in range(lo, hi):
        plane = 0.5 * (k[2 * i + offset] + k[2 * i + 1 + offset])
        held[(i - lo) * size : (i - lo + 1) * size, :] = dot(cy[...], plane)
    return dot(held[: (hi - lo) * size, :], cz[...])


def prolong(e, first, count, py, pz, finer, use):
    rows = e.shape[1]
    spread = dot(e[pl.ds(first, count)].reshape(count * rows, e.shape[2]), pz)
    for i in range(count):
        finer[i] = dot(py, spread[i * rows : (i + 1) * rows])

    def step(i, n, carry):
        below, here, above = finer[i - 1], finer[i], finer[i + 1]
        use(2 * (i - 1), 0.75 * here + 0.25 * below)
        use(2 * (i - 1) + 1, 0.75 * here + 0.25 * above)
        return carry

    planes(1, count - 1, step)


def three(w):
    return tuple(w.at[i] for i in range(3))


def inside(k, value):
    return jnp.where(k > 0.0, value, 0.0)


U0, U1, U2, U3 = 2, 4, 2, 4


def down0(f, k, ry, rz, cy, cz, wx, wy, wz, d, g1, k1, d1, v, r, held, kc, wc):
    shifts = Open()
    weigh(k, wx, wy, wz, 1, 25, 1.0, shifts, d, inside, unroll=U0)
    first_sweep(f, d, v, 1, 25, U0)
    residual_of(v, f, r, (wx, wy, wz), 4, 22, shifts, k, unroll=U0)
    g1[...] = restrict(r, 5, 0, 8, ry, rz, held).reshape(g1.shape)
    kc[...] = halve(k, 5, -1, 9, cy, cz, held).reshape(kc.shape)
    coarse(kc, wc, 8, 0.25)
    for i in range(8):
        k1[i] = kc[i + 1, :16]
        d1[i] = wc[3, i + 1, :16]


def coarse(kc, wc, count, factor):
    weigh(kc, *three(wc), 1, count + 1, factor, Open(), wc.at[3], unroll=U1)


def tile_of(values):
    total = None
    for i, value in enumerate(values):
        if value is None:
            continue
        lane = lax.broadcasted_iota(jnp.int32, value.shape, 1)
        part = jnp.where(lane < 32, value, 0.0)
        part = pltpu.roll(part, 32 * i, 1) if i else part
        total = part if total is None else total + part
    return total


def down1(first, *refs):
    shifts = Open()
    g, k, d, ry, rz = refs[:5]
    if first:
        cy, cz, out, v, r, held, w, kc, wc = refs[5:]
    else:
        out, v, r, held, w = refs[5:]
    w = three(w)
    weigh(k, *w, 1, 23, 0.25, shifts, unroll=U1)
    first_sweep(g, d, v, 0, 24, U1)
    if first:
        residual_of(v, g, r, w, 7, 17, shifts, d, unroll=U1)
        value = restrict(r, 8, 0, 4, ry, rz, held).reshape(4, 8, 128)
        kc[...] = halve(k, 8, -1, 5, cy, cz, held).reshape(kc.shape)
        coarse(kc, wc, 4, 0.25**2)
        tiles = [
            tile_of([value[i] for i in range(4)]),
            tile_of([kc[i + 1, :8] for i in range(4)]),
            tile_of([wc[3, i + 1, :8] for i in range(4)]),
        ]
    else:
        residual_of(v, g, r, w, 1, 23, shifts, d, unroll=U1)
        value = restrict(r, 8, -3, 7, ry, rz, held).reshape(10, 8, 128)
        tiles = [
            tile_of([None] + [value[i] for i in range(3)]),
            tile_of([value[i + 3] for i in range(4)]),
            tile_of([value[i + 7] for i in range(3)]),
        ]
    for i in range(out.shape[0]):
        for t in range(3):
            out[i, t] = tiles[t]


def unpack(s, t, nz, put):
    lane = lax.broadcasted_iota(jnp.int32, (8, 128), 1) // 32
    for j in range(s.shape[0] // nz):
        for x in range(4):
            for half in range(2):
                total = jnp.zeros((8, 128), F32)
                for q in range(4):
                    if half * 4 + q < nz:
                        part = s[j * nz + half * 4 + q, t]
                        if q != x:
                            part = pltpu.roll(part, (32 * (q - x)) % 128, 1)
                        total = jnp.where(lane == q, part, total)
                put(x, pl.ds(8 * j, 8), pl.ds(128 * half, 128), total)


def arrange(nz, s, out):
    for t in range(3):

        def put(x, rows, lanes, value):
            out[t, x, rows, lanes] = value

        unpack(s, t, nz, put)


def closed2(shape, nz):
    return Closed(shape, (shape[0], 32 * nz))


def down2(nz, first, *refs):
    if first:
        before, own, after, ry, rz, cy, cz, out, g, k, d, v, r, held, w, b = refs
        for part, at in ((before, 0), (own, 4), (after, 8)):
            for ref, field in ((g, 0), (k, 1), (d, 2)):
                for i in range(4):
                    ref[at + i] = part[field, i]
    else:
        s, k, d, ry, rz, out, g, v, r, held, w, b = refs
        for t in range(3):

            def put(x, rows, lanes, value):
                g[4 * t + x, rows, lanes] = value

            unpack(s, t, nz, put)
    shifts, w = closed2(g.shape[1:], nz), three(w)
    weigh(k, *w, 3, 9, 0.25**2, shifts, b=b, unroll=U2)
    first_sweep(g, d, v, 2, 10, U2)
    residual_of(v, g, r, w, 3, 9, shifts, d, b, unroll=U2)
    value = restrict(r, 4, 0, 2, ry, rz, held)
    rows = ry.shape[0]
    parts = [value]
    if first:
        parts.append(halve(k, 4, 0, 2, cy, cz, held))
    for i in range(out.shape[0]):
        for j, part in enumerate(parts):
            for x in range(2):
                out[i, j, x] = part[x * rows : (x + 1) * rows]


def bottom(nz, s, k3, scratch, mats):
    g3, v3, r3, w3, d3, b3, k4, g4, v4, w4, d4, b4, held, fine4 = scratch
    ry3, rz3, cy3, cz3, py3, pz3 = mats
    nx = s.shape[0]
    n3, n4 = 2 * nx, nx
    rows, lanes = g3.shape[1], g3.shape[2]
    zero = jnp.zeros((rows, lanes), F32)
    for i in (0, 1, 2, n3 + 3, n3 + 4, n3 + 5):
        v3[i], r3[i] = zero, zero
        if s.shape[1] == 2:
            k3[i] = zero
    for ref in (k4, v4):
        for i in (0, n4 + 1):
            ref[i] = jnp.zeros(ref.shape[1:], F32)
    for i in range(nx):
        for x in range(2):
            g3[2 * i + x + 3] = s[i, 0, x]
            if s.shape[1] == 2:
                k3[2 * i + x + 3] = s[i, 1, x]
    k4[1 : n4 + 1] = halve(k3, 3, 0, n4, cy3, cz3, held).reshape(g4.shape)
    shifts3 = Closed((rows, lanes), (rows, 16 * nz))
    shifts4 = Closed((k4.shape[1], lanes), (k4.shape[1], 8 * nz))
    w3, w4 = three(w3), three(w4)
    weigh(k3, *w3, 3, n3 + 3, 0.25**3, shifts3, d3, inside, b3, U3)
    weigh(k4, *w4, 1, n4 + 1, 0.25**4, shifts4, d4, inside, b4, U3)
    first_sweep(g3, d3, v3, 3, n3 + 3, U3)
    residual_of(v3, g3, r3, w3, 3, n3 + 3, shifts3, b=b3, unroll=U3)
    g4[...] = restrict(r3, 3, 0, n4, ry3, rz3, held).reshape(g4.shape)
    first_sweep(g4, d4, v4, 1, n4 + 1, U3, by=-1)

    def turn(j, carry):
        smooth(v4, g4, d4, w4, 1, n4 + 1, shifts4, b4, n4, by=-1)
        return carry

    lax.fori_loop(0, CSWEEPS - 1, turn, 0)

    def use(i, value):
        v3[i + 3] = v3[i + 3] + value

    prolong(v4, 0, n4 + 2, py3[...], pz3[...], fine4, use)
    smooth(v3, g3, d3, w3, 3, n3 + 3, shifts3, b3, U3)
    return v3


def spread_matrix(shape, dim_fine, coarse_start, block_fine):
    fine = lax.broadcasted_iota(jnp.int32, shape, dim_fine)
    size = shape[dim_fine]
    fine = jnp.where(fine < (size + block_fine) // 2, fine, fine - size)
    whole = lax.broadcasted_iota(jnp.int32, shape, 1 - dim_fine)
    near = (fine >> 1) + coarse_start
    far = near + 2 * (fine & 1) - 1
    return jnp.where(whole == near, 0.75, jnp.where(whole == far, 0.25, 0.0))


def upward(nz, index, e3, g2, k2, d2, g1, k1, d1, scratch, mats):
    v2, w2, b2, v1, w1, fine2, fine1 = scratch
    py2, pz2 = mats
    open_, closed, w2, w1 = Open(), closed2(g2.shape[1:], nz), three(w2), three(w1)
    weigh(k2, *w2, 1, 11, 0.25**2, closed, b=b2, unroll=U2)
    first_sweep(g2, d2, v2, 0, 12, U2)
    weigh(k1, *w1, 5, 19, 0.25, open_, unroll=U1)
    first_sweep(g1, d1, v1, 4, 20, U1)

    def use2(i, value):
        v2[i] = jnp.where(d2[i] > 0.0, v2[i] + value, 0.0)

    prolong(e3, index[0] * 2, 8, py2[...], pz2[...], fine2, use2)
    smooth(v2, g2, d2, w2, 1, 11, closed, b2, U2)

    def use1(i, value):
        v1[i + 4] = jnp.where(d1[i + 4] > 0.0, v1[i + 4] + value, 0.0)

    py1 = spread_matrix((g1.shape[1], g2.shape[1]), 0, index[1] * 8, 16)
    pz1 = spread_matrix((g2.shape[2], g1.shape[2]), 1, index[2] * 32, 64)
    prolong(v2, 1, 10, py1, pz1, fine1, use1)
    smooth(v1, g1, d1, w1, 5, 19, open_, unroll=U1)
    return v1


BOTTOM = 14
UP = 7


def middle(nz, index, s, g2, k2, d2, g1, k1, d1, f, wx, wy, wz, d, k, *refs):
    m3, m2, (py0, pz0, ry, rz) = refs[:6], refs[6:8], refs[8:12]
    v, gn, k3 = refs[12:15]
    low, mid, (fine0, r, held0) = refs[15 : 15 + BOTTOM], refs[15 + BOTTOM : 15 + BOTTOM + UP], refs[15 + BOTTOM + UP :]
    e3 = bottom(nz, s, k3, low, m3)
    e1 = upward(nz, index, e3, g2, k2, d2, g1, k1, d1, mid, m2)
    w, shifts = (wx, wy, wz), Open()

    def use(i, value):
        v[i + 1] = inside(k[i + 1], f[i + 1] * d[i + 1] + value)

    prolong(e1, 5, 14, py0[...], pz0[...], fine0, use)
    smooth(v, f, d, w, 2, 24, shifts, unroll=U0)
    smooth(v, f, d, w, 3, 23, shifts, unroll=U0)
    residual_of(v, f, r, w, 4, 22, shifts, k, unroll=U0)
    gn[...] = restrict(r, 5, 0, 8, ry, rz, held0).reshape(gn.shape)


def final(nz, index, s, g2, k2, d2, g1, k1, d1, f, wx, wy, wz, d, k, *refs):
    m3, m2, (py0, pz0) = refs[:6], refs[6:8], refs[8:10]
    k3, v0, solution_, residual_ = refs[10:14]
    low, mid, (fine0, v) = refs[14 : 14 + BOTTOM], refs[14 + BOTTOM : 14 + BOTTOM + UP], refs[14 + BOTTOM + UP :]
    e3 = bottom(nz, s, k3, low, m3)
    e1 = upward(nz, index, e3, g2, k2, d2, g1, k1, d1, mid, m2)
    w, shifts = (wx, wy, wz), Open()

    def use(i, value):
        v[i + 3] = inside(k[i + 3], v0[i + 3] + value)

    prolong(e1, 6, 12, py0[...], pz0[...], fine0, use)
    smooth(v, f, d, w, 4, 22, shifts, unroll=U0)

    def last(i, here, im):
        return here[:32, :128], (f[i] - im)[:32, :128]

    def out(i, values):
        solution_[i - 5], residual_[i - 5] = values

    image(v, *w, 5, 21, last, out, shifts, unroll=U0)


def call(kernel, outs, scratch, *args, name, scalars=0):
    vmem = pl.BlockSpec(memory_space=pltpu.VMEM)
    smem = pl.BlockSpec(memory_space=pltpu.SMEM)
    return pl.pallas_call(
        kernel,
        out_shape=[jax.ShapeDtypeStruct(o, F32) for o in outs],
        in_specs=[smem] * scalars + [vmem] * (len(args) - scalars),
        out_specs=[vmem] * len(outs),
        scratch_shapes=[pltpu.VMEM(s, F32) for s in scratch],
        compiler_params=pltpu.CompilerParams(vmem_limit_bytes=48 << 20),
        name=name,
    )(*args)


def neighbours(last, initial, axis):
    count = lax.axis_size(axis)
    if axis == "gz":
        up = [(i, (i + 1) % count) for i in range(count)]
    else:
        up = [(i, i + 1) for i in range(count - 1)]
    down = [(j, i) for i, j in up]
    before = lax.ppermute(last, axis, up)
    after = lax.ppermute(initial, axis, down)
    if axis == "gz":
        at = lax.axis_index(axis)
        before = jnp.where(at == 0, 0.0, before)
        after = jnp.where(at == count - 1, 0.0, after)
    return before, after


def exchange(fields, block, sizes, widths):
    count = len(fields)
    for axis, dim in (("gz", 2), ("gy", 1), ("gx", 0)):
        along = 2 if dim == 2 else 0
        size, width = block[dim], widths[dim]
        last = [lax.slice_in_dim(f, size - width, size, axis=dim) for f in fields]
        initial = [lax.slice_in_dim(f, 0, width, axis=dim) for f in fields]
        before, after = neighbours(
            jnp.concatenate(last, along), jnp.concatenate(initial, along), axis
        )
        before = jnp.split(before, count, along)
        after = jnp.split(after, count, along)
        if dim == 0:
            fields = [jnp.concatenate([b, f, a], 0) for b, f, a in zip(before, fields, after)]
            continue
        own = [lax.slice_in_dim(f, 0, size, axis=dim) for f in fields]
        gap = list(own[0].shape)
        gap[dim] = sizes[dim - 1] - size - 2 * width
        parts = [[jnp.zeros(gap, F32)] if gap[dim] else []] * count
        fields = [
            jnp.concatenate([f, a] + z + [b], dim)
            for b, f, a, z in zip(before, own, after, parts)
        ]
    return fields


def everyone(pieces, axes):
    return lax.all_to_all(pieces, axes, 0, 0)


def body(right_side, conductivity):
    nx, ny, nz = (lax.axis_size(axis) for axis in ("gx", "gy", "gz"))
    index = jnp.stack([lax.axis_index(axis) for axis in ("gx", "gy", "gz")]).astype(jnp.int32)

    def ends(size, count, away=-1000):
        return np.where(np.arange(size) < count, np.arange(size), away)

    y0, z0 = coords(48, 32), coords(256, 128)
    y1, z1 = coords(24, 16), coords(128, 64)
    y2, z2 = coords(16, 8), coords(128, 32)
    rows2, rows3, rows4 = np.arange(8 * ny), np.arange(4 * ny), np.arange(2 * ny)
    lanes2, lanes3, lanes4 = ends(256, 32 * nz), ends(128, 16 * nz, -3000), ends(128, 8 * nz, -9000)
    ry0, rz0 = restriction(np.arange(16), y0), restriction(ends(128, 64), z0).T
    cy0, cz0 = halving(y1, y0), halving(z1, z0).T
    ry1, rz1 = restriction(np.arange(8), y1), restriction(ends(128, 32), z1).T
    cy1, cz1 = halving(y2, y1), halving(z2, z1).T
    ry2, rz2 = restriction(rows3, rows2), restriction(lanes3, lanes2).T
    cy2, cz2 = halving(rows3, rows2), halving(lanes3, lanes2).T
    ry3, rz3 = restriction(rows4, rows3), restriction(lanes4, lanes3).T
    cy3, cz3 = halving(rows4, rows3), halving(lanes4, lanes3).T
    py0, pz0 = prolongation(y0, y1), prolongation(z0, z1).T
    py2, pz2 = prolongation(rows2, rows3), prolongation(lanes2, lanes3).T
    py3, pz3 = prolongation(rows3, rows4), prolongation(lanes3, lanes4).T
    m3, m2 = (ry3, rz3, cy3, cz3, py3, pz3), (py2, pz2)

    wide, l1, l2 = (26, 48, 256), (24, 24, 128), (12, 8 * ny, 256)
    n3, n4 = (2 * nx + 6, 4 * ny, 128), (nx + 2, 2 * ny, 128)
    low = [
        n3, n3, n3, (3,) + n3, n3, n3,
        n4, (nx, 2 * ny, 128), n4, (3,) + n4, n4, n4,
        (nx * 2 * ny, 128), (nx + 2, 4 * ny, 128),
    ]
    mid = [l2, (3,) + l2, l2, l1, (3,) + l1, (8, 8 * ny, 256), (10, 24, 128)]

    f, k = exchange([right_side, conductivity], (16, 32, 128), (48, 256), (5, 5, 5))
    b1 = (8, 16, 128)
    wx, wy, wz, d, g1, k1, d1 = call(
        down0, [wide] * 4 + [b1] * 3,
        [wide, wide, (240, 256), (10, 24, 128), (4, 10, 24, 128)],
        f, k, ry0, rz0, cy0, cz0, name="down0",
    )
    ring1 = ((8, 16, 64), (24, 128), (8, 4, 4))
    g1, k1, d1 = exchange([g1, k1, d1], *ring1)
    inner1 = [l1, l1, (96, 128), (3,) + l1]
    (pieces,) = call(
        functools.partial(down1, True), [(ny * nz, 3, 8, 128)],
        inner1 + [(6, 16, 128), (4, 6, 16, 128)],
        g1, k1, d1, ry1, rz1, cy1, cz1, name="down1",
    )
    pieces = everyone(pieces, ("gy", "gz"))
    (own,) = call(
        functools.partial(arrange, nz), [(3, 4, 8 * ny, 256)], [], pieces, name="arrange"
    )
    before, after = neighbours(own, own, "gx")
    inner2 = [l2, l2, (8 * ny, 256), (3,) + l2, l2]
    pieces, g2, k2, d2 = call(
        functools.partial(down2, nz, True), [(nx, 2, 2, 4 * ny, 128), l2, l2, l2], inner2,
        before, own, after, ry2, rz2, cy2, cz2, name="down2",
    )
    s = everyone(pieces, "gx")
    fields = (f, wx, wy, wz, d, k)
    v, g1b, k3 = call(
        functools.partial(middle, nz), [wide, b1, n3],
        low + mid + [(14, 48, 256), wide, (128, 256)],
        index, s, g2, k2, d2, g1, k1, d1, *fields, *m3, *m2, py0, pz0, ry0, rz0,
        name="middle", scalars=1,
    )
    (g1,) = exchange([g1b], *ring1)
    (pieces,) = call(
        functools.partial(down1, False), [(ny * nz, 3, 8, 128)], inner1,
        g1, k1, d1, ry1, rz1, name="again1",
    )
    pieces = everyone(pieces, ("gy", "gz"))
    pieces, g2 = call(
        functools.partial(down2, nz, False), [(nx, 1, 2, 4 * ny, 128), l2], inner2,
        pieces, k2, d2, ry2, rz2, name="again2",
    )
    s = everyone(pieces, "gx")
    return tuple(call(
        functools.partial(final, nz), [(16, 32, 128)] * 2,
        low + mid + [(12, 48, 256), wide],
        index, s, g2, k2, d2, g1, k1, d1, *fields, *m3, *m2, py0, pz0, k3, v,
        name="final", scalars=1,
    ))


def solution(mesh):
    placed = P("gx", "gy", "gz")
    return jax.shard_map(
        body, mesh=mesh, in_specs=(placed, placed), out_specs=(placed, placed), check_vma=False
    )
```

```python
import functools

import jax
import jax.numpy as jnp
import numpy as np
from jax import lax
from jax.experimental import pallas as pl
from jax.experimental.pallas import tpu as pltpu
from jax.sharding import PartitionSpec as P

LEVELS = 4
CSWEEPS = 6
absorption = 0.01
relaxation = 0.8
F32 = jnp.float32


def coords(n, b):
    at = np.arange(n)
    return np.where(at < (n + b) // 2, at, at - n)


def restriction(coarse, fine):
    gap = fine[None, :] - 2 * coarse[:, None]
    outer, inner = (gap == -1) | (gap == 2), (gap == 0) | (gap == 1)
    return np.where(outer, 0.125, np.where(inner, 0.375, 0.0)).astype(np.float32)


def halving(coarse, fine):
    return np.where(fine[None, :] // 2 == coarse[:, None], 0.5, 0.0).astype(np.float32)


def prolongation(fine, coarse):
    near = fine[:, None] // 2 == coarse[None, :]
    far = fine[:, None] // 2 + 2 * (fine[:, None] % 2) - 1 == coarse[None, :]
    return np.where(near, 0.75, np.where(far, 0.25, 0.0)).astype(np.float32)


def dot(a, b):
    return lax.dot_general(
        a, b, (((1,), (0,)), ((), ())),
        precision=lax.Precision.HIGHEST, preferred_element_type=F32,
    )


def planes(lo, hi, step, carry=0, unroll=1):
    whole = (hi - lo) // unroll
    if whole > 1:
        carry = lax.fori_loop(0, whole, lambda t, c: step(lo + t * unroll, unroll, c), carry)
    elif whole == 1:
        carry = step(lo, unroll, carry)
    rest = (hi - lo) % unroll
    return step(hi - rest, rest, carry) if rest else carry


class Open:
    def above(self, v, dim):
        return pltpu.roll(v, v.shape[dim] - 1, dim)

    def below(self, v, dim):
        return pltpu.roll(v, 1, dim)

    def closed(self, k):
        return None


class Closed(Open):
    def __init__(self, shape, counts):
        self.last, self.first = [], []
        for dim in range(2):
            at = lax.broadcasted_iota(jnp.int32, shape, dim)
            self.last.append(jnp.where(at == counts[dim] - 1, 0.0, 1.0))
            self.first.append(jnp.where(at == 0, 0.0, 1.0))

    def above(self, v, dim):
        return super().above(v, dim) * self.last[dim]

    def below(self, v, dim):
        return super().below(v, dim) * self.first[dim]

    def closed(self, k):
        return k * ((1.0 - self.first[0]) + (1.0 - self.first[1]))


def weigh(k, wx, wy, wz, lo, hi, factor, shifts, d=None, mask=None, b=None, unroll=1):
    half = 0.5 * factor
    first = half * (k[lo - 1] + k[lo])
    wx[lo - 1] = first

    def step(i, n, below):
        here = [k[i + j] for j in range(n + 1)]
        outs = []
        for j in range(n):
            x = half * (here[j] + here[j + 1])
            y = half * (here[j] + shifts.above(here[j], 0))
            z = half * (here[j] + shifts.above(here[j], 1))
            ends, value = shifts.closed(half * here[j]), None
            if d is not None:
                value = (x + below) + (y + shifts.below(y, 0)) + (z + shifts.below(z, 1))
                if ends is not None:
                    value = value + ends
                value = relaxation / (value + absorption)
                if mask is not None:
                    value = mask(here[j], value)
            outs.append((x, y, z, ends, value))
            below = x
        for j, (x, y, z, ends, value) in enumerate(outs):
            wx[i + j], wy[i + j], wz[i + j] = x, y, z
            if ends is not None:
                b[i + j] = ends
            if value is not None:
                d[i + j] = value
        return below

    planes(lo, hi, step, first, unroll)


def image(v, wx, wy, wz, lo, hi, use, put, shifts, b=None, unroll=1):
    def step(i, n, below):
        here = [v[i + j] for j in range(n + 1)]
        outs = []
        for j in range(n):
            x = wx[i + j] * (here[j] - here[j + 1])
            y = wy[i + j] * (here[j] - shifts.above(here[j], 0))
            z = wz[i + j] * (here[j] - shifts.above(here[j], 1))
            total = (x - below) + (y - shifts.below(y, 0)) + (z - shifts.below(z, 1))
            if b is not None:
                total = total + b[i + j] * here[j]
            outs.append(use(i + j, here[j], total + absorption * here[j]))
            below = x
        for j, value in enumerate(outs):
            put(i + j, value)
        return below

    planes(lo, hi, step, wx[lo - 1] * (v[lo - 1] - v[lo]), unroll)


def into(ref, by=0):
    def put(i, value):
        ref[i + by] = value

    return put


def smooth(v, f, d, w, lo, hi, shifts, b=None, unroll=1, by=0):
    def use(i, here, im):
        return here + d[i] * (f[i + by] - im)

    image(v, *w, lo, hi, use, into(v), shifts, b, unroll)


def residual_of(v, f, r, w, lo, hi, shifts, mask=None, b=None, unroll=1):
    def use(i, here, im):
        value = f[i] - im
        return value if mask is None else jnp.where(mask[i] > 0.0, value, 0.0)

    image(v, *w, lo, hi, use, into(r), shifts, b, unroll)


def first_sweep(g, d, v, lo, hi, unroll, by=0):
    def step(i, n, carry):
        values = [g[i + j + by] * d[i + j] for j in range(n)]
        for j, value in enumerate(values):
            v[i + j] = value
        return carry

    planes(lo, hi, step, unroll=unroll)


def restrict(r, offset, lo, hi, ry, rz, held):
    size = ry.shape[0]
    for i in range(lo, hi):
        at = 2 * i + offset
        plane = 0.125 * (r[at - 1] + r[at + 2]) + 0.375 * (r[at] + r[at + 1])
        held[(i - lo) * size : (i - lo + 1) * size, :] = dot(ry[...], plane)
    return dot(held[: (hi - lo) * size, :], rz[...])


def halve(k, offset, lo, hi, cy, cz, held):
    size = cy.shape[0]
    for i in range(lo, hi):
        plane = 0.5 * (k[2 * i + offset] + k[2 * i + 1 + offset])
        held[(i - lo) * size : (i - lo + 1) * size, :] = dot(cy[...], plane)
    return dot(held[: (hi - lo) * size, :], cz[...])


def prolong(e, first, count, py, pz, finer, use):
    rows = e.shape[1]
    spread = dot(e[pl.ds(first, count)].reshape(count * rows, e.shape[2]), pz)
    for i in range(count):
        finer[i] = dot(py, spread[i * rows : (i + 1) * rows])

    def step(i, n, carry):
        below, here, above = finer[i - 1], finer[i], finer[i + 1]
        use(2 * (i - 1), 0.75 * here + 0.25 * below)
        use(2 * (i - 1) + 1, 0.75 * here + 0.25 * above)
        return carry

    planes(1, count - 1, step)


def three(w):
    return tuple(w.at[i] for i in range(3))


def inside(k, value):
    return jnp.where(k > 0.0, value, 0.0)


U0, U1, U2, U3 = 2, 2, 4, 4


def down0(f, k, ry, rz, cy, cz, wx_, wy_, wz_, d_, g1, k1, wx, wy, wz, d, v, r, held, sem):
    shifts = Open()
    weigh(k, wx, wy, wz, 1, 25, 1.0, shifts, d, inside, unroll=U0)
    copies = [
        pltpu.make_async_copy(here, there, sem.at[i])
        for i, (here, there) in enumerate(((wx, wx_), (wy, wy_), (wz, wz_), (d, d_)))
    ]
    for copy in copies:
        copy.start()
    first_sweep(f, d, v, 1, 25, U0)
    residual_of(v, f, r, (wx, wy, wz), 2, 24, shifts, k, unroll=U0)
    g1[...] = restrict(r, 5, -1, 9, ry, rz, held).reshape(g1.shape)
    k1[...] = halve(k, 5, -1, 9, cy, cz, held).reshape(k1.shape)
    for copy in copies:
        copy.wait()


def descend(first, *refs):
    shifts = Open()
    if first:
        g1, k1, ry1, rz1, ry2, rz2, cy1, cz1, cy2, cz2 = refs[:10]
        out, d1, g2, k2, d2 = refs[10:15]
    else:
        g1, k1, d1, k2, d2, ry1, rz1, ry2, rz2 = refs[:9]
        out, g2 = refs[9:11]
    v1, r1, held, w1, v2, r2, w2, part = refs[-8:]
    w1, w2 = three(w1), three(w2)
    rows = g2.shape[1]
    if first:
        zero = jnp.zeros(d1.shape[1:], F32)
        d1[0], d1[25] = zero, zero
        weigh(k1, *w1, 1, 25, 0.25, shifts, d1, inside, unroll=U1)
    else:
        weigh(k1, *w1, 1, 25, 0.25, shifts, unroll=U1)
    first_sweep(g1, d1, v1, 1, 25, U1)
    residual_of(v1, g1, r1, w1, 2, 24, shifts, d1, unroll=U1)
    zero = jnp.zeros(g2.shape[1:], F32)
    g2[0], g2[11] = zero, zero
    g2[1:11] = restrict(r1, 9, -3, 7, ry1, rz1, held).reshape(10, rows, 128)
    if first:
        d2[0], d2[11] = zero, zero
        k2[...] = halve(k1, 9, -4, 8, cy1, cz1, held).reshape(k2.shape)
        weigh(k2, *w2, 1, 11, 0.25**2, shifts, d2, inside, unroll=U2)
    else:
        weigh(k2, *w2, 1, 11, 0.25**2, shifts, unroll=U2)
    first_sweep(g2, d2, v2, 1, 11, U2)
    residual_of(v2, g2, r2, w2, 3, 9, shifts, d2, unroll=U2)
    total = None
    for i in range(2):
        at = 2 * i + 4
        plane = 0.125 * (r2[at - 1] + r2[at + 2]) + 0.375 * (r2[at] + r2[at + 1])
        value = dot(ry2[i], plane)
        total = value if total is None else total + value
    tile = dot(total, rz2[...])
    if first:
        total = dot(cy2[0], 0.5 * (k2[4] + k2[5])) + dot(cy2[1], 0.5 * (k2[6] + k2[7]))
        tile = tile + dot(total, cz2[...])
    for i in range(out.shape[0]):
        out[i] = tile


def repack(s, out):
    tiles = 2 * s.shape[0] // 16
    lane = lax.broadcasted_iota(jnp.int32, (8, 128), 1) // 16
    row = lax.broadcasted_iota(jnp.int32, (8, 128), 0) // 4
    for field in range(out.shape[1] // tiles):
        for t in range(tiles):
            total = jnp.zeros((8, 128), F32)
            for half in range(2):
                for p in range(8):
                    plane = 16 * t + 8 * half + p
                    part = s[plane // 2]
                    if plane % 2 != half:
                        part = pltpu.roll(part, 4, 0)
                    if p != field:
                        part = pltpu.roll(part, (16 * (p - field)) % 128, 1)
                    total = jnp.where((lane == p) & (row == half), part, total)
            for i in range(out.shape[0]):
                out[i, field * tiles + t] = total


def unpack(s, first, tiles, nz, whole):
    lane = lax.broadcasted_iota(jnp.int32, (8, 128), 1) // 16
    for j in range(s.shape[0] // nz):
        for t in range(tiles):
            for p in range(8):
                total = jnp.zeros((8, 128), F32)
                for q in range(nz):
                    part = s[j * nz + q, first + t]
                    if p != q:
                        part = pltpu.roll(part, (16 * (q - p)) % 128, 1)
                    total = jnp.where(lane == q, part, total)
                whole[16 * t + p + 3, 4 * j : 4 * j + 4] = total[:4]
                whole[16 * t + p + 11, 4 * j : 4 * j + 4] = total[4:]


def bottom(nz, s, k3, scratch, mats):
    g3, v3, r3, w3, d3, b3, k4, g4, v4, w4, d4, b4, held, fine4 = scratch
    ry3, rz3, cy3, cz3, py3, pz3 = mats
    n4 = g4.shape[0]
    n3, two = 2 * n4, s.shape[1] == n4 // 4
    rows, lanes = g3.shape[1], g3.shape[2]
    zero = jnp.zeros((rows, lanes), F32)
    for i in (0, 1, 2, n3 + 3, n3 + 4, n3 + 5):
        v3[i], r3[i] = zero, zero
        if two:
            k3[i] = zero
    for ref in (k4, v4):
        for i in (0, n4 + 1):
            ref[i] = jnp.zeros(ref.shape[1:], F32)
    unpack(s, 0, n3 // 16, nz, g3)
    if two:
        unpack(s, n3 // 16, n3 // 16, nz, k3)
    k4[1 : n4 + 1] = halve(k3, 3, 0, n4, cy3, cz3, held).reshape(g4.shape)
    shifts3 = Closed((rows, lanes), (rows, 16 * nz))
    shifts4 = Closed((k4.shape[1], lanes), (k4.shape[1], 8 * nz))
    w3, w4 = three(w3), three(w4)
    weigh(k3, *w3, 3, n3 + 3, 0.25**3, shifts3, d3, inside, b3, U3)
    weigh(k4, *w4, 1, n4 + 1, 0.25**4, shifts4, d4, inside, b4, U3)
    first_sweep(g3, d3, v3, 3, n3 + 3, U3)
    residual_of(v3, g3, r3, w3, 3, n3 + 3, shifts3, b=b3, unroll=U3)
    g4[...] = restrict(r3, 3, 0, n4, ry3, rz3, held).reshape(g4.shape)
    first_sweep(g4, d4, v4, 1, n4 + 1, U3, by=-1)

    def turn(j, carry):
        smooth(v4, g4, d4, w4, 1, n4 + 1, shifts4, b4, n4, by=-1)
        return carry

    lax.fori_loop(0, CSWEEPS - 1, turn, 0)

    def use(i, value):
        v3[i + 3] = v3[i + 3] + value

    prolong(v4, 0, n4 + 2, py3[...], pz3[...], fine4, use)
    smooth(v3, g3, d3, w3, 3, n3 + 3, shifts3, b3, U3)
    return v3


def spread_matrix(shape, dim_fine, coarse_start, block_fine):
    fine = lax.broadcasted_iota(jnp.int32, shape, dim_fine)
    size = shape[dim_fine]
    fine = jnp.where(fine < (size + block_fine) // 2, fine, fine - size)
    whole = lax.broadcasted_iota(jnp.int32, shape, 1 - dim_fine)
    near = (fine >> 1) + coarse_start
    far = near + 2 * (fine & 1) - 1
    return jnp.where(whole == near, 0.75, jnp.where(whole == far, 0.25, 0.0))


def upward(index, e3, g2, k2, d2, g1, k1, d1, ends, scratch, mats):
    v2, w2, m2, v1, w1, fine2, fine1 = scratch
    py1, pz1 = mats
    shifts, w2, w1 = Open(), three(w2), three(w1)
    weigh(k2, *w2, 1, 11, 0.25**2, shifts, unroll=U2)
    weigh(k1, *w1, 6, 20, 0.25, shifts, unroll=U1)
    first_sweep(g2, d2, v2, 0, 12, U2)
    first_sweep(g1, d1, v1, 5, 21, U1)
    m2[...] = d2[...]
    if ends is not None:
        for ref, i in zip(ends, (0, 11)):
            v2[i], m2[i] = ref[0] * ref[1], ref[1]

    def use2(i, value):
        v2[i] = jnp.where(m2[i] > 0.0, v2[i] + value, 0.0)

    py2 = spread_matrix((g2.shape[1], e3.shape[1]), 0, index[1] * 4, 8)
    pz2 = spread_matrix((e3.shape[2], g2.shape[2]), 1, index[2] * 16, 32)
    prolong(e3, index[0] * 2, 8, py2, pz2, fine2, use2)
    smooth(v2, g2, d2, w2, 1, 11, shifts, unroll=U2)

    def use1(i, value):
        v1[i + 5] = jnp.where(d1[i + 5] > 0.0, v1[i + 5] + value, 0.0)

    prolong(v2, 1, 10, py1[...], pz1[...], fine1, use1)
    smooth(v1, g1, d1, w1, 6, 20, shifts, unroll=U1)
    return v1


BOTTOM = 14
UP = 7


def fetch(sources, targets, sem):
    copies = [
        pltpu.make_async_copy(there, here, sem.at[i])
        for i, (there, here) in enumerate(zip(sources, targets))
    ]
    for copy in copies:
        copy.start()
    return copies


def middle(nz, index, f_, wx_, wy_, wz_, d_, k_, s, g2, k2, d2, g1, k1, d1, *refs):
    ends, m3, m1, (py0, pz0, ry, rz), (v_, gn, k3) = refs[:2], refs[2:8], refs[8:10], refs[10:14], refs[14:17]
    low, mid, (fine0, r, held0, f, wx, wy, wz, d, k, v, sem) = refs[17:31], refs[31:38], refs[38:]
    copies = fetch((f_, wx_, wy_, wz_, d_, k_), (f, wx, wy, wz, d, k), sem)
    e3 = bottom(nz, s, k3, low, m3)
    e1 = upward(index, e3, g2, k2, d2, g1, k1, d1, ends, mid, m1)
    for copy in copies:
        copy.wait()
    w, shifts = (wx, wy, wz), Open()

    def use(i, value):
        v[i + 1] = inside(k[i + 1], f[i + 1] * d[i + 1] + value)

    prolong(e1, 6, 14, py0[...], pz0[...], fine0, use)
    smooth(v, f, d, w, 2, 24, shifts, unroll=U0)
    smooth(v, f, d, w, 3, 23, shifts, unroll=U0)
    copy = pltpu.make_async_copy(v, v_, sem.at[0])
    copy.start()
    residual_of(v, f, r, w, 4, 22, shifts, k, unroll=U0)
    gn[...] = restrict(r, 5, 0, 8, ry, rz, held0).reshape(gn.shape)
    copy.wait()


def final(nz, index, f_, wx_, wy_, wz_, d_, k_, v_, s, g2, k2, d2, g1, k1, d1, *refs):
    m3, m1, (py0, pz0, k3), (solution_, residual_) = refs[:6], refs[6:8], refs[8:11], refs[11:13]
    low, mid, (fine0, f, wx, wy, wz, d, k, v, sem) = refs[13:27], refs[27:34], refs[34:]
    copies = fetch((f_, wx_, wy_, wz_, d_, k_, v_), (f, wx, wy, wz, d, k, v), sem)
    e3 = bottom(nz, s, k3, low, m3)
    e1 = upward(index, e3, g2, k2, d2, g1, k1, d1, None, mid, m1)
    for copy in copies:
        copy.wait()
    w, shifts = (wx, wy, wz), Open()

    def use(i, value):
        v[i + 3] = inside(k[i + 3], v[i + 3] + value)

    prolong(e1, 7, 12, py0[...], pz0[...], fine0, use)
    smooth(v, f, d, w, 4, 22, shifts, unroll=U0)

    def last(i, here, im):
        return here[:32, :128], (f[i] - im)[:32, :128]

    def out(i, values):
        solution_[i - 5], residual_[i - 5] = values

    image(v, *w, 5, 21, last, out, shifts, unroll=U0)


def call(kernel, outs, scratch, *args, name, scalars=0, loose=0, away=0, sems=0):
    vmem = pl.BlockSpec(memory_space=pltpu.VMEM)
    smem = pl.BlockSpec(memory_space=pltpu.SMEM)
    hbm = pl.BlockSpec(memory_space=pl.ANY)
    return pl.pallas_call(
        kernel,
        out_shape=[jax.ShapeDtypeStruct(o, F32) for o in outs],
        in_specs=[smem] * scalars + [hbm] * loose + [vmem] * (len(args) - scalars - loose),
        out_specs=[hbm] * away + [vmem] * (len(outs) - away),
        scratch_shapes=[pltpu.VMEM(s, F32) for s in scratch]
        + ([pltpu.SemaphoreType.DMA((sems,))] if sems else []),
        compiler_params=pltpu.CompilerParams(vmem_limit_bytes=56 << 20),
        name=name,
    )(*args)


def neighbours(last, initial, axis):
    count = lax.axis_size(axis)
    if axis == "gz":
        up = [(i, (i + 1) % count) for i in range(count)]
    else:
        up = [(i, i + 1) for i in range(count - 1)]
    down = [(j, i) for i, j in up]
    before = lax.ppermute(last, axis, up)
    after = lax.ppermute(initial, axis, down)
    if axis == "gz":
        at = lax.axis_index(axis)
        before = jnp.where(at == 0, 0.0, before)
        after = jnp.where(at == count - 1, 0.0, after)
    return before, after


def exchange(fields, block, sizes, widths, extra=0):
    count = len(fields)
    for axis, dim in (("gz", 2), ("gy", 1), ("gx", 0)):
        along = 2 if dim == 2 else 0
        size, width, shift = block[dim], widths[dim], extra if dim == 0 else 0
        last = [lax.slice_in_dim(f, size + shift - width, size + shift, axis=dim) for f in fields]
        initial = [lax.slice_in_dim(f, shift, shift + width, axis=dim) for f in fields]
        before, after = neighbours(
            jnp.concatenate(last, along), jnp.concatenate(initial, along), axis
        )
        before = jnp.split(before, count, along)
        after = jnp.split(after, count, along)
        own = [lax.slice_in_dim(f, shift, shift + size, axis=dim) for f in fields]
        if dim == 0:
            fields = [jnp.concatenate([b, f, a], 0) for b, f, a in zip(before, own, after)]
            continue
        gap = list(own[0].shape)
        gap[dim] = sizes[dim - 1] - size - 2 * width
        parts = [[jnp.zeros(gap, F32)] if gap[dim] else []] * count
        fields = [
            jnp.concatenate([f, a] + z + [b], dim)
            for b, f, a, z in zip(before, own, after, parts)
        ]
    return fields


def everyone(pieces, axes):
    return lax.all_to_all(pieces, axes, 0, 0)


def body(right_side, conductivity):
    nx, ny, nz = (lax.axis_size(axis) for axis in ("gx", "gy", "gz"))
    index = jnp.stack([lax.axis_index(axis) for axis in ("gx", "gy", "gz")]).astype(jnp.int32)

    def ends(size, count, away=-1000, start=0):
        at = np.arange(size)
        return np.where((at >= start) & (at < start + count), at - start, away)

    y0, z0 = coords(48, 32), coords(256, 128)
    y1, z1 = coords(40, 16), coords(128, 64)
    y2, z2 = coords(24, 8), coords(128, 32)
    rows3, rows4 = np.arange(4 * ny), np.arange(2 * ny)
    lanes3, lanes4 = ends(128, 16 * nz, -3000), ends(128, 8 * nz, -9000)
    ry0, rz0 = restriction(np.arange(16), y0), restriction(ends(128, 64), z0).T
    cy0, cz0 = halving(np.arange(16), y0), halving(ends(128, 64), z0).T
    ry1, rz1 = restriction(y2, y1), restriction(z2, z1).T
    cy1, cz1 = halving(y2, y1), halving(z2, z1).T

    def both(matrix):
        zero = np.zeros_like(matrix)
        return np.stack([np.concatenate([matrix, zero]), np.concatenate([zero, matrix])])

    ry2, rz2 = both(restriction(np.arange(4), y2)), restriction(ends(128, 16), z2).T
    cy2, cz2 = both(halving(np.arange(4), y2)), halving(ends(128, 16, start=16), z2).T
    ry3, rz3 = restriction(rows4, rows3), restriction(lanes4, lanes3).T
    cy3, cz3 = halving(rows4, rows3), halving(lanes4, lanes3).T
    py0, pz0 = prolongation(y0, y1), prolongation(z0, z1).T
    py1, pz1 = prolongation(y1, y2), prolongation(z1, z2).T
    py3, pz3 = prolongation(rows3, rows4), prolongation(lanes3, lanes4).T
    m3, m1 = (ry3, rz3, cy3, cz3, py3, pz3), (py1, pz1)

    wide, l1, l2 = (26, 48, 256), (26, 40, 128), (12, 24, 128)
    n3, n4 = (2 * nx + 6, 4 * ny, 128), (nx + 2, 2 * ny, 128)
    low = [
        n3, n3, n3, (3,) + n3, n3, n3,
        n4, (nx, 2 * ny, 128), n4, (3,) + n4, n4, n4,
        (nx * 2 * ny, 128), (nx + 2, 4 * ny, 128),
    ]
    mid = [l2, (3,) + l2, l2, l1, (3,) + l1, (8, 24, 128), (10, 40, 128)]
    tiles = nx // 8

    f, k = exchange([right_side, conductivity], (16, 32, 128), (48, 256), (5, 5, 5))
    b1 = (10, 16, 128)
    wx, wy, wz, d, g1, k1 = call(
        down0, [wide] * 4 + [b1] * 2, [wide] * 6 + [(160, 256)],
        f, k, ry0, rz0, cy0, cz0, name="down0", away=4, sems=4,
    )
    size1 = ((8, 16, 64), (40, 128))
    g1, k1 = exchange([g1, k1], *size1, (9, 11, 11), 1)
    inner = [l1, l1, (288, 128), (3,) + l1, l2, l2, (3,) + l2, (8, 128)]
    pieces, d1, g2, k2, d2 = call(
        functools.partial(descend, True), [(nx, 8, 128), l1, l2, l2, l2], inner,
        g1, k1, ry1, rz1, ry2, rz2, cy1, cz1, cy2, cz2, name="descend",
    )
    first, last = jnp.stack([g2[4], d2[4]]), jnp.stack([g2[7], d2[7]])
    outer = neighbours(first, last, "gx")
    pieces = everyone(pieces, "gx")
    (pieces,) = call(repack, [(ny * nz, 2 * tiles, 8, 128)], [], pieces, name="repack")
    s = everyone(pieces, ("gy", "gz"))
    fields = (f, wx, wy, wz, d, k)
    v, g1b, k3 = call(
        functools.partial(middle, nz), [wide, (8, 16, 128), n3],
        low + mid + [(14, 48, 256), wide, (128, 256)] + [wide] * 7,
        index, *fields, s, g2, k2, d2, g1, k1, d1, *outer, *m3, *m1, py0, pz0, ry0, rz0,
        name="middle", scalars=1, loose=6, away=1, sems=6,
    )
    (g1,) = exchange([g1b], *size1, (8, 11, 11))
    g1 = jnp.pad(g1, ((1, 1), (0, 0), (0, 0)))
    pieces, g2 = call(
        functools.partial(descend, False), [(nx, 8, 128), l2], inner,
        g1, k1, d1, k2, d2, ry1, rz1, ry2, rz2, name="again",
    )
    pieces = everyone(pieces, "gx")
    (pieces,) = call(repack, [(ny * nz, tiles, 8, 128)], [], pieces, name="repack2")
    s = everyone(pieces, ("gy", "gz"))
    return tuple(call(
        functools.partial(final, nz), [(16, 32, 128)] * 2,
        low + mid + [(12, 48, 256)] + [wide] * 7,
        index, *fields, v, s, g2, k2, d2, g1, k1, d1, *m3, *m1, py0, pz0, k3,
        name="final", scalars=1, loose=7, sems=7,
    ))


def solution(mesh):
    placed = P("gx", "gy", "gz")
    return jax.shard_map(
        body, mesh=mesh, in_specs=(placed, placed), out_specs=(placed, placed), check_vma=False
    )
```

```python
import functools

import jax
import jax.numpy as jnp
import numpy as np
from jax import lax
from jax.experimental import pallas as pl
from jax.experimental.pallas import tpu as pltpu
from jax.sharding import PartitionSpec as P

LEVELS = 4
CSWEEPS = 6
absorption = 0.01
relaxation = 0.8
F32 = jnp.float32


def coords(n, b):
    at = np.arange(n)
    return np.where(at < (n + b) // 2, at, at - n)


def restriction(coarse, fine):
    gap = fine[None, :] - 2 * coarse[:, None]
    outer, inner = (gap == -1) | (gap == 2), (gap == 0) | (gap == 1)
    return np.where(outer, 0.125, np.where(inner, 0.375, 0.0)).astype(np.float32)


def halving(coarse, fine):
    return np.where(fine[None, :] // 2 == coarse[:, None], 0.5, 0.0).astype(np.float32)


def prolongation(fine, coarse):
    near = fine[:, None] // 2 == coarse[None, :]
    far = fine[:, None] // 2 + 2 * (fine[:, None] % 2) - 1 == coarse[None, :]
    return np.where(near, 0.75, np.where(far, 0.25, 0.0)).astype(np.float32)


def dot(a, b):
    return lax.dot_general(
        a, b, (((1,), (0,)), ((), ())),
        precision=lax.Precision.HIGHEST, preferred_element_type=F32,
    )


def planes(lo, hi, step, carry=0, unroll=1):
    whole = (hi - lo) // unroll
    if whole > 1:
        carry = lax.fori_loop(0, whole, lambda t, c: step(lo + t * unroll, unroll, c), carry)
    elif whole == 1:
        carry = step(lo, unroll, carry)
    rest = (hi - lo) % unroll
    return step(hi - rest, rest, carry) if rest else carry


class Open:
    def above(self, v, dim):
        return pltpu.roll(v, v.shape[dim] - 1, dim)

    def below(self, v, dim):
        return pltpu.roll(v, 1, dim)

    def closed(self, k):
        return None


class Closed(Open):
    def __init__(self, shape, counts):
        self.last, self.first = [], []
        for dim in range(2):
            at = lax.broadcasted_iota(jnp.int32, shape, dim)
            self.last.append(jnp.where(at == counts[dim] - 1, 0.0, 1.0))
            self.first.append(jnp.where(at == 0, 0.0, 1.0))

    def above(self, v, dim):
        return super().above(v, dim) * self.last[dim]

    def below(self, v, dim):
        return super().below(v, dim) * self.first[dim]

    def closed(self, k):
        return k * ((1.0 - self.first[0]) + (1.0 - self.first[1]))


def weigh(k, wx, wy, wz, lo, hi, factor, shifts, d=None, mask=None, b=None, unroll=1):
    half = 0.5 * factor
    first = half * (k[lo - 1] + k[lo])
    wx[lo - 1] = first

    def step(i, n, below):
        here = [k[i + j] for j in range(n + 1)]
        outs = []
        for j in range(n):
            x = half * (here[j] + here[j + 1])
            y = half * (here[j] + shifts.above(here[j], 0))
            z = half * (here[j] + shifts.above(here[j], 1))
            ends, value = shifts.closed(half * here[j]), None
            if d is not None:
                value = (x + below) + (y + shifts.below(y, 0)) + (z + shifts.below(z, 1))
                if ends is not None:
                    value = value + ends
                value = relaxation / (value + absorption)
                if mask is not None:
                    value = mask(here[j], value)
            outs.append((x, y, z, ends, value))
            below = x
        for j, (x, y, z, ends, value) in enumerate(outs):
            wx[i + j], wy[i + j], wz[i + j] = x, y, z
            if ends is not None:
                b[i + j] = ends
            if value is not None:
                d[i + j] = value
        return below

    planes(lo, hi, step, first, unroll)


def image(v, wx, wy, wz, lo, hi, use, put, shifts, b=None, unroll=1):
    def step(i, n, below):
        here = [v[i + j] for j in range(n + 1)]
        outs = []
        for j in range(n):
            x = wx[i + j] * (here[j] - here[j + 1])
            y = wy[i + j] * (here[j] - shifts.above(here[j], 0))
            z = wz[i + j] * (here[j] - shifts.above(here[j], 1))
            total = (x - below) + (y - shifts.below(y, 0)) + (z - shifts.below(z, 1))
            if b is not None:
                total = total + b[i + j] * here[j]
            outs.append(use(i + j, here[j], total + absorption * here[j]))
            below = x
        for j, value in enumerate(outs):
            put(i + j, value)
        return below

    planes(lo, hi, step, wx[lo - 1] * (v[lo - 1] - v[lo]), unroll)


def into(ref, by=0):
    def put(i, value):
        ref[i + by] = value

    return put


def smooth(v, f, d, w, lo, hi, shifts, b=None, unroll=1, by=0):
    def use(i, here, im):
        return here + d[i] * (f[i + by] - im)

    image(v, *w, lo, hi, use, into(v), shifts, b, unroll)


def residual_of(v, f, r, w, lo, hi, shifts, mask=None, b=None, unroll=1):
    def use(i, here, im):
        value = f[i] - im
        return value if mask is None else jnp.where(mask[i] > 0.0, value, 0.0)

    image(v, *w, lo, hi, use, into(r), shifts, b, unroll)


def first_sweep(g, d, v, lo, hi, unroll, by=0):
    def step(i, n, carry):
        values = [g[i + j + by] * d[i + j] for j in range(n)]
        for j, value in enumerate(values):
            v[i + j] = value
        return carry

    planes(lo, hi, step, unroll=unroll)


def restrict(r, offset, lo, hi, ry, rz, held):
    size = ry.shape[0]
    for i in range(lo, hi):
        at = 2 * i + offset
        plane = 0.125 * (r[at - 1] + r[at + 2]) + 0.375 * (r[at] + r[at + 1])
        held[(i - lo) * size : (i - lo + 1) * size, :] = dot(ry[...], plane)
    return dot(held[: (hi - lo) * size, :], rz[...])


def halve(k, offset, lo, hi, cy, cz, held):
    size = cy.shape[0]
    for i in range(lo, hi):
        plane = 0.5 * (k[2 * i + offset] + k[2 * i + 1 + offset])
        held[(i - lo) * size : (i - lo + 1) * size, :] = dot(cy[...], plane)
    return dot(held[: (hi - lo) * size, :], cz[...])


def prolong(e, first, count, py, pz, finer, use):
    rows = e.shape[1]
    spread = dot(e[pl.ds(first, count)].reshape(count * rows, e.shape[2]), pz)
    for i in range(count):
        finer[i] = dot(py, spread[i * rows : (i + 1) * rows])

    def step(i, n, carry):
        below, here, above = finer[i - 1], finer[i], finer[i + 1]
        use(2 * (i - 1), 0.75 * here + 0.25 * below)
        use(2 * (i - 1) + 1, 0.75 * here + 0.25 * above)
        return carry

    planes(1, count - 1, step)


def three(w):
    return tuple(w.at[i] for i in range(3))


def inside(k, value):
    return jnp.where(k > 0.0, value, 0.0)


U0, U1, U2, U3 = 6, 12, 10, 16


def place(target, at, source, start, count, unroll=4):
    def step(i, n, carry):
        values = [source[start + i + j] for j in range(n)]
        for j, value in enumerate(values):
            target[at + i + j] = value
        return carry

    planes(0, count, step, unroll=unroll)


def down0(before, fo, ko, after, ry, rz, cy, cz, f_, k_, wx_, wy_, wz_, d_, out, f, k, wx, wy, wz, d, v, r, held, sem):
    shifts = Open()
    for ref, own, at in ((f, fo, 0), (k, ko, 5)):
        place(ref, 0, before, at, 5, 5)
        place(ref, 5, own, 0, 16)
        place(ref, 21, after, at, 5, 5)
    weigh(k, wx, wy, wz, 1, 25, 1.0, shifts, d, inside, unroll=U0)
    copies = [
        pltpu.make_async_copy(here, there, sem.at[i])
        for i, (here, there) in enumerate(((f, f_), (k, k_), (wx, wx_), (wy, wy_), (wz, wz_), (d, d_)))
    ]
    for copy in copies:
        copy.start()
    first_sweep(f, d, v, 1, 25, U0)
    residual_of(v, f, r, (wx, wy, wz), 2, 24, shifts, k, unroll=U0)
    out[:10] = restrict(r, 5, -1, 9, ry, rz, held).reshape(10, 16, 128)
    out[10:] = halve(k, 5, -1, 9, cy, cz, held).reshape(10, 16, 128)
    for copy in copies:
        copy.wait()


def descend(first, *refs):
    shifts = Open()
    before, own, after = refs[:3]
    if first:
        ry1, rz1, ry2, rz2, cy1, cz1, cy2, cz2 = refs[3:11]
        out, g1, k1, d1, g2, k2, d2 = refs[11:18]
        for ref, at in ((g1, 0), (k1, 1)):
            place(ref, 0, before, 9 * at, 9, 9)
            place(ref, 9, own, 10 * at + 1, 8, 8)
            place(ref, 17, after, 9 * at, 9, 9)
    else:
        k1, d1, k2, d2, ry1, rz1, ry2, rz2 = refs[3:11]
        out, g1, g2 = refs[11:14]
        zero = jnp.zeros(g1.shape[1:], F32)
        g1[0], g1[25] = zero, zero
        for ref, at in ((before, 1), (own, 9), (after, 17)):
            place(g1, at, ref, 0, 8, 8)
    v1, r1, held, w1, v2, r2, w2, part = refs[-8:]
    w1, w2 = three(w1), three(w2)
    rows = g2.shape[1]
    if first:
        zero = jnp.zeros(d1.shape[1:], F32)
        d1[0], d1[25] = zero, zero
        weigh(k1, *w1, 1, 25, 0.25, shifts, d1, inside, unroll=U1)
    else:
        weigh(k1, *w1, 1, 25, 0.25, shifts, unroll=U1)
    first_sweep(g1, d1, v1, 1, 25, U1)
    residual_of(v1, g1, r1, w1, 2, 24, shifts, d1, unroll=U1)
    zero = jnp.zeros(g2.shape[1:], F32)
    g2[0], g2[11] = zero, zero
    g2[1:11] = restrict(r1, 9, -3, 7, ry1, rz1, held).reshape(10, rows, 128)
    if first:
        d2[0], d2[11] = zero, zero
        k2[...] = halve(k1, 9, -4, 8, cy1, cz1, held).reshape(k2.shape)
        weigh(k2, *w2, 1, 11, 0.25**2, shifts, d2, inside, unroll=U2)
    else:
        weigh(k2, *w2, 1, 11, 0.25**2, shifts, unroll=U2)
    first_sweep(g2, d2, v2, 1, 11, U2)
    residual_of(v2, g2, r2, w2, 3, 9, shifts, d2, unroll=U2)
    total = None
    for i in range(2):
        at = 2 * i + 4
        plane = 0.125 * (r2[at - 1] + r2[at + 2]) + 0.375 * (r2[at] + r2[at + 1])
        value = dot(ry2[i], plane)
        total = value if total is None else total + value
    tile = dot(total, rz2[...])
    if first:
        total = dot(cy2[0], 0.5 * (k2[4] + k2[5])) + dot(cy2[1], 0.5 * (k2[6] + k2[7]))
        tile = tile + dot(total, cz2[...])
    for i in range(out.shape[0]):
        out[i] = tile


def repack(s, out):
    tiles = 2 * s.shape[0] // 16
    lane = lax.broadcasted_iota(jnp.int32, (8, 128), 1) // 16
    row = lax.broadcasted_iota(jnp.int32, (8, 128), 0) // 4
    for field in range(out.shape[1] // tiles):
        for t in range(tiles):
            total = jnp.zeros((8, 128), F32)
            for half in range(2):
                for p in range(8):
                    plane = 16 * t + 8 * half + p
                    part = s[plane // 2]
                    if plane % 2 != half:
                        part = pltpu.roll(part, 4, 0)
                    if p != field:
                        part = pltpu.roll(part, (16 * (p - field)) % 128, 1)
                    total = jnp.where((lane == p) & (row == half), part, total)
            for i in range(out.shape[0]):
                out[i, field * tiles + t] = total


def unpack(s, first, tiles, nz, whole):
    lane = lax.broadcasted_iota(jnp.int32, (8, 128), 1) // 16
    for j in range(s.shape[0] // nz):
        for t in range(tiles):
            for p in range(8):
                total = jnp.zeros((8, 128), F32)
                for q in range(nz):
                    part = s[j * nz + q, first + t]
                    if p != q:
                        part = pltpu.roll(part, (16 * (q - p)) % 128, 1)
                    total = jnp.where(lane == q, part, total)
                whole[16 * t + p + 3, 4 * j : 4 * j + 4] = total[:4]
                whole[16 * t + p + 11, 4 * j : 4 * j + 4] = total[4:]


def bottom(nz, s, k3, scratch, mats):
    g3, v3, r3, w3, d3, b3, k4, g4, v4, w4, d4, b4, held, fine4 = scratch
    ry3, rz3, cy3, cz3, py3, pz3 = mats
    n4 = g4.shape[0]
    n3, two = 2 * n4, s.shape[1] == n4 // 4
    rows, lanes = g3.shape[1], g3.shape[2]
    zero = jnp.zeros((rows, lanes), F32)
    for i in (0, 1, 2, n3 + 3, n3 + 4, n3 + 5):
        v3[i], r3[i] = zero, zero
        if two:
            k3[i] = zero
    for ref in (k4, v4):
        for i in (0, n4 + 1):
            ref[i] = jnp.zeros(ref.shape[1:], F32)
    unpack(s, 0, n3 // 16, nz, g3)
    if two:
        unpack(s, n3 // 16, n3 // 16, nz, k3)
    k4[1 : n4 + 1] = halve(k3, 3, 0, n4, cy3, cz3, held).reshape(g4.shape)
    shifts3 = Closed((rows, lanes), (rows, 16 * nz))
    shifts4 = Closed((k4.shape[1], lanes), (k4.shape[1], 8 * nz))
    w3, w4 = three(w3), three(w4)
    weigh(k3, *w3, 3, n3 + 3, 0.25**3, shifts3, d3, inside, b3, U3)
    weigh(k4, *w4, 1, n4 + 1, 0.25**4, shifts4, d4, inside, b4, U3)
    first_sweep(g3, d3, v3, 3, n3 + 3, U3)
    residual_of(v3, g3, r3, w3, 3, n3 + 3, shifts3, b=b3, unroll=U3)
    g4[...] = restrict(r3, 3, 0, n4, ry3, rz3, held).reshape(g4.shape)
    first_sweep(g4, d4, v4, 1, n4 + 1, U3, by=-1)

    def turn(j, carry):
        smooth(v4, g4, d4, w4, 1, n4 + 1, shifts4, b4, n4, by=-1)
        return carry

    lax.fori_loop(0, CSWEEPS - 1, turn, 0)

    def use(i, value):
        v3[i + 3] = v3[i + 3] + value

    prolong(v4, 0, n4 + 2, py3[...], pz3[...], fine4, use)
    smooth(v3, g3, d3, w3, 3, n3 + 3, shifts3, b3, U3)
    return v3


def spread_matrix(shape, dim_fine, coarse_start, block_fine):
    fine = lax.broadcasted_iota(jnp.int32, shape, dim_fine)
    size = shape[dim_fine]
    fine = jnp.where(fine < (size + block_fine) // 2, fine, fine - size)
    whole = lax.broadcasted_iota(jnp.int32, shape, 1 - dim_fine)
    near = (fine >> 1) + coarse_start
    far = near + 2 * (fine & 1) - 1
    return jnp.where(whole == near, 0.75, jnp.where(whole == far, 0.25, 0.0))


def upward(index, e3, g2, k2, d2, g1, k1, d1, ends, scratch, mats):
    v2, w2, m2, v1, w1, fine2, fine1 = scratch
    py1, pz1 = mats
    shifts, w2, w1 = Open(), three(w2), three(w1)
    weigh(k2, *w2, 1, 11, 0.25**2, shifts, unroll=U2)
    weigh(k1, *w1, 6, 20, 0.25, shifts, unroll=U1)
    first_sweep(g2, d2, v2, 0, 12, U2)
    first_sweep(g1, d1, v1, 5, 21, U1)
    m2[...] = d2[...]
    if ends is not None:
        for ref, i in zip(ends, (0, 11)):
            v2[i], m2[i] = ref[0] * ref[1], ref[1]

    def use2(i, value):
        v2[i] = jnp.where(m2[i] > 0.0, v2[i] + value, 0.0)

    py2 = spread_matrix((g2.shape[1], e3.shape[1]), 0, index[1] * 4, 8)
    pz2 = spread_matrix((e3.shape[2], g2.shape[2]), 1, index[2] * 16, 32)
    prolong(e3, index[0] * 2, 8, py2, pz2, fine2, use2)
    smooth(v2, g2, d2, w2, 1, 11, shifts, unroll=U2)

    def use1(i, value):
        v1[i + 5] = jnp.where(d1[i + 5] > 0.0, v1[i + 5] + value, 0.0)

    prolong(v2, 1, 10, py1[...], pz1[...], fine1, use1)
    smooth(v1, g1, d1, w1, 6, 20, shifts, unroll=U1)
    return v1


BOTTOM = 14
UP = 7


def fetch(sources, targets, sem):
    copies = [
        pltpu.make_async_copy(there, here, sem.at[i])
        for i, (there, here) in enumerate(zip(sources, targets))
    ]
    for copy in copies:
        copy.start()
    return copies


def middle(nz, index, f_, wx_, wy_, wz_, d_, k_, s, g2, k2, d2, g1, k1, d1, *refs):
    ends, m3, m1, (py0, pz0, ry, rz), (v_, gn, turned, k3) = refs[:2], refs[2:8], refs[8:10], refs[10:14], refs[14:18]
    low, mid, (fine0, r, held0, f, wx, wy, wz, d, k, v, sem) = refs[18:32], refs[32:39], refs[39:]
    copies = fetch((f_, wx_, wy_, wz_, d_, k_), (f, wx, wy, wz, d, k), sem)
    e3 = bottom(nz, s, k3, low, m3)
    e1 = upward(index, e3, g2, k2, d2, g1, k1, d1, ends, mid, m1)
    for copy in copies:
        copy.wait()
    w, shifts = (wx, wy, wz), Open()

    def use(i, value):
        v[i + 1] = inside(k[i + 1], f[i + 1] * d[i + 1] + value)

    prolong(e1, 6, 14, py0[...], pz0[...], fine0, use)
    smooth(v, f, d, w, 2, 24, shifts, unroll=U0)
    smooth(v, f, d, w, 3, 23, shifts, unroll=U0)
    copy = pltpu.make_async_copy(v, v_, sem.at[0])
    copy.start()
    residual_of(v, f, r, w, 4, 22, shifts, k, unroll=U0)
    value = restrict(r, 5, 0, 8, ry, rz, held0)
    gn[...] = value.reshape(gn.shape)
    turned[...] = pltpu.roll(value, 64, 1).reshape(gn.shape)
    copy.wait()


def final(nz, index, f_, wx_, wy_, wz_, d_, k_, v_, s, g2, k2, d2, g1, k1, d1, *refs):
    m3, m1, (py0, pz0, k3), (solution_, residual_) = refs[:6], refs[6:8], refs[8:11], refs[11:13]
    low, mid, (fine0, f, wx, wy, wz, d, k, v, sem) = refs[13:27], refs[27:34], refs[34:]
    copies = fetch((f_, wx_, wy_, wz_, d_, k_, v_), (f, wx, wy, wz, d, k, v), sem)
    e3 = bottom(nz, s, k3, low, m3)
    e1 = upward(index, e3, g2, k2, d2, g1, k1, d1, None, mid, m1)
    for copy in copies:
        copy.wait()
    w, shifts = (wx, wy, wz), Open()

    def use(i, value):
        v[i + 3] = inside(k[i + 3], v[i + 3] + value)

    prolong(e1, 7, 12, py0[...], pz0[...], fine0, use)
    smooth(v, f, d, w, 4, 22, shifts, unroll=U0)

    def last(i, here, im):
        return here[:32, :128], (f[i] - im)[:32, :128]

    def out(i, values):
        solution_[i - 5], residual_[i - 5] = values

    image(v, *w, 5, 21, last, out, shifts, unroll=U0)


def call(kernel, outs, scratch, *args, name, scalars=0, loose=0, away=0, sems=0):
    vmem = pl.BlockSpec(memory_space=pltpu.VMEM)
    smem = pl.BlockSpec(memory_space=pltpu.SMEM)
    hbm = pl.BlockSpec(memory_space=pl.ANY)
    return pl.pallas_call(
        kernel,
        out_shape=[jax.ShapeDtypeStruct(o, F32) for o in outs],
        in_specs=[smem] * scalars + [hbm] * loose + [vmem] * (len(args) - scalars - loose),
        out_specs=[hbm] * away + [vmem] * (len(outs) - away),
        scratch_shapes=[pltpu.VMEM(s, F32) for s in scratch]
        + ([pltpu.SemaphoreType.DMA((sems,))] if sems else []),
        compiler_params=pltpu.CompilerParams(vmem_limit_bytes=56 << 20),
        name=name,
    )(*args)


def neighbours(last, initial, axis):
    count = lax.axis_size(axis)
    if axis == "gz":
        up = [(i, (i + 1) % count) for i in range(count)]
    else:
        up = [(i, i + 1) for i in range(count - 1)]
    down = [(j, i) for i, j in up]
    before = lax.ppermute(last, axis, up)
    after = lax.ppermute(initial, axis, down)
    if axis == "gz":
        at = lax.axis_index(axis)
        before = jnp.where(at == 0, 0.0, before)
        after = jnp.where(at == count - 1, 0.0, after)
    return before, after


def finest(fields):
    for axis, dim, size, count, width in (("gz", 2, 128, 256, 25), ("gy", 1, 32, 48, 5)):
        along = 2 if dim == 2 else 0
        last = [lax.slice_in_dim(v, size - width, size, axis=dim) for v in fields]
        initial = [lax.slice_in_dim(v, 0, width, axis=dim) for v in fields]
        before, after = neighbours(
            jnp.concatenate(last, along), jnp.concatenate(initial, along), axis
        )
        before, after = jnp.split(before, 2, along), jnp.split(after, 2, along)
        gap = list(fields[0].shape)
        gap[dim] = count - size - 2 * width
        gap = jnp.zeros(gap, F32)
        fields = [
            jnp.concatenate([v, a, gap, b], dim) for b, v, a in zip(before, fields, after)
        ]
    last = jnp.concatenate([v[11:] for v in fields])
    initial = jnp.concatenate([v[:5] for v in fields])
    before, after = neighbours(last, initial, "gx")
    return before, *fields, after


def rows1(values):
    before, after = neighbours(values, values, "gy")
    gap = jnp.zeros((values.shape[0], 2, 128), F32)
    return jnp.concatenate([values, after[:, :11], gap, before[:, 5:]], 1)


def lanes1(values, turned):
    before, after = neighbours(turned, turned, "gz")
    lane = jnp.arange(128)
    zero = jnp.where(lane >= 117, before, 0.0)
    return jnp.where(lane < 64, values, jnp.where(lane < 75, after, zero))


def everyone(pieces, axes):
    return lax.all_to_all(pieces, axes, 0, 0)


def body(right_side, conductivity):
    nx, ny, nz = (lax.axis_size(axis) for axis in ("gx", "gy", "gz"))
    index = jnp.stack([lax.axis_index(axis) for axis in ("gx", "gy", "gz")]).astype(jnp.int32)

    def ends(size, count, away=-1000, start=0):
        at = np.arange(size)
        return np.where((at >= start) & (at < start + count), at - start, away)

    y0, z0 = coords(48, 32), coords(256, 128)
    y1, z1 = coords(40, 16), coords(128, 64)
    y2, z2 = coords(24, 8), coords(128, 32)
    rows3, rows4 = np.arange(4 * ny), np.arange(2 * ny)
    lanes3, lanes4 = ends(128, 16 * nz, -3000), ends(128, 8 * nz, -9000)
    ry0, rz0 = restriction(np.arange(16), y0), restriction(z1, z0).T
    cy0, cz0 = halving(np.arange(16), y0), halving(z1, z0).T
    ry1, rz1 = restriction(y2, y1), restriction(z2, z1).T
    cy1, cz1 = halving(y2, y1), halving(z2, z1).T

    def both(matrix):
        zero = np.zeros_like(matrix)
        return np.stack([np.concatenate([matrix, zero]), np.concatenate([zero, matrix])])

    ry2, rz2 = both(restriction(np.arange(4), y2)), restriction(ends(128, 16), z2).T
    cy2, cz2 = both(halving(np.arange(4), y2)), halving(ends(128, 16, start=16), z2).T
    ry3, rz3 = restriction(rows4, rows3), restriction(lanes4, lanes3).T
    cy3, cz3 = halving(rows4, rows3), halving(lanes4, lanes3).T
    py0, pz0 = prolongation(y0, y1), prolongation(z0, z1).T
    py1, pz1 = prolongation(y1, y2), prolongation(z1, z2).T
    py3, pz3 = prolongation(rows3, rows4), prolongation(lanes3, lanes4).T
    m3, m1 = (ry3, rz3, cy3, cz3, py3, pz3), (py1, pz1)

    wide, l1, l2 = (26, 48, 256), (26, 40, 128), (12, 24, 128)
    n3, n4 = (2 * nx + 6, 4 * ny, 128), (nx + 2, 2 * ny, 128)
    low = [
        n3, n3, n3, (3,) + n3, n3, n3,
        n4, (nx, 2 * ny, 128), n4, (3,) + n4, n4, n4,
        (nx * 2 * ny, 128), (nx + 2, 4 * ny, 128),
    ]
    mid = [l2, (3,) + l2, l2, l1, (3,) + l1, (8, 24, 128), (10, 40, 128)]
    tiles = nx // 8

    f, k, wx, wy, wz, d, both1 = call(
        down0, [wide] * 6 + [(20, 16, 128)], [wide] * 8 + [(160, 256)],
        *finest([right_side, conductivity]), ry0, rz0, cy0, cz0, name="down0", away=6, sems=6,
    )
    own = rows1(both1)
    last = jnp.concatenate([own[0:9], own[10:19]])
    initial = jnp.concatenate([own[1:10], own[11:20]])
    before, after = neighbours(last, initial, "gx")
    inner = [l1, l1, (288, 128), (3,) + l1, l2, l2, (3,) + l2, (8, 128)]
    pieces, g1, k1, d1, g2, k2, d2 = call(
        functools.partial(descend, True), [(nx, 8, 128), l1, l1, l1, l2, l2, l2], inner,
        before, own, after, ry1, rz1, ry2, rz2, cy1, cz1, cy2, cz2, name="descend",
    )
    first, last = jnp.stack([g2[4], d2[4]]), jnp.stack([g2[7], d2[7]])
    outer = neighbours(first, last, "gx")
    pieces = everyone(pieces, "gx")
    (pieces,) = call(repack, [(ny * nz, 2 * tiles, 8, 128)], [], pieces, name="repack")
    s = everyone(pieces, ("gy", "gz"))
    fields = (f, wx, wy, wz, d, k)
    v, value, turned, k3 = call(
        functools.partial(middle, nz), [wide, (8, 16, 128), (8, 16, 128), n3],
        low + mid + [(14, 48, 256), wide, (128, 256)] + [wide] * 7,
        index, *fields, s, g2, k2, d2, g1, k1, d1, *outer, *m3, *m1, py0, pz0, ry0, rz0,
        name="middle", scalars=1, loose=6, away=1, sems=6,
    )
    own = rows1(lanes1(value, turned))
    before, after = neighbours(own, own, "gx")
    pieces, g1, g2 = call(
        functools.partial(descend, False), [(nx, 8, 128), l1, l2], inner,
        before, own, after, k1, d1, k2, d2, ry1, rz1, ry2, rz2, name="again",
    )
    pieces = everyone(pieces, "gx")
    (pieces,) = call(repack, [(ny * nz, tiles, 8, 128)], [], pieces, name="repack2")
    s = everyone(pieces, ("gy", "gz"))
    return tuple(call(
        functools.partial(final, nz), [(16, 32, 128)] * 2,
        low + mid + [(12, 48, 256)] + [wide] * 7,
        index, *fields, v, s, g2, k2, d2, g1, k1, d1, *m3, *m1, py0, pz0, k3,
        name="final", scalars=1, loose=7, sems=7,
    ))


def solution(mesh):
    placed = P("gx", "gy", "gz")
    return jax.shard_map(
        body, mesh=mesh, in_specs=(placed, placed), out_specs=(placed, placed), check_vma=False
    )
```

```python
import functools

import jax
import jax.numpy as jnp
import numpy as np
from jax import lax
from jax.experimental import pallas as pl
from jax.experimental.pallas import tpu as pltpu
from jax.sharding import PartitionSpec as P

LEVELS = 4
CSWEEPS = 6
absorption = 0.01
relaxation = 0.8
F32 = jnp.float32


def coords(n, b):
    at = np.arange(n)
    return np.where(at < (n + b) // 2, at, at - n)


def restriction(coarse, fine):
    gap = fine[None, :] - 2 * coarse[:, None]
    outer, inner = (gap == -1) | (gap == 2), (gap == 0) | (gap == 1)
    return np.where(outer, 0.125, np.where(inner, 0.375, 0.0)).astype(np.float32)


def halving(coarse, fine):
    return np.where(fine[None, :] // 2 == coarse[:, None], 0.5, 0.0).astype(np.float32)


def prolongation(fine, coarse):
    near = fine[:, None] // 2 == coarse[None, :]
    far = fine[:, None] // 2 + 2 * (fine[:, None] % 2) - 1 == coarse[None, :]
    return np.where(near, 0.75, np.where(far, 0.25, 0.0)).astype(np.float32)


def dot(a, b):
    return lax.dot_general(
        a, b, (((1,), (0,)), ((), ())),
        precision=lax.Precision.HIGHEST, preferred_element_type=F32,
    )


def planes(lo, hi, step, carry=0, unroll=1):
    whole = (hi - lo) // unroll
    if whole > 1:
        carry = lax.fori_loop(0, whole, lambda t, c: step(lo + t * unroll, unroll, c), carry)
    elif whole == 1:
        carry = step(lo, unroll, carry)
    rest = (hi - lo) % unroll
    return step(hi - rest, rest, carry) if rest else carry


class Open:
    def above(self, v, dim):
        return pltpu.roll(v, v.shape[dim] - 1, dim)

    def below(self, v, dim):
        return pltpu.roll(v, 1, dim)

    def closed(self, k):
        return None


class Closed(Open):
    def __init__(self, shape, counts):
        self.last, self.first = [], []
        for dim in range(2):
            at = lax.broadcasted_iota(jnp.int32, shape, dim)
            self.last.append(jnp.where(at == counts[dim] - 1, 0.0, 1.0))
            self.first.append(jnp.where(at == 0, 0.0, 1.0))

    def above(self, v, dim):
        return super().above(v, dim) * self.last[dim]

    def below(self, v, dim):
        return super().below(v, dim) * self.first[dim]

    def closed(self, k):
        return k * ((1.0 - self.first[0]) + (1.0 - self.first[1]))


def weigh(k, wx, wy, wz, lo, hi, factor, shifts, d=None, mask=None, b=None, unroll=1):
    half = 0.5 * factor
    first = half * (k[lo - 1] + k[lo])
    wx[lo - 1] = first

    def step(i, n, below):
        here = [k[i + j] for j in range(n + 1)]
        outs = []
        for j in range(n):
            x = half * (here[j] + here[j + 1])
            y = half * (here[j] + shifts.above(here[j], 0))
            z = half * (here[j] + shifts.above(here[j], 1))
            ends, value = shifts.closed(half * here[j]), None
            if d is not None:
                value = (x + below) + (y + shifts.below(y, 0)) + (z + shifts.below(z, 1))
                if ends is not None:
                    value = value + ends
                value = relaxation / (value + absorption)
                if mask is not None:
                    value = mask(here[j], value)
            outs.append((x, y, z, ends, value))
            below = x
        for j, (x, y, z, ends, value) in enumerate(outs):
            wx[i + j], wy[i + j], wz[i + j] = x, y, z
            if ends is not None:
                b[i + j] = ends
            if value is not None:
                d[i + j] = value
        return below

    planes(lo, hi, step, first, unroll)


def image(v, wx, wy, wz, lo, hi, use, put, shifts, b=None, unroll=1):
    def step(i, n, below):
        here = [v[i + j] for j in range(n + 1)]
        outs = []
        for j in range(n):
            x = wx[i + j] * (here[j] - here[j + 1])
            y = wy[i + j] * (here[j] - shifts.above(here[j], 0))
            z = wz[i + j] * (here[j] - shifts.above(here[j], 1))
            total = (x - below) + (y - shifts.below(y, 0)) + (z - shifts.below(z, 1))
            if b is not None:
                total = total + b[i + j] * here[j]
            outs.append(use(i + j, here[j], total + absorption * here[j]))
            below = x
        for j, value in enumerate(outs):
            put(i + j, value)
        return below

    planes(lo, hi, step, wx[lo - 1] * (v[lo - 1] - v[lo]), unroll)


def into(ref, by=0):
    def put(i, value):
        ref[i + by] = value

    return put


def smooth(v, f, d, w, lo, hi, shifts, b=None, unroll=1, by=0):
    def use(i, here, im):
        return here + d[i] * (f[i + by] - im)

    image(v, *w, lo, hi, use, into(v), shifts, b, unroll)


def residual_of(v, f, r, w, lo, hi, shifts, mask=None, b=None, unroll=1):
    def use(i, here, im):
        value = f[i] - im
        return value if mask is None else jnp.where(mask[i] > 0.0, value, 0.0)

    image(v, *w, lo, hi, use, into(r), shifts, b, unroll)


def first_sweep(g, d, v, lo, hi, unroll, by=0):
    def step(i, n, carry):
        values = [g[i + j + by] * d[i + j] for j in range(n)]
        for j, value in enumerate(values):
            v[i + j] = value
        return carry

    planes(lo, hi, step, unroll=unroll)


def restrict(r, offset, lo, hi, ry, rz, held):
    size = ry.shape[0]
    for i in range(lo, hi):
        at = 2 * i + offset
        plane = 0.125 * (r[at - 1] + r[at + 2]) + 0.375 * (r[at] + r[at + 1])
        held[(i - lo) * size : (i - lo + 1) * size, :] = dot(ry[...], plane)
    return dot(held[: (hi - lo) * size, :], rz[...])


def halve(k, offset, lo, hi, cy, cz, held):
    size = cy.shape[0]
    for i in range(lo, hi):
        plane = 0.5 * (k[2 * i + offset] + k[2 * i + 1 + offset])
        held[(i - lo) * size : (i - lo + 1) * size, :] = dot(cy[...], plane)
    return dot(held[: (hi - lo) * size, :], cz[...])


def prolong(e, first, count, py, pz, finer, use):
    rows = e.shape[1]
    spread = dot(e[pl.ds(first, count)].reshape(count * rows, e.shape[2]), pz)
    for i in range(count):
        finer[i] = dot(py, spread[i * rows : (i + 1) * rows])

    def step(i, n, carry):
        below, here, above = finer[i - 1], finer[i], finer[i + 1]
        use(2 * (i - 1), 0.75 * here + 0.25 * below)
        use(2 * (i - 1) + 1, 0.75 * here + 0.25 * above)
        return carry

    planes(1, count - 1, step)


def three(w):
    return tuple(w.at[i] for i in range(3))


def inside(k, value):
    return jnp.where(k > 0.0, value, 0.0)


U0, U1, U2, U3 = 6, 12, 10, 16


def place(target, at, source, start, count, unroll=4):
    def step(i, n, carry):
        values = [source[start + i + j] for j in range(n)]
        for j, value in enumerate(values):
            target[at + i + j] = value
        return carry

    planes(0, count, step, unroll=unroll)


def down0(before, fo, ko, after, ry, rz, cy, cz, f, k, wx, wy, wz, d, out, v, r, held):
    shifts = Open()
    for ref, own, at in ((f, fo, 0), (k, ko, 5)):
        place(ref, 0, before, at, 5, 5)
        place(ref, 5, own, 0, 16)
        place(ref, 21, after, at, 5, 5)
    weigh(k, wx, wy, wz, 1, 25, 1.0, shifts, d, inside, unroll=U0)
    first_sweep(f, d, v, 1, 25, U0)
    residual_of(v, f, r, (wx, wy, wz), 2, 24, shifts, k, unroll=U0)
    out[:10] = restrict(r, 5, -1, 9, ry, rz, held).reshape(10, 16, 128)
    out[10:] = halve(k, 5, -1, 9, cy, cz, held).reshape(10, 16, 128)


def descend(first, *refs):
    shifts = Open()
    before, own, after = refs[:3]
    if first:
        ry1, rz1, ry2, rz2, cy1, cz1, cy2, cz2 = refs[3:11]
        out, g1, k1, d1, g2, k2, d2 = refs[11:18]
        for ref, at in ((g1, 0), (k1, 1)):
            place(ref, 0, before, 9 * at, 9, 9)
            place(ref, 9, own, 10 * at + 1, 8, 8)
            place(ref, 17, after, 9 * at, 9, 9)
    else:
        k1, d1, k2, d2, ry1, rz1, ry2, rz2 = refs[3:11]
        out, g1, g2 = refs[11:14]
        zero = jnp.zeros(g1.shape[1:], F32)
        g1[0], g1[25] = zero, zero
        for ref, at in ((before, 1), (own, 9), (after, 17)):
            place(g1, at, ref, 0, 8, 8)
    v1, r1, held, w1, v2, r2, w2, part = refs[-8:]
    w1, w2 = three(w1), three(w2)
    rows = g2.shape[1]
    if first:
        zero = jnp.zeros(d1.shape[1:], F32)
        d1[0], d1[25] = zero, zero
        weigh(k1, *w1, 1, 25, 0.25, shifts, d1, inside, unroll=U1)
    else:
        weigh(k1, *w1, 1, 25, 0.25, shifts, unroll=U1)
    first_sweep(g1, d1, v1, 1, 25, U1)
    residual_of(v1, g1, r1, w1, 2, 24, shifts, d1, unroll=U1)
    zero = jnp.zeros(g2.shape[1:], F32)
    g2[0], g2[11] = zero, zero
    g2[1:11] = restrict(r1, 9, -3, 7, ry1, rz1, held).reshape(10, rows, 128)
    if first:
        d2[0], d2[11] = zero, zero
        k2[...] = halve(k1, 9, -4, 8, cy1, cz1, held).reshape(k2.shape)
        weigh(k2, *w2, 1, 11, 0.25**2, shifts, d2, inside, unroll=U2)
    else:
        weigh(k2, *w2, 1, 11, 0.25**2, shifts, unroll=U2)
    first_sweep(g2, d2, v2, 1, 11, U2)
    residual_of(v2, g2, r2, w2, 3, 9, shifts, d2, unroll=U2)
    total = None
    for i in range(2):
        at = 2 * i + 4
        plane = 0.125 * (r2[at - 1] + r2[at + 2]) + 0.375 * (r2[at] + r2[at + 1])
        value = dot(ry2[i], plane)
        total = value if total is None else total + value
    tile = dot(total, rz2[...])
    if first:
        total = dot(cy2[0], 0.5 * (k2[4] + k2[5])) + dot(cy2[1], 0.5 * (k2[6] + k2[7]))
        tile = tile + dot(total, cz2[...])
    for i in range(out.shape[0]):
        out[i] = tile


def repack(s, out):
    tiles = 2 * s.shape[0] // 16
    lane = lax.broadcasted_iota(jnp.int32, (8, 128), 1) // 16
    row = lax.broadcasted_iota(jnp.int32, (8, 128), 0) // 4
    for field in range(out.shape[1] // tiles):
        for t in range(tiles):
            total = jnp.zeros((8, 128), F32)
            for half in range(2):
                for p in range(8):
                    plane = 16 * t + 8 * half + p
                    part = s[plane // 2]
                    if plane % 2 != half:
                        part = pltpu.roll(part, 4, 0)
                    if p != field:
                        part = pltpu.roll(part, (16 * (p - field)) % 128, 1)
                    total = jnp.where((lane == p) & (row == half), part, total)
            for i in range(out.shape[0]):
                out[i, field * tiles + t] = total


def unpack(s, first, tiles, nz, whole):
    lane = lax.broadcasted_iota(jnp.int32, (8, 128), 1) // 16
    for j in range(s.shape[0] // nz):
        for t in range(tiles):
            for p in range(8):
                total = jnp.zeros((8, 128), F32)
                for q in range(nz):
                    part = s[j * nz + q, first + t]
                    if p != q:
                        part = pltpu.roll(part, (16 * (q - p)) % 128, 1)
                    total = jnp.where(lane == q, part, total)
                whole[16 * t + p + 3, 4 * j : 4 * j + 4] = total[:4]
                whole[16 * t + p + 11, 4 * j : 4 * j + 4] = total[4:]


def bottom(nz, s, k3, scratch, mats):
    g3, v3, r3, w3, d3, b3, k4, g4, v4, w4, d4, b4, held, fine4 = scratch
    ry3, rz3, cy3, cz3, py3, pz3 = mats
    n4 = g4.shape[0]
    n3, two = 2 * n4, s.shape[1] == n4 // 4
    rows, lanes = g3.shape[1], g3.shape[2]
    zero = jnp.zeros((rows, lanes), F32)
    for i in (0, 1, 2, n3 + 3, n3 + 4, n3 + 5):
        v3[i], r3[i] = zero, zero
        if two:
            k3[i] = zero
    for ref in (k4, v4):
        for i in (0, n4 + 1):
            ref[i] = jnp.zeros(ref.shape[1:], F32)
    unpack(s, 0, n3 // 16, nz, g3)
    if two:
        unpack(s, n3 // 16, n3 // 16, nz, k3)
    k4[1 : n4 + 1] = halve(k3, 3, 0, n4, cy3, cz3, held).reshape(g4.shape)
    shifts3 = Closed((rows, lanes), (rows, 16 * nz))
    shifts4 = Closed((k4.shape[1], lanes), (k4.shape[1], 8 * nz))
    w3, w4 = three(w3), three(w4)
    weigh(k3, *w3, 3, n3 + 3, 0.25**3, shifts3, d3, inside, b3, U3)
    weigh(k4, *w4, 1, n4 + 1, 0.25**4, shifts4, d4, inside, b4, U3)
    first_sweep(g3, d3, v3, 3, n3 + 3, U3)
    residual_of(v3, g3, r3, w3, 3, n3 + 3, shifts3, b=b3, unroll=U3)
    g4[...] = restrict(r3, 3, 0, n4, ry3, rz3, held).reshape(g4.shape)
    first_sweep(g4, d4, v4, 1, n4 + 1, U3, by=-1)

    def turn(j, carry):
        smooth(v4, g4, d4, w4, 1, n4 + 1, shifts4, b4, n4, by=-1)
        return carry

    lax.fori_loop(0, CSWEEPS - 1, turn, 0)

    def use(i, value):
        v3[i + 3] = v3[i + 3] + value

    prolong(v4, 0, n4 + 2, py3[...], pz3[...], fine4, use)
    smooth(v3, g3, d3, w3, 3, n3 + 3, shifts3, b3, U3)
    return v3


def spread_matrix(shape, dim_fine, coarse_start, block_fine):
    fine = lax.broadcasted_iota(jnp.int32, shape, dim_fine)
    size = shape[dim_fine]
    fine = jnp.where(fine < (size + block_fine) // 2, fine, fine - size)
    whole = lax.broadcasted_iota(jnp.int32, shape, 1 - dim_fine)
    near = (fine >> 1) + coarse_start
    far = near + 2 * (fine & 1) - 1
    return jnp.where(whole == near, 0.75, jnp.where(whole == far, 0.25, 0.0))


def upward(index, e3, g2, k2, d2, g1, k1, d1, ends, scratch, mats):
    v2, w2, m2, v1, w1, fine2, fine1 = scratch
    py1, pz1 = mats
    shifts, w2, w1 = Open(), three(w2), three(w1)
    weigh(k2, *w2, 1, 11, 0.25**2, shifts, unroll=U2)
    weigh(k1, *w1, 6, 20, 0.25, shifts, unroll=U1)
    first_sweep(g2, d2, v2, 0, 12, U2)
    first_sweep(g1, d1, v1, 5, 21, U1)
    m2[...] = d2[...]
    if ends is not None:
        for ref, i in zip(ends, (0, 11)):
            v2[i], m2[i] = ref[0] * ref[1], ref[1]

    def use2(i, value):
        v2[i] = jnp.where(m2[i] > 0.0, v2[i] + value, 0.0)

    py2 = spread_matrix((g2.shape[1], e3.shape[1]), 0, index[1] * 4, 8)
    pz2 = spread_matrix((e3.shape[2], g2.shape[2]), 1, index[2] * 16, 32)
    prolong(e3, index[0] * 2, 8, py2, pz2, fine2, use2)
    smooth(v2, g2, d2, w2, 1, 11, shifts, unroll=U2)

    def use1(i, value):
        v1[i + 5] = jnp.where(d1[i + 5] > 0.0, v1[i + 5] + value, 0.0)

    prolong(v2, 1, 10, py1[...], pz1[...], fine1, use1)
    smooth(v1, g1, d1, w1, 6, 20, shifts, unroll=U1)
    return v1


BOTTOM = 14
UP = 7


def middle(nz, index, f, wx, wy, wz, d, k, s, g2, k2, d2, g1, k1, d1, *refs):
    ends, m3, m1, (py0, pz0, ry, rz), (v, gn, turned, k3) = refs[:2], refs[2:8], refs[8:10], refs[10:14], refs[14:18]
    low, mid, (fine0, r, held0) = refs[18:32], refs[32:39], refs[39:]
    e3 = bottom(nz, s, k3, low, m3)
    e1 = upward(index, e3, g2, k2, d2, g1, k1, d1, ends, mid, m1)
    w, shifts = (wx, wy, wz), Open()

    def use(i, value):
        v[i + 1] = inside(k[i + 1], f[i + 1] * d[i + 1] + value)

    prolong(e1, 6, 14, py0[...], pz0[...], fine0, use)
    smooth(v, f, d, w, 2, 24, shifts, unroll=U0)
    smooth(v, f, d, w, 3, 23, shifts, unroll=U0)
    residual_of(v, f, r, w, 4, 22, shifts, k, unroll=U0)
    value = restrict(r, 5, 0, 8, ry, rz, held0)
    gn[...] = value.reshape(gn.shape)
    turned[...] = pltpu.roll(value, 64, 1).reshape(gn.shape)


def final(nz, index, f, wx, wy, wz, d, k, v0, s, g2, k2, d2, g1, k1, d1, *refs):
    m3, m1, (py0, pz0, k3), (solution_, residual_) = refs[:6], refs[6:8], refs[8:11], refs[11:13]
    low, mid, (fine0, v) = refs[13:27], refs[27:34], refs[34:]
    e3 = bottom(nz, s, k3, low, m3)
    e1 = upward(index, e3, g2, k2, d2, g1, k1, d1, None, mid, m1)
    w, shifts = (wx, wy, wz), Open()

    def use(i, value):
        v[i + 3] = inside(k[i + 3], v0[i + 3] + value)

    prolong(e1, 7, 12, py0[...], pz0[...], fine0, use)
    smooth(v, f, d, w, 4, 22, shifts, unroll=U0)

    def last(i, here, im):
        return here[:32, :128], (f[i] - im)[:32, :128]

    def out(i, values):
        solution_[i - 5], residual_[i - 5] = values

    image(v, *w, 5, 21, last, out, shifts, unroll=U0)


def call(kernel, outs, scratch, *args, name, scalars=0, room=4):
    vmem = pl.BlockSpec(memory_space=pltpu.VMEM)
    smem = pl.BlockSpec(memory_space=pltpu.SMEM)
    return pl.pallas_call(
        kernel,
        out_shape=[jax.ShapeDtypeStruct(o, F32) for o in outs],
        in_specs=[smem] * scalars + [vmem] * (len(args) - scalars),
        out_specs=[vmem] * len(outs),
        scratch_shapes=[pltpu.VMEM(s, F32) for s in scratch],
        compiler_params=pltpu.CompilerParams(vmem_limit_bytes=room << 20),
        name=name,
    )(*args)


def neighbours(last, initial, axis):
    count = lax.axis_size(axis)
    if axis == "gz":
        up = [(i, (i + 1) % count) for i in range(count)]
    else:
        up = [(i, i + 1) for i in range(count - 1)]
    down = [(j, i) for i, j in up]
    before = lax.ppermute(last, axis, up)
    after = lax.ppermute(initial, axis, down)
    if axis == "gz":
        at = lax.axis_index(axis)
        before = jnp.where(at == 0, 0.0, before)
        after = jnp.where(at == count - 1, 0.0, after)
    return before, after


def finest(fields):
    for axis, dim, size, count, width in (("gz", 2, 128, 256, 25), ("gy", 1, 32, 48, 5)):
        along = 2 if dim == 2 else 0
        last = [lax.slice_in_dim(v, size - width, size, axis=dim) for v in fields]
        initial = [lax.slice_in_dim(v, 0, width, axis=dim) for v in fields]
        before, after = neighbours(
            jnp.concatenate(last, along), jnp.concatenate(initial, along), axis
        )
        before, after = jnp.split(before, 2, along), jnp.split(after, 2, along)
        gap = list(fields[0].shape)
        gap[dim] = count - size - 2 * width
        gap = jnp.zeros(gap, F32)
        fields = [
            jnp.concatenate([v, a, gap, b], dim) for b, v, a in zip(before, fields, after)
        ]
    last = jnp.concatenate([v[11:] for v in fields])
    initial = jnp.concatenate([v[:5] for v in fields])
    before, after = neighbours(last, initial, "gx")
    return before, *fields, after


def rows1(values):
    before, after = neighbours(values, values, "gy")
    gap = jnp.zeros((values.shape[0], 2, 128), F32)
    return jnp.concatenate([values, after[:, :11], gap, before[:, 5:]], 1)


def lanes1(values, turned):
    before, after = neighbours(turned, turned, "gz")
    lane = jnp.arange(128)
    zero = jnp.where(lane >= 117, before, 0.0)
    return jnp.where(lane < 64, values, jnp.where(lane < 75, after, zero))


def everyone(pieces, axes):
    return lax.all_to_all(pieces, axes, 0, 0)


def body(right_side, conductivity):
    nx, ny, nz = (lax.axis_size(axis) for axis in ("gx", "gy", "gz"))
    index = jnp.stack([lax.axis_index(axis) for axis in ("gx", "gy", "gz")]).astype(jnp.int32)

    def ends(size, count, away=-1000, start=0):
        at = np.arange(size)
        return np.where((at >= start) & (at < start + count), at - start, away)

    y0, z0 = coords(48, 32), coords(256, 128)
    y1, z1 = coords(40, 16), coords(128, 64)
    y2, z2 = coords(24, 8), coords(128, 32)
    rows3, rows4 = np.arange(4 * ny), np.arange(2 * ny)
    lanes3, lanes4 = ends(128, 16 * nz, -3000), ends(128, 8 * nz, -9000)
    ry0, rz0 = restriction(np.arange(16), y0), restriction(z1, z0).T
    cy0, cz0 = halving(np.arange(16), y0), halving(z1, z0).T
    ry1, rz1 = restriction(y2, y1), restriction(z2, z1).T
    cy1, cz1 = halving(y2, y1), halving(z2, z1).T

    def both(matrix):
        zero = np.zeros_like(matrix)
        return np.stack([np.concatenate([matrix, zero]), np.concatenate([zero, matrix])])

    ry2, rz2 = both(restriction(np.arange(4), y2)), restriction(ends(128, 16), z2).T
    cy2, cz2 = both(halving(np.arange(4), y2)), halving(ends(128, 16, start=16), z2).T
    ry3, rz3 = restriction(rows4, rows3), restriction(lanes4, lanes3).T
    cy3, cz3 = halving(rows4, rows3), halving(lanes4, lanes3).T
    py0, pz0 = prolongation(y0, y1), prolongation(z0, z1).T
    py1, pz1 = prolongation(y1, y2), prolongation(z1, z2).T
    py3, pz3 = prolongation(rows3, rows4), prolongation(lanes3, lanes4).T
    m3, m1 = (ry3, rz3, cy3, cz3, py3, pz3), (py1, pz1)

    wide, l1, l2 = (26, 48, 256), (26, 40, 128), (12, 24, 128)
    n3, n4 = (2 * nx + 6, 4 * ny, 128), (nx + 2, 2 * ny, 128)
    low = [
        n3, n3, n3, (3,) + n3, n3, n3,
        n4, (nx, 2 * ny, 128), n4, (3,) + n4, n4, n4,
        (nx * 2 * ny, 128), (nx + 2, 4 * ny, 128),
    ]
    mid = [l2, (3,) + l2, l2, l1, (3,) + l1, (8, 24, 128), (10, 40, 128)]
    tiles = nx // 8

    f, k, wx, wy, wz, d, both1 = call(
        down0, [wide] * 6 + [(20, 16, 128)], [wide] * 2 + [(160, 256)],
        *finest([right_side, conductivity]), ry0, rz0, cy0, cz0, name="down0", room=6,
    )
    own = rows1(both1)
    last = jnp.concatenate([own[0:9], own[10:19]])
    initial = jnp.concatenate([own[1:10], own[11:20]])
    before, after = neighbours(last, initial, "gx")
    inner = [l1, l1, (288, 128), (3,) + l1, l2, l2, (3,) + l2, (8, 128)]
    pieces, g1, k1, d1, g2, k2, d2 = call(
        functools.partial(descend, True), [(nx, 8, 128), l1, l1, l1, l2, l2, l2], inner,
        before, own, after, ry1, rz1, ry2, rz2, cy1, cz1, cy2, cz2, name="descend", room=14,
    )
    first, last = jnp.stack([g2[4], d2[4]]), jnp.stack([g2[7], d2[7]])
    outer = neighbours(first, last, "gx")
    pieces = everyone(pieces, "gx")
    (pieces,) = call(repack, [(ny * nz, 2 * tiles, 8, 128)], [], pieces, name="repack")
    s = everyone(pieces, ("gy", "gz"))
    fields = (f, wx, wy, wz, d, k)
    v, value, turned, k3 = call(
        functools.partial(middle, nz), [wide, (8, 16, 128), (8, 16, 128), n3],
        low + mid + [(14, 48, 256), wide, (128, 256)],
        index, *fields, s, g2, k2, d2, g1, k1, d1, *outer, *m3, *m1, py0, pz0, ry0, rz0,
        name="middle", room=14, scalars=1,
    )
    own = rows1(lanes1(value, turned))
    before, after = neighbours(own, own, "gx")
    pieces, g1, g2 = call(
        functools.partial(descend, False), [(nx, 8, 128), l1, l2], inner,
        before, own, after, k1, d1, k2, d2, ry1, rz1, ry2, rz2, name="again", room=14,
    )
    pieces = everyone(pieces, "gx")
    (pieces,) = call(repack, [(ny * nz, tiles, 8, 128)], [], pieces, name="repack2")
    s = everyone(pieces, ("gy", "gz"))
    return tuple(call(
        functools.partial(final, nz), [(16, 32, 128)] * 2,
        low + mid + [(12, 48, 256), wide],
        index, *fields, v, s, g2, k2, d2, g1, k1, d1, *m3, *m1, py0, pz0, k3,
        name="final", room=14, scalars=1,
    ))


def solution(mesh):
    placed = P("gx", "gy", "gz")
    return jax.shard_map(
        body, mesh=mesh, in_specs=(placed, placed), out_specs=(placed, placed), check_vma=False
    )
```

```python
import functools

import jax
import jax.numpy as jnp
from jax import lax
from jax.experimental import pallas as pl
from jax.experimental.pallas import tpu as pltpu
from jax.sharding import PartitionSpec as P

LEVELS = 4
CSWEEPS = 6
absorption = 0.01
relaxation = 0.8
F32 = jnp.float32


def ring(n, b):
    return lambda at: jnp.where(at < (n + b) // 2, at, at - n)


def span(count, away=-1000, start=0):
    return lambda at: jnp.where((at >= start) & (at < start + count), at - start, away)


def matrix(shape, rows, columns, turned, values):
    a = rows(lax.broadcasted_iota(jnp.int32, shape, 0))
    b = columns(lax.broadcasted_iota(jnp.int32, shape, 1))
    return values(b, a) if turned else values(a, b)


def restriction(shape, rows, columns, turned=False):
    def values(coarse, fine):
        gap = fine - 2 * coarse
        outer, inner = (gap == -1) | (gap == 2), (gap == 0) | (gap == 1)
        return jnp.where(outer, 0.125, jnp.where(inner, 0.375, 0.0))

    return matrix(shape, rows, columns, turned, values)


def halving(shape, rows, columns, turned=False):
    def values(coarse, fine):
        return jnp.where((fine >> 1) == coarse, 0.5, 0.0)

    return matrix(shape, rows, columns, turned, values)


def prolongation(shape, rows, columns, turned=False):
    def values(fine, coarse):
        near = (fine >> 1) == coarse
        far = (fine >> 1) + 2 * (fine & 1) - 1 == coarse
        return jnp.where(near, 0.75, jnp.where(far, 0.25, 0.0))

    return matrix(shape, rows, columns, turned, values)


Y0, Z0, Y1, Z1, Y2, Z2 = ring(48, 32), ring(256, 128), ring(40, 16), ring(128, 64), ring(24, 8), ring(128, 32)


def dot(a, b):
    return lax.dot_general(
        a, b, (((1,), (0,)), ((), ())),
        precision=lax.Precision.HIGHEST, preferred_element_type=F32,
    )


def planes(lo, hi, step, carry=0, unroll=1):
    whole = (hi - lo) // unroll
    if whole > 1:
        carry = lax.fori_loop(0, whole, lambda t, c: step(lo + t * unroll, unroll, c), carry)
    elif whole == 1:
        carry = step(lo, unroll, carry)
    rest = (hi - lo) % unroll
    return step(hi - rest, rest, carry) if rest else carry


class Open:
    def above(self, v, dim):
        return pltpu.roll(v, v.shape[dim] - 1, dim)

    def below(self, v, dim):
        return pltpu.roll(v, 1, dim)

    def closed(self, k):
        return None


class Closed(Open):
    def __init__(self, shape, counts):
        self.last, self.first = [], []
        for dim in range(2):
            at = lax.broadcasted_iota(jnp.int32, shape, dim)
            self.last.append(jnp.where(at == counts[dim] - 1, 0.0, 1.0))
            self.first.append(jnp.where(at == 0, 0.0, 1.0))

    def above(self, v, dim):
        return super().above(v, dim) * self.last[dim]

    def below(self, v, dim):
        return super().below(v, dim) * self.first[dim]

    def closed(self, k):
        return k * ((1.0 - self.first[0]) + (1.0 - self.first[1]))


def weigh(k, wx, wy, wz, lo, hi, factor, shifts, d=None, mask=None, b=None, unroll=1):
    half = 0.5 * factor
    first = half * (k[lo - 1] + k[lo])
    wx[lo - 1] = first

    def step(i, n, below):
        here = [k[i + j] for j in range(n + 1)]
        outs = []
        for j in range(n):
            x = half * (here[j] + here[j + 1])
            y = half * (here[j] + shifts.above(here[j], 0))
            z = half * (here[j] + shifts.above(here[j], 1))
            ends, value = shifts.closed(half * here[j]), None
            if d is not None:
                value = (x + below) + (y + shifts.below(y, 0)) + (z + shifts.below(z, 1))
                if ends is not None:
                    value = value + ends
                value = relaxation / (value + absorption)
                if mask is not None:
                    value = mask(here[j], value)
            outs.append((x, y, z, ends, value))
            below = x
        for j, (x, y, z, ends, value) in enumerate(outs):
            wx[i + j], wy[i + j], wz[i + j] = x, y, z
            if ends is not None:
                b[i + j] = ends
            if value is not None:
                d[i + j] = value
        return below

    planes(lo, hi, step, first, unroll)


def image(v, wx, wy, wz, lo, hi, use, put, shifts, b=None, unroll=1):
    def step(i, n, below):
        here = [v[i + j] for j in range(n + 1)]
        outs = []
        for j in range(n):
            x = wx[i + j] * (here[j] - here[j + 1])
            y = wy[i + j] * (here[j] - shifts.above(here[j], 0))
            z = wz[i + j] * (here[j] - shifts.above(here[j], 1))
            total = (x - below) + (y - shifts.below(y, 0)) + (z - shifts.below(z, 1))
            if b is not None:
                total = total + b[i + j] * here[j]
            outs.append(use(i + j, here[j], total + absorption * here[j]))
            below = x
        for j, value in enumerate(outs):
            put(i + j, value)
        return below

    planes(lo, hi, step, wx[lo - 1] * (v[lo - 1] - v[lo]), unroll)


def into(ref, by=0):
    def put(i, value):
        ref[i + by] = value

    return put


def smooth(v, f, d, w, lo, hi, shifts, b=None, unroll=1, by=0):
    def use(i, here, im):
        return here + d[i] * (f[i + by] - im)

    image(v, *w, lo, hi, use, into(v), shifts, b, unroll)


def residual_of(v, f, r, w, lo, hi, shifts, mask=None, b=None, unroll=1):
    def use(i, here, im):
        value = f[i] - im
        return value if mask is None else jnp.where(mask[i] > 0.0, value, 0.0)

    image(v, *w, lo, hi, use, into(r), shifts, b, unroll)


def first_sweep(g, d, v, lo, hi, unroll, by=0):
    def step(i, n, carry):
        values = [g[i + j + by] * d[i + j] for j in range(n)]
        for j, value in enumerate(values):
            v[i + j] = value
        return carry

    planes(lo, hi, step, unroll=unroll)


def restrict(r, offset, lo, hi, ry, rz, held):
    size = ry.shape[0]
    for i in range(lo, hi):
        at = 2 * i + offset
        plane = 0.125 * (r[at - 1] + r[at + 2]) + 0.375 * (r[at] + r[at + 1])
        held[(i - lo) * size : (i - lo + 1) * size, :] = dot(ry, plane)
    return dot(held[: (hi - lo) * size, :], rz)


def halve(k, offset, lo, hi, cy, cz, held):
    size = cy.shape[0]
    for i in range(lo, hi):
        plane = 0.5 * (k[2 * i + offset] + k[2 * i + 1 + offset])
        held[(i - lo) * size : (i - lo + 1) * size, :] = dot(cy, plane)
    return dot(held[: (hi - lo) * size, :], cz)


def prolong(e, first, count, py, pz, finer, use):
    rows = e.shape[1]
    spread = dot(e[pl.ds(first, count)].reshape(count * rows, e.shape[2]), pz)
    for i in range(count):
        finer[i] = dot(py, spread[i * rows : (i + 1) * rows])

    def step(i, n, carry):
        below, here, above = finer[i - 1], finer[i], finer[i + 1]
        use(2 * (i - 1), 0.75 * here + 0.25 * below)
        use(2 * (i - 1) + 1, 0.75 * here + 0.25 * above)
        return carry

    planes(1, count - 1, step)


def three(w):
    return tuple(w.at[i] for i in range(3))


def inside(k, value):
    return jnp.where(k > 0.0, value, 0.0)


U0, U1, U2, U3 = 6, 12, 10, 16


def place(target, at, source, start, count, unroll=4):
    def step(i, n, carry):
        values = [source[start + i + j] for j in range(n)]
        for j, value in enumerate(values):
            target[at + i + j] = value
        return carry

    planes(0, count, step, unroll=unroll)


def down0(before, fo, ko, after, f, k, out, wx, wy, wz, d, v, r, held):
    shifts = Open()
    for ref, own, at in ((f, fo, 0), (k, ko, 5)):
        place(ref, 0, before, at, 5, 5)
        place(ref, 5, own, 0, 16)
        place(ref, 21, after, at, 5, 5)
    weigh(k, wx, wy, wz, 1, 25, 1.0, shifts, d, inside, unroll=U0)
    first_sweep(f, d, v, 1, 25, U0)
    residual_of(v, f, r, (wx, wy, wz), 2, 24, shifts, k, unroll=U0)
    ry, rz = restriction((16, 48), span(16), Y0), restriction((256, 128), Z0, Z1, True)
    out[:10] = restrict(r, 5, -1, 9, ry, rz, held).reshape(10, 16, 128)
    cy, cz = halving((16, 48), span(16), Y0), halving((256, 128), Z0, Z1, True)
    out[10:] = halve(k, 5, -1, 9, cy, cz, held).reshape(10, 16, 128)


def descend(first, *refs):
    shifts = Open()
    before, own, after = refs[:3]
    if first:
        out, g1, k1, g2, k2, below, above = refs[3:10]
        for ref, at in ((g1, 0), (k1, 1)):
            place(ref, 0, before, 9 * at, 9, 9)
            place(ref, 9, own, 10 * at + 1, 8, 8)
            place(ref, 17, after, 9 * at, 9, 9)
    else:
        k1, k2, out, g1, g2 = refs[3:8]
        zero = jnp.zeros(g1.shape[1:], F32)
        g1[0], g1[25] = zero, zero
        for ref, at in ((before, 1), (own, 9), (after, 17)):
            place(g1, at, ref, 0, 8, 8)
    v1, r1, held, w1, d1, v2, r2, w2, d2 = refs[-9:]
    w1, w2 = three(w1), three(w2)
    rows = g2.shape[1]
    weigh(k1, *w1, 1, 25, 0.25, shifts, d1, inside, unroll=U1)
    first_sweep(g1, d1, v1, 1, 25, U1)
    residual_of(v1, g1, r1, w1, 2, 24, shifts, d1, unroll=U1)
    zero = jnp.zeros(g2.shape[1:], F32)
    g2[0], g2[11] = zero, zero
    ry1, rz1 = restriction((24, 40), Y2, Y1), restriction((128, 128), Z1, Z2, True)
    g2[1:11] = restrict(r1, 9, -3, 7, ry1, rz1, held).reshape(10, rows, 128)
    if first:
        cy1, cz1 = halving((24, 40), Y2, Y1), halving((128, 128), Z1, Z2, True)
        k2[...] = halve(k1, 9, -4, 8, cy1, cz1, held).reshape(k2.shape)
    weigh(k2, *w2, 1, 11, 0.25**2, shifts, d2, inside, unroll=U2)
    if first:
        below[0], below[1], above[0], above[1] = g2[4], d2[4], g2[7], d2[7]
    first_sweep(g2, d2, v2, 1, 11, U2)
    residual_of(v2, g2, r2, w2, 3, 9, shifts, d2, unroll=U2)
    total = None
    for i in range(2):
        at = 2 * i + 4
        plane = 0.125 * (r2[at - 1] + r2[at + 2]) + 0.375 * (r2[at] + r2[at + 1])
        value = dot(restriction((8, 24), span(4, start=4 * i), Y2), plane)
        total = value if total is None else total + value
    tile = dot(total, restriction((128, 128), Z2, span(16), True))
    if first:
        part = [
            dot(halving((8, 24), span(4, start=4 * i), Y2), 0.5 * (k2[2 * i + 4] + k2[2 * i + 5]))
            for i in range(2)
        ]
        tile = tile + dot(part[0] + part[1], halving((128, 128), Z2, span(16, start=16), True))
    for i in range(out.shape[0]):
        out[i] = tile


def repack(s, out):
    tiles = 2 * s.shape[0] // 16
    lane = lax.broadcasted_iota(jnp.int32, (8, 128), 1) // 16
    row = lax.broadcasted_iota(jnp.int32, (8, 128), 0) // 4
    for field in range(out.shape[1] // tiles):
        for t in range(tiles):
            total = jnp.zeros((8, 128), F32)
            for half in range(2):
                for p in range(8):
                    plane = 16 * t + 8 * half + p
                    part = s[plane // 2]
                    if plane % 2 != half:
                        part = pltpu.roll(part, 4, 0)
                    if p != field:
                        part = pltpu.roll(part, (16 * (p - field)) % 128, 1)
                    total = jnp.where((lane == p) & (row == half), part, total)
            for i in range(out.shape[0]):
                out[i, field * tiles + t] = total


def unpack(s, first, tiles, nz, whole):
    lane = lax.broadcasted_iota(jnp.int32, (8, 128), 1) // 16
    for j in range(s.shape[0] // nz):
        for t in range(tiles):
            for p in range(8):
                total = jnp.zeros((8, 128), F32)
                for q in range(nz):
                    part = s[j * nz + q, first + t]
                    if p != q:
                        part = pltpu.roll(part, (16 * (q - p)) % 128, 1)
                    total = jnp.where(lane == q, part, total)
                whole[16 * t + p + 3, 4 * j : 4 * j + 4] = total[:4]
                whole[16 * t + p + 11, 4 * j : 4 * j + 4] = total[4:]


def bottom(nz, s, k3, scratch):
    g3, v3, r3, w3, d3, b3, k4, g4, v4, w4, d4, b4, held, fine4 = scratch
    n4 = g4.shape[0]
    lanes3, lanes4 = span(16 * nz, -3000), span(8 * nz, -9000)
    rows3, rows4 = span(g3.shape[1]), span(g4.shape[1])
    tall, wide = (g4.shape[1], g3.shape[1]), (128, 128)
    n3, two = 2 * n4, s.shape[1] == n4 // 4
    rows, lanes = g3.shape[1], g3.shape[2]
    zero = jnp.zeros((rows, lanes), F32)
    for i in (0, 1, 2, n3 + 3, n3 + 4, n3 + 5):
        v3[i], r3[i] = zero, zero
        if two:
            k3[i] = zero
    for ref in (k4, v4):
        for i in (0, n4 + 1):
            ref[i] = jnp.zeros(ref.shape[1:], F32)
    unpack(s, 0, n3 // 16, nz, g3)
    if two:
        unpack(s, n3 // 16, n3 // 16, nz, k3)
    cy3, cz3 = halving(tall, rows4, rows3), halving(wide, lanes3, lanes4, True)
    k4[1 : n4 + 1] = halve(k3, 3, 0, n4, cy3, cz3, held).reshape(g4.shape)
    shifts3 = Closed((rows, lanes), (rows, 16 * nz))
    shifts4 = Closed((k4.shape[1], lanes), (k4.shape[1], 8 * nz))
    w3, w4 = three(w3), three(w4)
    weigh(k3, *w3, 3, n3 + 3, 0.25**3, shifts3, d3, inside, b3, U3)
    weigh(k4, *w4, 1, n4 + 1, 0.25**4, shifts4, d4, inside, b4, U3)
    first_sweep(g3, d3, v3, 3, n3 + 3, U3)
    residual_of(v3, g3, r3, w3, 3, n3 + 3, shifts3, b=b3, unroll=U3)
    ry3, rz3 = restriction(tall, rows4, rows3), restriction(wide, lanes3, lanes4, True)
    g4[...] = restrict(r3, 3, 0, n4, ry3, rz3, held).reshape(g4.shape)
    first_sweep(g4, d4, v4, 1, n4 + 1, U3, by=-1)

    def turn(j, carry):
        smooth(v4, g4, d4, w4, 1, n4 + 1, shifts4, b4, n4, by=-1)
        return carry

    lax.fori_loop(0, CSWEEPS - 1, turn, 0)

    def use(i, value):
        v3[i + 3] = v3[i + 3] + value

    py3, pz3 = prolongation(tall[::-1], rows3, rows4), prolongation(wide, lanes4, lanes3, True)
    prolong(v4, 0, n4 + 2, py3, pz3, fine4, use)
    smooth(v3, g3, d3, w3, 3, n3 + 3, shifts3, b3, U3)
    return v3


def spread_matrix(shape, dim_fine, coarse_start, block_fine):
    fine = lax.broadcasted_iota(jnp.int32, shape, dim_fine)
    size = shape[dim_fine]
    fine = jnp.where(fine < (size + block_fine) // 2, fine, fine - size)
    whole = lax.broadcasted_iota(jnp.int32, shape, 1 - dim_fine)
    near = (fine >> 1) + coarse_start
    far = near + 2 * (fine & 1) - 1
    return jnp.where(whole == near, 0.75, jnp.where(whole == far, 0.25, 0.0))


def upward(index, e3, g2, k2, g1, k1, ends, scratch):
    v2, w2, d2, v1, w1, d1, fine2, fine1 = scratch
    shifts, w2, w1 = Open(), three(w2), three(w1)
    weigh(k2, *w2, 1, 11, 0.25**2, shifts, d2, inside, unroll=U2)
    weigh(k1, *w1, 5, 21, 0.25, shifts, d1, inside, unroll=U1)
    first_sweep(g2, d2, v2, 1, 11, U2)
    first_sweep(g1, d1, v1, 5, 21, U1)
    zero = jnp.zeros(d2.shape[1:], F32)
    for i, n in ((0, 0), (11, 1)):
        v2[i] = zero if ends is None else ends[n][0] * ends[n][1]
        d2[i] = zero if ends is None else ends[n][1]

    def use2(i, value):
        v2[i] = jnp.where(d2[i] > 0.0, v2[i] + value, 0.0)

    py2 = spread_matrix((g2.shape[1], e3.shape[1]), 0, index[1] * 4, 8)
    pz2 = spread_matrix((e3.shape[2], g2.shape[2]), 1, index[2] * 16, 32)
    prolong(e3, index[0] * 2, 8, py2, pz2, fine2, use2)
    smooth(v2, g2, d2, w2, 1, 11, shifts, unroll=U2)

    def use1(i, value):
        v1[i + 5] = jnp.where(d1[i + 5] > 0.0, v1[i + 5] + value, 0.0)

    py1, pz1 = prolongation((40, 24), Y1, Y2), prolongation((128, 128), Z2, Z1, True)
    prolong(v2, 1, 10, py1, pz1, fine1, use1)
    smooth(v1, g1, d1, w1, 6, 20, shifts, unroll=U1)
    return v1


BOTTOM = 14
UP = 8


def middle(nz, index, f, k, s, g2, k2, g1, k1, *refs):
    ends, (v, gn, turned, k3) = refs[:2], refs[2:6]
    low, mid, (fine0, r, held0, wx, wy, wz, d) = refs[6:20], refs[20:28], refs[28:]
    weigh(k, wx, wy, wz, 1, 25, 1.0, Open(), d, inside, unroll=U0)
    e3 = bottom(nz, s, k3, low)
    e1 = upward(index, e3, g2, k2, g1, k1, ends, mid)
    w, shifts = (wx, wy, wz), Open()

    def use(i, value):
        v[i + 1] = inside(k[i + 1], f[i + 1] * d[i + 1] + value)

    py0, pz0 = prolongation((48, 40), Y0, Y1), prolongation((128, 256), Z1, Z0, True)
    prolong(e1, 6, 14, py0, pz0, fine0, use)
    smooth(v, f, d, w, 2, 24, shifts, unroll=U0)
    smooth(v, f, d, w, 3, 23, shifts, unroll=U0)
    residual_of(v, f, r, w, 4, 22, shifts, k, unroll=U0)
    ry, rz = restriction((16, 48), span(16), Y0), restriction((256, 128), Z0, Z1, True)
    value = restrict(r, 5, 0, 8, ry, rz, held0)
    gn[...] = value.reshape(gn.shape)
    turned[...] = pltpu.roll(value, 64, 1).reshape(gn.shape)


def final(nz, index, f, k, v0, s, g2, k2, g1, k1, *refs):
    k3, (solution_, residual_) = refs[0], refs[1:3]
    low, mid, (fine0, wx, wy, wz, d, v) = refs[3:17], refs[17:25], refs[25:]
    weigh(k, wx, wy, wz, 3, 22, 1.0, Open(), d, inside, unroll=U0)
    e3 = bottom(nz, s, k3, low)
    e1 = upward(index, e3, g2, k2, g1, k1, None, mid)
    w, shifts = (wx, wy, wz), Open()

    def use(i, value):
        v[i + 3] = inside(k[i + 3], v0[i + 3] + value)

    py0, pz0 = prolongation((48, 40), Y0, Y1), prolongation((128, 256), Z1, Z0, True)
    prolong(e1, 7, 12, py0, pz0, fine0, use)
    smooth(v, f, d, w, 4, 22, shifts, unroll=U0)

    def last(i, here, im):
        return here[:32, :128], (f[i] - im)[:32, :128]

    def out(i, values):
        solution_[i - 5], residual_[i - 5] = values

    image(v, *w, 5, 21, last, out, shifts, unroll=U0)


def call(kernel, outs, scratch, *args, name, scalars=0, room=4):
    vmem = pl.BlockSpec(memory_space=pltpu.VMEM)
    smem = pl.BlockSpec(memory_space=pltpu.SMEM)
    return pl.pallas_call(
        kernel,
        out_shape=[jax.ShapeDtypeStruct(o, F32) for o in outs],
        in_specs=[smem] * scalars + [vmem] * (len(args) - scalars),
        out_specs=[vmem] * len(outs),
        scratch_shapes=[pltpu.VMEM(s, F32) for s in scratch],
        compiler_params=pltpu.CompilerParams(vmem_limit_bytes=room << 20),
        name=name,
    )(*args)


def neighbours(last, initial, axis):
    count = lax.axis_size(axis)
    if axis == "gz":
        up = [(i, (i + 1) % count) for i in range(count)]
    else:
        up = [(i, i + 1) for i in range(count - 1)]
    down = [(j, i) for i, j in up]
    before = lax.ppermute(last, axis, up)
    after = lax.ppermute(initial, axis, down)
    if axis == "gz":
        at = lax.axis_index(axis)
        before = jnp.where(at == 0, 0.0, before)
        after = jnp.where(at == count - 1, 0.0, after)
    return before, after


def finest(fields):
    for axis, dim, size, count, width in (("gz", 2, 128, 256, 25), ("gy", 1, 32, 48, 5)):
        along = 2 if dim == 2 else 0
        last = [lax.slice_in_dim(v, size - width, size, axis=dim) for v in fields]
        initial = [lax.slice_in_dim(v, 0, width, axis=dim) for v in fields]
        before, after = neighbours(
            jnp.concatenate(last, along), jnp.concatenate(initial, along), axis
        )
        before, after = jnp.split(before, 2, along), jnp.split(after, 2, along)
        gap = list(fields[0].shape)
        gap[dim] = count - size - 2 * width
        gap = jnp.zeros(gap, F32)
        fields = [
            jnp.concatenate([v, a, gap, b], dim) for b, v, a in zip(before, fields, after)
        ]
    last = jnp.concatenate([v[11:] for v in fields])
    initial = jnp.concatenate([v[:5] for v in fields])
    before, after = neighbours(last, initial, "gx")
    return before, *fields, after


def rows1(values):
    before, after = neighbours(values, values, "gy")
    gap = jnp.zeros((values.shape[0], 2, 128), F32)
    return jnp.concatenate([values, after[:, :11], gap, before[:, 5:]], 1)


def lanes1(values, turned):
    before, after = neighbours(turned, turned, "gz")
    lane = jnp.arange(128)
    zero = jnp.where(lane >= 117, before, 0.0)
    return jnp.where(lane < 64, values, jnp.where(lane < 75, after, zero))


def everyone(pieces, axes):
    return lax.all_to_all(pieces, axes, 0, 0)


def body(right_side, conductivity):
    nx, ny, nz = (lax.axis_size(axis) for axis in ("gx", "gy", "gz"))
    index = jnp.stack([lax.axis_index(axis) for axis in ("gx", "gy", "gz")]).astype(jnp.int32)

    wide, l1, l2 = (26, 48, 256), (26, 40, 128), (12, 24, 128)
    n3, n4 = (2 * nx + 6, 4 * ny, 128), (nx + 2, 2 * ny, 128)
    low = [
        n3, n3, n3, (3,) + n3, n3, n3,
        n4, (nx, 2 * ny, 128), n4, (3,) + n4, n4, n4,
        (nx * 2 * ny, 128), (nx + 2, 4 * ny, 128),
    ]
    mid = [l2, (3,) + l2, l2, l1, (3,) + l1, l1, (8, 24, 128), (10, 40, 128)]
    tiles = nx // 8

    right_side, conductivity, index = lax.optimization_barrier((right_side, conductivity, index))
    f, k, both1 = call(
        down0, [wide] * 2 + [(20, 16, 128)], [wide] * 6 + [(160, 256)],
        *finest([right_side, conductivity]), name="down0", room=14,
    )
    own = rows1(both1)
    last = jnp.concatenate([own[0:9], own[10:19]])
    initial = jnp.concatenate([own[1:10], own[11:20]])
    before, after = neighbours(last, initial, "gx")
    inner = [l1, l1, (288, 128), (3,) + l1, l1, l2, l2, (3,) + l2, l2]
    pair = (2, 24, 128)
    pieces, g1, k1, g2, k2, below, above = call(
        functools.partial(descend, True), [(nx, 8, 128), l1, l1, l2, l2, pair, pair], inner,
        before, own, after, name="descend", room=10,
    )
    pieces = everyone(pieces, "gx")
    (pieces,) = call(repack, [(ny * nz, 2 * tiles, 8, 128)], [], pieces, name="repack")
    outer = neighbours(below, above, "gx")
    s = everyone(pieces, ("gy", "gz"))
    v, value, turned, k3 = call(
        functools.partial(middle, nz), [wide, (8, 16, 128), (8, 16, 128), n3],
        low + mid + [(14, 48, 256), wide, (128, 256)] + [wide] * 4,
        index, f, k, s, g2, k2, g1, k1, *outer, name="middle", room=20, scalars=1,
    )
    own = rows1(lanes1(value, turned))
    before, after = neighbours(own, own, "gx")
    pieces, g1, g2 = call(
        functools.partial(descend, False), [(nx, 8, 128), l1, l2], inner,
        before, own, after, k1, k2, name="again", room=10,
    )
    pieces = everyone(pieces, "gx")
    (pieces,) = call(repack, [(ny * nz, tiles, 8, 128)], [], pieces, name="repack2")
    s = everyone(pieces, ("gy", "gz"))
    return tuple(call(
        functools.partial(final, nz), [(16, 32, 128)] * 2,
        low + mid + [(12, 48, 256)] + [wide] * 5,
        index, f, k, v, s, g2, k2, g1, k1, k3, name="final", room=20, scalars=1,
    ))


def solution(mesh):
    placed = P("gx", "gy", "gz")
    return jax.shard_map(
        body, mesh=mesh, in_specs=(placed, placed), out_specs=(placed, placed), check_vma=False
    )
```

```python
import functools

import jax
import jax.numpy as jnp
from jax import lax
from jax.experimental import pallas as pl
from jax.experimental.pallas import tpu as pltpu
from jax.sharding import PartitionSpec as P

LEVELS = 4
CSWEEPS = 6
absorption = 0.01
relaxation = 0.8
F32 = jnp.float32


def ring(n, b):
    return lambda at: jnp.where(at < (n + b) // 2, at, at - n)


def span(count, away=-1000, start=0):
    return lambda at: jnp.where((at >= start) & (at < start + count), at - start, away)


def matrix(shape, rows, columns, turned, values):
    a = rows(lax.broadcasted_iota(jnp.int32, shape, 0))
    b = columns(lax.broadcasted_iota(jnp.int32, shape, 1))
    return values(b, a) if turned else values(a, b)


def restriction(shape, rows, columns, turned=False):
    def values(coarse, fine):
        gap = fine - 2 * coarse
        outer, inner = (gap == -1) | (gap == 2), (gap == 0) | (gap == 1)
        return jnp.where(outer, 0.125, jnp.where(inner, 0.375, 0.0))

    return matrix(shape, rows, columns, turned, values)


def halving(shape, rows, columns, turned=False):
    def values(coarse, fine):
        return jnp.where((fine >> 1) == coarse, 0.5, 0.0)

    return matrix(shape, rows, columns, turned, values)


def prolongation(shape, rows, columns, turned=False):
    def values(fine, coarse):
        near = (fine >> 1) == coarse
        far = (fine >> 1) + 2 * (fine & 1) - 1 == coarse
        return jnp.where(near, 0.75, jnp.where(far, 0.25, 0.0))

    return matrix(shape, rows, columns, turned, values)


Y0, Z0, Y1, Z1, Y2, Z2 = ring(48, 32), ring(256, 128), ring(40, 16), ring(128, 64), ring(24, 8), ring(128, 32)


def parts(v):
    high = v.astype(jnp.bfloat16)
    rest = v - high.astype(F32)
    middle = rest.astype(jnp.bfloat16)
    return high, middle, (rest - middle.astype(F32)).astype(jnp.bfloat16)


def product(a, b):
    return lax.dot_general(a, b, (((1,), (0,)), ((), ())), preferred_element_type=F32)


def dot_left(m, v):
    m = m.astype(jnp.bfloat16)
    high, middle, low = (product(m, part) for part in parts(v))
    return high + (middle + low)


def dot_right(v, m):
    m = m.astype(jnp.bfloat16)
    high, middle, low = (product(part, m) for part in parts(v))
    return high + (middle + low)


def planes(lo, hi, step, carry=0, unroll=1):
    whole = (hi - lo) // unroll
    if whole > 1:
        carry = lax.fori_loop(0, whole, lambda t, c: step(lo + t * unroll, unroll, c), carry)
    elif whole == 1:
        carry = step(lo, unroll, carry)
    rest = (hi - lo) % unroll
    return step(hi - rest, rest, carry) if rest else carry


class Open:
    def above(self, v, dim):
        return pltpu.roll(v, v.shape[dim] - 1, dim)

    def below(self, v, dim):
        return pltpu.roll(v, 1, dim)

    def closed(self, k):
        return None


class Closed(Open):
    def __init__(self, shape, counts):
        self.last, self.first = [], []
        for dim in range(2):
            at = lax.broadcasted_iota(jnp.int32, shape, dim)
            self.last.append(jnp.where(at == counts[dim] - 1, 0.0, 1.0))
            self.first.append(jnp.where(at == 0, 0.0, 1.0))

    def above(self, v, dim):
        return super().above(v, dim) * self.last[dim]

    def below(self, v, dim):
        return super().below(v, dim) * self.first[dim]

    def closed(self, k):
        return k * ((1.0 - self.first[0]) + (1.0 - self.first[1]))


def weigh(k, wx, wy, wz, lo, hi, factor, shifts, d=None, mask=None, b=None, unroll=1):
    half = 0.5 * factor
    first = half * (k[lo - 1] + k[lo])
    wx[lo - 1] = first

    def step(i, n, below):
        here = [k[i + j] for j in range(n + 1)]
        outs = []
        for j in range(n):
            x = half * (here[j] + here[j + 1])
            y = half * (here[j] + shifts.above(here[j], 0))
            z = half * (here[j] + shifts.above(here[j], 1))
            ends, value = shifts.closed(half * here[j]), None
            if d is not None:
                value = (x + below) + (y + shifts.below(y, 0)) + (z + shifts.below(z, 1))
                if ends is not None:
                    value = value + ends
                value = relaxation / (value + absorption)
                if mask is not None:
                    value = mask(here[j], value)
            outs.append((x, y, z, ends, value))
            below = x
        for j, (x, y, z, ends, value) in enumerate(outs):
            wx[i + j], wy[i + j], wz[i + j] = x, y, z
            if ends is not None:
                b[i + j] = ends
            if value is not None:
                d[i + j] = value
        return below

    planes(lo, hi, step, first, unroll)


def image(v, wx, wy, wz, lo, hi, use, put, shifts, b=None, unroll=1):
    def step(i, n, below):
        here = [v[i + j] for j in range(n + 1)]
        outs = []
        for j in range(n):
            x = wx[i + j] * (here[j] - here[j + 1])
            y = wy[i + j] * (here[j] - shifts.above(here[j], 0))
            z = wz[i + j] * (here[j] - shifts.above(here[j], 1))
            total = (x - below) + (y - shifts.below(y, 0)) + (z - shifts.below(z, 1))
            if b is not None:
                total = total + b[i + j] * here[j]
            outs.append(use(i + j, here[j], total + absorption * here[j]))
            below = x
        for j, value in enumerate(outs):
            put(i + j, value)
        return below

    planes(lo, hi, step, wx[lo - 1] * (v[lo - 1] - v[lo]), unroll)


def into(ref, by=0):
    def put(i, value):
        ref[i + by] = value

    return put


def smooth(v, f, d, w, lo, hi, shifts, b=None, unroll=1, by=0):
    def use(i, here, im):
        return here + d[i] * (f[i + by] - im)

    image(v, *w, lo, hi, use, into(v), shifts, b, unroll)


def residual_of(v, f, r, w, lo, hi, shifts, mask=None, b=None, unroll=1):
    def use(i, here, im):
        value = f[i] - im
        return value if mask is None else jnp.where(mask[i] > 0.0, value, 0.0)

    image(v, *w, lo, hi, use, into(r), shifts, b, unroll)


def first_sweep(g, d, v, lo, hi, unroll, by=0):
    def step(i, n, carry):
        values = [g[i + j + by] * d[i + j] for j in range(n)]
        for j, value in enumerate(values):
            v[i + j] = value
        return carry

    planes(lo, hi, step, unroll=unroll)


def restrict(r, offset, lo, hi, ry, rz, held):
    size = ry.shape[0]
    for i in range(lo, hi):
        at = 2 * i + offset
        plane = 0.125 * (r[at - 1] + r[at + 2]) + 0.375 * (r[at] + r[at + 1])
        held[(i - lo) * size : (i - lo + 1) * size, :] = dot_left(ry, plane)
    return dot_right(held[: (hi - lo) * size, :], rz)


def halve(k, offset, lo, hi, cy, cz, held):
    size = cy.shape[0]
    for i in range(lo, hi):
        plane = 0.5 * (k[2 * i + offset] + k[2 * i + 1 + offset])
        held[(i - lo) * size : (i - lo + 1) * size, :] = dot_left(cy, plane)
    return dot_right(held[: (hi - lo) * size, :], cz)


def prolong(e, first, count, py, pz, finer, use, put):
    rows = e.shape[1]
    spread = dot_right(e[pl.ds(first, count)].reshape(count * rows, e.shape[2]), pz)
    for i in range(count):
        finer[i] = dot_left(py, spread[i * rows : (i + 1) * rows])

    def step(i, n, carry):
        held = [finer[i - 1 + j] for j in range(n + 2)]
        outs = []
        for j in range(n):
            here = 0.75 * held[j + 1]
            outs.append(use(2 * (i + j - 1), here + 0.25 * held[j]))
            outs.append(use(2 * (i + j - 1) + 1, here + 0.25 * held[j + 2]))
        for j, value in enumerate(outs):
            put(2 * (i - 1) + j, value)
        return carry

    planes(1, count - 1, step, unroll=max(1, 36 // (finer.shape[1] * finer.shape[2] // 1024)))


def three(w):
    return tuple(w.at[i] for i in range(3))


def inside(k, value):
    return jnp.where(k > 0.0, value, 0.0)


U0, U1, U2, U3 = 6, 12, 10, 16


def place(target, at, source, start, count, unroll=4):
    def step(i, n, carry):
        values = [source[start + i + j] for j in range(n)]
        for j, value in enumerate(values):
            target[at + i + j] = value
        return carry

    planes(0, count, step, unroll=unroll)


def down0(before, fo, ko, after, f, k, out, wx, wy, wz, d, v, r, held):
    shifts = Open()
    for ref, own, at in ((f, fo, 0), (k, ko, 5)):
        place(ref, 0, before, at, 5, 5)
        place(ref, 5, own, 0, 16)
        place(ref, 21, after, at, 5, 5)
    weigh(k, wx, wy, wz, 1, 25, 1.0, shifts, d, inside, unroll=U0)
    first_sweep(f, d, v, 1, 25, U0)
    residual_of(v, f, r, (wx, wy, wz), 2, 24, shifts, k, unroll=U0)
    ry, rz = restriction((16, 48), span(16), Y0), restriction((256, 128), Z0, Z1, True)
    out[:10] = restrict(r, 5, -1, 9, ry, rz, held).reshape(10, 16, 128)
    cy, cz = halving((16, 48), span(16), Y0), halving((256, 128), Z0, Z1, True)
    out[10:] = halve(k, 5, -1, 9, cy, cz, held).reshape(10, 16, 128)


def descend(first, *refs):
    shifts = Open()
    before, own, after = refs[:3]
    if first:
        out, g1, k1, g2, k2, below, above = refs[3:10]
        for ref, at in ((g1, 0), (k1, 1)):
            place(ref, 0, before, 9 * at, 9, 9)
            place(ref, 9, own, 10 * at + 1, 8, 8)
            place(ref, 17, after, 9 * at, 9, 9)
    else:
        k1, k2, out, g1, g2 = refs[3:8]
        zero = jnp.zeros(g1.shape[1:], F32)
        g1[0], g1[25] = zero, zero
        for ref, at in ((before, 1), (own, 9), (after, 17)):
            place(g1, at, ref, 0, 8, 8)
    v1, r1, held, w1, d1, v2, r2, w2, d2 = refs[-9:]
    w1, w2 = three(w1), three(w2)
    rows = g2.shape[1]
    weigh(k1, *w1, 1, 25, 0.25, shifts, d1, inside, unroll=U1)
    first_sweep(g1, d1, v1, 1, 25, U1)
    residual_of(v1, g1, r1, w1, 2, 24, shifts, d1, unroll=U1)
    zero = jnp.zeros(g2.shape[1:], F32)
    g2[0], g2[11] = zero, zero
    ry1, rz1 = restriction((24, 40), Y2, Y1), restriction((128, 128), Z1, Z2, True)
    g2[1:11] = restrict(r1, 9, -3, 7, ry1, rz1, held).reshape(10, rows, 128)
    if first:
        cy1, cz1 = halving((24, 40), Y2, Y1), halving((128, 128), Z1, Z2, True)
        k2[...] = halve(k1, 9, -4, 8, cy1, cz1, held).reshape(k2.shape)
    weigh(k2, *w2, 1, 11, 0.25**2, shifts, d2, inside, unroll=U2)
    if first:
        below[0], below[1], above[0], above[1] = g2[4], d2[4], g2[7], d2[7]
    first_sweep(g2, d2, v2, 1, 11, U2)
    residual_of(v2, g2, r2, w2, 3, 9, shifts, d2, unroll=U2)
    total = None
    for i in range(2):
        at = 2 * i + 4
        plane = 0.125 * (r2[at - 1] + r2[at + 2]) + 0.375 * (r2[at] + r2[at + 1])
        value = dot_left(restriction((8, 24), span(4, start=4 * i), Y2), plane)
        total = value if total is None else total + value
    tile = dot_right(total, restriction((128, 128), Z2, span(16), True))
    if first:
        part = [
            dot_left(halving((8, 24), span(4, start=4 * i), Y2), 0.5 * (k2[2 * i + 4] + k2[2 * i + 5]))
            for i in range(2)
        ]
        tile = tile + dot_right(part[0] + part[1], halving((128, 128), Z2, span(16, start=16), True))
    for i in range(out.shape[0]):
        out[i] = tile


def repack(s, out):
    tiles = 2 * s.shape[0] // 16
    lane = lax.broadcasted_iota(jnp.int32, (8, 128), 1) // 16
    row = lax.broadcasted_iota(jnp.int32, (8, 128), 0) // 4
    for field in range(out.shape[1] // tiles):
        for t in range(tiles):
            total = jnp.zeros((8, 128), F32)
            for half in range(2):
                for p in range(8):
                    plane = 16 * t + 8 * half + p
                    part = s[plane // 2]
                    if plane % 2 != half:
                        part = pltpu.roll(part, 4, 0)
                    if p != field:
                        part = pltpu.roll(part, (16 * (p - field)) % 128, 1)
                    total = jnp.where((lane == p) & (row == half), part, total)
            for i in range(out.shape[0]):
                out[i, field * tiles + t] = total


def unpack(s, first, tiles, nz, whole):
    lane = lax.broadcasted_iota(jnp.int32, (8, 128), 1) // 16
    for j in range(s.shape[0] // nz):
        for t in range(tiles):
            for p in range(8):
                total = jnp.zeros((8, 128), F32)
                for q in range(nz):
                    part = s[j * nz + q, first + t]
                    if p != q:
                        part = pltpu.roll(part, (16 * (q - p)) % 128, 1)
                    total = jnp.where(lane == q, part, total)
                whole[16 * t + p + 3, 4 * j : 4 * j + 4] = total[:4]
                whole[16 * t + p + 11, 4 * j : 4 * j + 4] = total[4:]


def bottom(nz, s, k3, scratch):
    g3, v3, r3, w3, d3, b3, k4, g4, v4, w4, d4, b4, held, fine4 = scratch
    n4 = g4.shape[0]
    lanes3, lanes4 = span(16 * nz, -3000), span(8 * nz, -9000)
    rows3, rows4 = span(g3.shape[1]), span(g4.shape[1])
    tall, wide = (g4.shape[1], g3.shape[1]), (128, 128)
    n3, two = 2 * n4, s.shape[1] == n4 // 4
    rows, lanes = g3.shape[1], g3.shape[2]
    zero = jnp.zeros((rows, lanes), F32)
    for i in (0, 1, 2, n3 + 3, n3 + 4, n3 + 5):
        v3[i], r3[i] = zero, zero
        if two:
            k3[i] = zero
    for ref in (k4, v4):
        for i in (0, n4 + 1):
            ref[i] = jnp.zeros(ref.shape[1:], F32)
    unpack(s, 0, n3 // 16, nz, g3)
    if two:
        unpack(s, n3 // 16, n3 // 16, nz, k3)
    cy3, cz3 = halving(tall, rows4, rows3), halving(wide, lanes3, lanes4, True)
    k4[1 : n4 + 1] = halve(k3, 3, 0, n4, cy3, cz3, held).reshape(g4.shape)
    shifts3 = Closed((rows, lanes), (rows, 16 * nz))
    shifts4 = Closed((k4.shape[1], lanes), (k4.shape[1], 8 * nz))
    w3, w4 = three(w3), three(w4)
    weigh(k3, *w3, 3, n3 + 3, 0.25**3, shifts3, d3, inside, b3, U3)
    weigh(k4, *w4, 1, n4 + 1, 0.25**4, shifts4, d4, inside, b4, U3)
    first_sweep(g3, d3, v3, 3, n3 + 3, U3)
    residual_of(v3, g3, r3, w3, 3, n3 + 3, shifts3, b=b3, unroll=U3)
    ry3, rz3 = restriction(tall, rows4, rows3), restriction(wide, lanes3, lanes4, True)
    g4[...] = restrict(r3, 3, 0, n4, ry3, rz3, held).reshape(g4.shape)
    first_sweep(g4, d4, v4, 1, n4 + 1, U3, by=-1)

    def turn(j, carry):
        smooth(v4, g4, d4, w4, 1, n4 + 1, shifts4, b4, n4, by=-1)
        return carry

    lax.fori_loop(0, CSWEEPS - 1, turn, 0)

    def use(i, value):
        return v3[i + 3] + value

    py3, pz3 = prolongation(tall[::-1], rows3, rows4), prolongation(wide, lanes4, lanes3, True)
    prolong(v4, 0, n4 + 2, py3, pz3, fine4, use, into(v3, 3))
    smooth(v3, g3, d3, w3, 3, n3 + 3, shifts3, b3, U3)
    return v3


def spread_matrix(shape, dim_fine, coarse_start, block_fine):
    fine = lax.broadcasted_iota(jnp.int32, shape, dim_fine)
    size = shape[dim_fine]
    fine = jnp.where(fine < (size + block_fine) // 2, fine, fine - size)
    whole = lax.broadcasted_iota(jnp.int32, shape, 1 - dim_fine)
    near = (fine >> 1) + coarse_start
    far = near + 2 * (fine & 1) - 1
    return jnp.where(whole == near, 0.75, jnp.where(whole == far, 0.25, 0.0))


def upward(index, e3, g2, k2, g1, k1, ends, scratch):
    v2, w2, d2, v1, w1, d1, fine2, fine1 = scratch
    shifts, w2, w1 = Open(), three(w2), three(w1)
    weigh(k2, *w2, 1, 11, 0.25**2, shifts, d2, inside, unroll=U2)
    weigh(k1, *w1, 5, 21, 0.25, shifts, d1, inside, unroll=U1)
    first_sweep(g2, d2, v2, 1, 11, U2)
    first_sweep(g1, d1, v1, 5, 21, U1)
    zero = jnp.zeros(d2.shape[1:], F32)
    for i, n in ((0, 0), (11, 1)):
        v2[i] = zero if ends is None else ends[n][0] * ends[n][1]
        d2[i] = zero if ends is None else ends[n][1]

    def use2(i, value):
        return jnp.where(d2[i] > 0.0, v2[i] + value, 0.0)

    py2 = spread_matrix((g2.shape[1], e3.shape[1]), 0, index[1] * 4, 8)
    pz2 = spread_matrix((e3.shape[2], g2.shape[2]), 1, index[2] * 16, 32)
    prolong(e3, index[0] * 2, 8, py2, pz2, fine2, use2, into(v2))
    smooth(v2, g2, d2, w2, 1, 11, shifts, unroll=U2)

    def use1(i, value):
        return jnp.where(d1[i + 5] > 0.0, v1[i + 5] + value, 0.0)

    py1, pz1 = prolongation((40, 24), Y1, Y2), prolongation((128, 128), Z2, Z1, True)
    prolong(v2, 1, 10, py1, pz1, fine1, use1, into(v1, 5))
    smooth(v1, g1, d1, w1, 6, 20, shifts, unroll=U1)
    return v1


BOTTOM = 14
UP = 8


def middle(nz, index, f, k, s, g2, k2, g1, k1, *refs):
    ends, (v, gn, turned, k3) = refs[:2], refs[2:6]
    low, mid, (fine0, r, held0, wx, wy, wz, d) = refs[6:20], refs[20:28], refs[28:]
    weigh(k, wx, wy, wz, 1, 25, 1.0, Open(), d, inside, unroll=U0)
    e3 = bottom(nz, s, k3, low)
    e1 = upward(index, e3, g2, k2, g1, k1, ends, mid)
    w, shifts = (wx, wy, wz), Open()

    def use(i, value):
        return inside(k[i + 1], f[i + 1] * d[i + 1] + value)

    py0, pz0 = prolongation((48, 40), Y0, Y1), prolongation((128, 256), Z1, Z0, True)
    prolong(e1, 6, 14, py0, pz0, fine0, use, into(v, 1))
    smooth(v, f, d, w, 2, 24, shifts, unroll=U0)
    smooth(v, f, d, w, 3, 23, shifts, unroll=U0)
    residual_of(v, f, r, w, 4, 22, shifts, k, unroll=U0)
    ry, rz = restriction((16, 48), span(16), Y0), restriction((256, 128), Z0, Z1, True)
    value = restrict(r, 5, 0, 8, ry, rz, held0)
    gn[...] = value.reshape(gn.shape)
    turned[...] = pltpu.roll(value, 64, 1).reshape(gn.shape)


def final(nz, index, f, k, v0, s, g2, k2, g1, k1, *refs):
    k3, (solution_, residual_) = refs[0], refs[1:3]
    low, mid, (fine0, wx, wy, wz, d, v) = refs[3:17], refs[17:25], refs[25:]
    weigh(k, wx, wy, wz, 3, 22, 1.0, Open(), d, inside, unroll=U0)
    e3 = bottom(nz, s, k3, low)
    e1 = upward(index, e3, g2, k2, g1, k1, None, mid)
    w, shifts = (wx, wy, wz), Open()

    def use(i, value):
        return inside(k[i + 3], v0[i + 3] + value)

    py0, pz0 = prolongation((48, 40), Y0, Y1), prolongation((128, 256), Z1, Z0, True)
    prolong(e1, 7, 12, py0, pz0, fine0, use, into(v, 3))
    smooth(v, f, d, w, 4, 22, shifts, unroll=U0)

    def last(i, here, im):
        return here[:32, :128], (f[i] - im)[:32, :128]

    def out(i, values):
        solution_[i - 5], residual_[i - 5] = values

    image(v, *w, 5, 21, last, out, shifts, unroll=U0)


def call(kernel, outs, scratch, *args, name, scalars=0, room=4):
    vmem = pl.BlockSpec(memory_space=pltpu.VMEM)
    smem = pl.BlockSpec(memory_space=pltpu.SMEM)
    return pl.pallas_call(
        kernel,
        out_shape=[jax.ShapeDtypeStruct(o, F32) for o in outs],
        in_specs=[smem] * scalars + [vmem] * (len(args) - scalars),
        out_specs=[vmem] * len(outs),
        scratch_shapes=[pltpu.VMEM(s, F32) for s in scratch],
        compiler_params=pltpu.CompilerParams(vmem_limit_bytes=room << 20),
        name=name,
    )(*args)


def neighbours(last, initial, axis):
    count = lax.axis_size(axis)
    if axis == "gz":
        up = [(i, (i + 1) % count) for i in range(count)]
    else:
        up = [(i, i + 1) for i in range(count - 1)]
    down = [(j, i) for i, j in up]
    before = lax.ppermute(last, axis, up)
    after = lax.ppermute(initial, axis, down)
    if axis == "gz":
        at = lax.axis_index(axis)
        before = jnp.where(at == 0, 0.0, before)
        after = jnp.where(at == count - 1, 0.0, after)
    return before, after


def finest(fields):
    for axis, dim, size, count, width in (("gz", 2, 128, 256, 25), ("gy", 1, 32, 48, 5)):
        along = 2 if dim == 2 else 0
        last = [lax.slice_in_dim(v, size - width, size, axis=dim) for v in fields]
        initial = [lax.slice_in_dim(v, 0, width, axis=dim) for v in fields]
        before, after = neighbours(
            jnp.concatenate(last, along), jnp.concatenate(initial, along), axis
        )
        before, after = jnp.split(before, 2, along), jnp.split(after, 2, along)
        gap = list(fields[0].shape)
        gap[dim] = count - size - 2 * width
        gap = jnp.zeros(gap, F32)
        fields = [
            jnp.concatenate([v, a, gap, b], dim) for b, v, a in zip(before, fields, after)
        ]
    last = jnp.concatenate([v[11:] for v in fields])
    initial = jnp.concatenate([v[:5] for v in fields])
    before, after = neighbours(last, initial, "gx")
    return before, *fields, after


def rows1(values):
    before, after = neighbours(values, values, "gy")
    gap = jnp.zeros((values.shape[0], 2, 128), F32)
    return jnp.concatenate([values, after[:, :11], gap, before[:, 5:]], 1)


def lanes1(values, turned):
    before, after = neighbours(turned, turned, "gz")
    lane = jnp.arange(128)
    zero = jnp.where(lane >= 117, before, 0.0)
    return jnp.where(lane < 64, values, jnp.where(lane < 75, after, zero))


def everyone(pieces, axes):
    return lax.all_to_all(pieces, axes, 0, 0)


def body(right_side, conductivity):
    nx, ny, nz = (lax.axis_size(axis) for axis in ("gx", "gy", "gz"))
    index = jnp.stack([lax.axis_index(axis) for axis in ("gx", "gy", "gz")]).astype(jnp.int32)

    wide, l1, l2 = (26, 48, 256), (26, 40, 128), (12, 24, 128)
    n3, n4 = (2 * nx + 6, 4 * ny, 128), (nx + 2, 2 * ny, 128)
    low = [
        n3, n3, n3, (3,) + n3, n3, n3,
        n4, (nx, 2 * ny, 128), n4, (3,) + n4, n4, n4,
        (nx * 2 * ny, 128), (nx + 2, 4 * ny, 128),
    ]
    mid = [l2, (3,) + l2, l2, l1, (3,) + l1, l1, (8, 24, 128), (10, 40, 128)]
    tiles = nx // 8

    right_side, conductivity, index = lax.optimization_barrier((right_side, conductivity, index))
    f, k, both1 = call(
        down0, [wide] * 2 + [(20, 16, 128)], [wide] * 6 + [(160, 256)],
        *finest([right_side, conductivity]), name="down0", room=14,
    )
    own = rows1(both1)
    last = jnp.concatenate([own[0:9], own[10:19]])
    initial = jnp.concatenate([own[1:10], own[11:20]])
    before, after = neighbours(last, initial, "gx")
    inner = [l1, l1, (288, 128), (3,) + l1, l1, l2, l2, (3,) + l2, l2]
    pair = (2, 24, 128)
    pieces, g1, k1, g2, k2, below, above = call(
        functools.partial(descend, True), [(nx, 8, 128), l1, l1, l2, l2, pair, pair], inner,
        before, own, after, name="descend", room=10,
    )
    pieces = everyone(pieces, "gx")
    (pieces,) = call(repack, [(ny * nz, 2 * tiles, 8, 128)], [], pieces, name="repack")
    outer = neighbours(below, above, "gx")
    s = everyone(pieces, ("gy", "gz"))
    v, value, turned, k3 = call(
        functools.partial(middle, nz), [wide, (8, 16, 128), (8, 16, 128), n3],
        low + mid + [(14, 48, 256), wide, (128, 256)] + [wide] * 4,
        index, f, k, s, g2, k2, g1, k1, *outer, name="middle", room=20, scalars=1,
    )
    own = rows1(lanes1(value, turned))
    before, after = neighbours(own, own, "gx")
    pieces, g1, g2 = call(
        functools.partial(descend, False), [(nx, 8, 128), l1, l2], inner,
        before, own, after, k1, k2, name="again", room=10,
    )
    pieces = everyone(pieces, "gx")
    (pieces,) = call(repack, [(ny * nz, tiles, 8, 128)], [], pieces, name="repack2")
    s = everyone(pieces, ("gy", "gz"))
    return tuple(call(
        functools.partial(final, nz), [(16, 32, 128)] * 2,
        low + mid + [(12, 48, 256)] + [wide] * 5,
        index, f, k, v, s, g2, k2, g1, k1, k3, name="final", room=20, scalars=1,
    ))


def solution(mesh):
    placed = P("gx", "gy", "gz")
    return jax.shard_map(
        body, mesh=mesh, in_specs=(placed, placed), out_specs=(placed, placed), check_vma=False
    )
```

```python
import functools

import jax
import jax.numpy as jnp
from jax import lax
from jax.experimental import pallas as pl
from jax.experimental.pallas import tpu as pltpu
from jax.sharding import PartitionSpec as P

LEVELS = 4
CSWEEPS = 6
absorption = 0.01
relaxation = 0.8
F32 = jnp.float32


def ring(n, b):
    return lambda at: jnp.where(at < (n + b) // 2, at, at - n)


def span(count, away=-1000, start=0):
    return lambda at: jnp.where((at >= start) & (at < start + count), at - start, away)


def matrix(shape, rows, columns, turned, values):
    a = rows(lax.broadcasted_iota(jnp.int32, shape, 0))
    b = columns(lax.broadcasted_iota(jnp.int32, shape, 1))
    return values(b, a) if turned else values(a, b)


def restriction(shape, rows, columns, turned=False):
    def values(coarse, fine):
        gap = fine - 2 * coarse
        outer, inner = (gap == -1) | (gap == 2), (gap == 0) | (gap == 1)
        return jnp.where(outer, 0.125, jnp.where(inner, 0.375, 0.0))

    return matrix(shape, rows, columns, turned, values)


def halving(shape, rows, columns, turned=False):
    def values(coarse, fine):
        return jnp.where((fine >> 1) == coarse, 0.5, 0.0)

    return matrix(shape, rows, columns, turned, values)


def prolongation(shape, rows, columns, turned=False):
    def values(fine, coarse):
        near = (fine >> 1) == coarse
        far = (fine >> 1) + 2 * (fine & 1) - 1 == coarse
        return jnp.where(near, 0.75, jnp.where(far, 0.25, 0.0))

    return matrix(shape, rows, columns, turned, values)


Y0, Z0, Y1, Z1, Y2, Z2 = ring(48, 32), ring(256, 128), ring(40, 16), ring(128, 64), ring(24, 8), ring(128, 32)


def parts(v):
    high = v.astype(jnp.bfloat16)
    rest = v - high.astype(F32)
    middle = rest.astype(jnp.bfloat16)
    return high, middle, (rest - middle.astype(F32)).astype(jnp.bfloat16)


def product(a, b):
    return lax.dot_general(a, b, (((1,), (0,)), ((), ())), preferred_element_type=F32)


def dot_left(m, v):
    m = m.astype(jnp.bfloat16)
    high, middle, low = (product(m, part) for part in parts(v))
    return high + (middle + low)


def dot_right(v, m):
    m = m.astype(jnp.bfloat16)
    high, middle, low = (product(part, m) for part in parts(v))
    return high + (middle + low)


def planes(lo, hi, step, carry=0, unroll=1):
    whole = (hi - lo) // unroll
    if whole > 1:
        carry = lax.fori_loop(0, whole, lambda t, c: step(lo + t * unroll, unroll, c), carry)
    elif whole == 1:
        carry = step(lo, unroll, carry)
    rest = (hi - lo) % unroll
    return step(hi - rest, rest, carry) if rest else carry


class Open:
    def above(self, v, dim):
        return pltpu.roll(v, v.shape[dim] - 1, dim)

    def below(self, v, dim):
        return pltpu.roll(v, 1, dim)

    def closed(self, k):
        return None


class Closed(Open):
    def __init__(self, shape, counts):
        self.last, self.first = [], []
        for dim in range(2):
            at = lax.broadcasted_iota(jnp.int32, shape, dim)
            self.last.append(jnp.where(at == counts[dim] - 1, 0.0, 1.0))
            self.first.append(jnp.where(at == 0, 0.0, 1.0))

    def above(self, v, dim):
        return super().above(v, dim) * self.last[dim]

    def below(self, v, dim):
        return super().below(v, dim) * self.first[dim]

    def closed(self, k):
        return k * ((1.0 - self.first[0]) + (1.0 - self.first[1]))


def weigh(k, wx, wy, wz, lo, hi, factor, shifts, d=None, mask=None, b=None, unroll=1):
    half = 0.5 * factor
    first = half * (k[lo - 1] + k[lo])
    wx[lo - 1] = first

    def step(i, n, below):
        here = [k[i + j] for j in range(n + 1)]
        outs = []
        for j in range(n):
            x = half * (here[j] + here[j + 1])
            y = half * (here[j] + shifts.above(here[j], 0))
            z = half * (here[j] + shifts.above(here[j], 1))
            ends, value = shifts.closed(half * here[j]), None
            if d is not None:
                value = (x + below) + (y + shifts.below(y, 0)) + (z + shifts.below(z, 1))
                if ends is not None:
                    value = value + ends
                value = relaxation / (value + absorption)
                if mask is not None:
                    value = mask(here[j], value)
            outs.append((x, y, z, ends, value))
            below = x
        for j, (x, y, z, ends, value) in enumerate(outs):
            wx[i + j], wy[i + j], wz[i + j] = x, y, z
            if ends is not None:
                b[i + j] = ends
            if value is not None:
                d[i + j] = value
        return below

    planes(lo, hi, step, first, unroll)


def image(v, wx, wy, wz, lo, hi, use, put, shifts, b=None, unroll=1):
    def step(i, n, below):
        here = [v[i + j] for j in range(n + 1)]
        outs = []
        for j in range(n):
            x = wx[i + j] * (here[j] - here[j + 1])
            y = wy[i + j] * (here[j] - shifts.above(here[j], 0))
            z = wz[i + j] * (here[j] - shifts.above(here[j], 1))
            total = (x - below) + (y - shifts.below(y, 0)) + (z - shifts.below(z, 1))
            if b is not None:
                total = total + b[i + j] * here[j]
            outs.append(use(i + j, here[j], total + absorption * here[j]))
            below = x
        for j, value in enumerate(outs):
            put(i + j, value)
        return below

    planes(lo, hi, step, wx[lo - 1] * (v[lo - 1] - v[lo]), unroll)


def into(ref, by=0):
    def put(i, value):
        ref[i + by] = value

    return put


def smooth(v, f, d, w, lo, hi, shifts, b=None, unroll=1, by=0):
    def use(i, here, im):
        return here + d[i] * (f[i + by] - im)

    image(v, *w, lo, hi, use, into(v), shifts, b, unroll)


def residual_of(v, f, r, w, lo, hi, shifts, mask=None, b=None, unroll=1):
    def use(i, here, im):
        value = f[i] - im
        return value if mask is None else jnp.where(mask[i] > 0.0, value, 0.0)

    image(v, *w, lo, hi, use, into(r), shifts, b, unroll)


def first_sweep(g, d, v, lo, hi, unroll, by=0):
    def step(i, n, carry):
        values = [g[i + j + by] * d[i + j] for j in range(n)]
        for j, value in enumerate(values):
            v[i + j] = value
        return carry

    planes(lo, hi, step, unroll=unroll)


def restrict(r, offset, lo, hi, ry, rz, held):
    size = ry.shape[0]
    for i in range(lo, hi):
        at = 2 * i + offset
        plane = 0.125 * (r[at - 1] + r[at + 2]) + 0.375 * (r[at] + r[at + 1])
        held[(i - lo) * size : (i - lo + 1) * size, :] = dot_left(ry, plane)
    return dot_right(held[: (hi - lo) * size, :], rz)


def halve(k, offset, lo, hi, cy, cz, held):
    size = cy.shape[0]
    for i in range(lo, hi):
        plane = 0.5 * (k[2 * i + offset] + k[2 * i + 1 + offset])
        held[(i - lo) * size : (i - lo + 1) * size, :] = dot_left(cy, plane)
    return dot_right(held[: (hi - lo) * size, :], cz)


def prolong(e, first, count, py, pz, finer, use, put):
    rows = e.shape[1]
    spread = dot_right(e[pl.ds(first, count)].reshape(count * rows, e.shape[2]), pz)
    for i in range(count):
        finer[i] = dot_left(py, spread[i * rows : (i + 1) * rows])

    def step(i, n, carry):
        held = [finer[i - 1 + j] for j in range(n + 2)]
        outs = []
        for j in range(n):
            here = 0.75 * held[j + 1]
            outs.append(use(2 * (i + j - 1), here + 0.25 * held[j]))
            outs.append(use(2 * (i + j - 1) + 1, here + 0.25 * held[j + 2]))
        for j, value in enumerate(outs):
            put(2 * (i - 1) + j, value)
        return carry

    planes(1, count - 1, step, unroll=max(1, 36 // (finer.shape[1] * finer.shape[2] // 1024)))


def three(w):
    return tuple(w.at[i] for i in range(3))


def inside(k, value):
    return jnp.where(k > 0.0, value, 0.0)


U0, U1, U2, U3 = 6, 12, 10, 16


def place(target, at, source, start, count, unroll=4):
    def step(i, n, carry):
        values = [source[start + i + j] for j in range(n)]
        for j, value in enumerate(values):
            target[at + i + j] = value
        return carry

    planes(0, count, step, unroll=unroll)


def down0(before, fo, ko, after, f, k, out, wx, wy, wz, d, v, r, held):
    shifts = Open()
    place(f, 5, fo, 0, 16)
    place(k, 5, ko, 0, 16)
    lane = lax.broadcasted_iota(jnp.int32, (48, 128), 1)
    ours = (lane < 25) | (lane >= 103)
    f[0] = f[25] = jnp.zeros((48, 256), F32)
    for ref, at, shift in ((before, 0, 1), (after, 21, 0)):
        for j in range(5):
            tail = ref[9 + j]
            k[at + j, :, :128] = ref[4 + j]
            k[at + j, :, 128:] = jnp.where(ours, pltpu.roll(tail, 78, 1), 0.0)
            if 0 <= j - shift < 4:
                f[at + j, :, :128] = ref[j - shift]
                f[at + j, :, 128:] = jnp.where(ours, tail, 0.0)
    weigh(k, wx, wy, wz, 1, 25, 1.0, shifts, d, inside, unroll=U0)
    first_sweep(f, d, v, 1, 25, U0)
    residual_of(v, f, r, (wx, wy, wz), 2, 24, shifts, k, unroll=U0)
    ry, rz = restriction((16, 48), span(16), Y0), restriction((256, 128), Z0, Z1, True)
    out[:10] = restrict(r, 5, -1, 9, ry, rz, held).reshape(10, 16, 128)
    cy, cz = halving((16, 48), span(16), Y0), halving((256, 128), Z0, Z1, True)
    out[10:] = halve(k, 5, -1, 9, cy, cz, held).reshape(10, 16, 128)


def descend(first, *refs):
    shifts = Open()
    before, own, after = refs[:3]
    if first:
        out, g1, k1, g2, k2, below, above = refs[3:10]
        for ref, at in ((g1, 0), (k1, 1)):
            place(ref, 0, before, 9 * at, 9, 9)
            place(ref, 9, own, 10 * at + 1, 8, 8)
            place(ref, 17, after, 9 * at, 9, 9)
    else:
        k1, k2, out, g1, g2 = refs[3:8]
        zero = jnp.zeros(g1.shape[1:], F32)
        g1[0], g1[25] = zero, zero
        for ref, at in ((before, 1), (own, 9), (after, 17)):
            place(g1, at, ref, 0, 8, 8)
    v1, r1, held, w1, d1, v2, r2, w2, d2 = refs[-9:]
    w1, w2 = three(w1), three(w2)
    rows = g2.shape[1]
    weigh(k1, *w1, 1, 25, 0.25, shifts, d1, inside, unroll=U1)
    first_sweep(g1, d1, v1, 1, 25, U1)
    residual_of(v1, g1, r1, w1, 2, 24, shifts, d1, unroll=U1)
    zero = jnp.zeros(g2.shape[1:], F32)
    g2[0], g2[11] = zero, zero
    ry1, rz1 = restriction((24, 40), Y2, Y1), restriction((128, 128), Z1, Z2, True)
    g2[1:11] = restrict(r1, 9, -3, 7, ry1, rz1, held).reshape(10, rows, 128)
    if first:
        cy1, cz1 = halving((24, 40), Y2, Y1), halving((128, 128), Z1, Z2, True)
        k2[...] = halve(k1, 9, -4, 8, cy1, cz1, held).reshape(k2.shape)
    weigh(k2, *w2, 1, 11, 0.25**2, shifts, d2, inside, unroll=U2)
    if first:
        below[0], below[1], above[0], above[1] = g2[4], d2[4], g2[7], d2[7]
    first_sweep(g2, d2, v2, 1, 11, U2)
    residual_of(v2, g2, r2, w2, 3, 9, shifts, d2, unroll=U2)
    total = None
    for i in range(2):
        at = 2 * i + 4
        plane = 0.125 * (r2[at - 1] + r2[at + 2]) + 0.375 * (r2[at] + r2[at + 1])
        value = dot_left(restriction((8, 24), span(4, start=4 * i), Y2), plane)
        total = value if total is None else total + value
    tile = dot_right(total, restriction((128, 128), Z2, span(16), True))
    if first:
        part = [
            dot_left(halving((8, 24), span(4, start=4 * i), Y2), 0.5 * (k2[2 * i + 4] + k2[2 * i + 5]))
            for i in range(2)
        ]
        tile = tile + dot_right(part[0] + part[1], halving((128, 128), Z2, span(16, start=16), True))
    for i in range(out.shape[0]):
        out[i] = tile


def repack(s, out):
    tiles = 2 * s.shape[0] // 16
    lane = lax.broadcasted_iota(jnp.int32, (8, 128), 1) // 16
    row = lax.broadcasted_iota(jnp.int32, (8, 128), 0) // 4
    for field in range(out.shape[1] // tiles):
        for t in range(tiles):
            total = jnp.zeros((8, 128), F32)
            for half in range(2):
                for p in range(8):
                    plane = 16 * t + 8 * half + p
                    part = s[plane // 2]
                    if plane % 2 != half:
                        part = pltpu.roll(part, 4, 0)
                    if p != field:
                        part = pltpu.roll(part, (16 * (p - field)) % 128, 1)
                    total = jnp.where((lane == p) & (row == half), part, total)
            for i in range(out.shape[0]):
                out[i, field * tiles + t] = total


def unpack(s, first, tiles, nz, whole):
    lane = lax.broadcasted_iota(jnp.int32, (8, 128), 1) // 16
    for j in range(s.shape[0] // nz):
        for t in range(tiles):
            for p in range(8):
                total = jnp.zeros((8, 128), F32)
                for q in range(nz):
                    part = s[j * nz + q, first + t]
                    if p != q:
                        part = pltpu.roll(part, (16 * (q - p)) % 128, 1)
                    total = jnp.where(lane == q, part, total)
                whole[16 * t + p + 3, 4 * j : 4 * j + 4] = total[:4]
                whole[16 * t + p + 11, 4 * j : 4 * j + 4] = total[4:]


def bottom(nz, s, k3, scratch):
    g3, v3, r3, w3, d3, b3, k4, g4, v4, w4, d4, b4, held, fine4 = scratch
    n4 = g4.shape[0]
    lanes3, lanes4 = span(16 * nz, -3000), span(8 * nz, -9000)
    rows3, rows4 = span(g3.shape[1]), span(g4.shape[1])
    tall, wide = (g4.shape[1], g3.shape[1]), (128, 128)
    n3, two = 2 * n4, s.shape[1] == n4 // 4
    rows, lanes = g3.shape[1], g3.shape[2]
    zero = jnp.zeros((rows, lanes), F32)
    for i in (0, 1, 2, n3 + 3, n3 + 4, n3 + 5):
        v3[i], r3[i] = zero, zero
        if two:
            k3[i] = zero
    for ref in (k4, v4):
        for i in (0, n4 + 1):
            ref[i] = jnp.zeros(ref.shape[1:], F32)
    unpack(s, 0, n3 // 16, nz, g3)
    if two:
        unpack(s, n3 // 16, n3 // 16, nz, k3)
    cy3, cz3 = halving(tall, rows4, rows3), halving(wide, lanes3, lanes4, True)
    k4[1 : n4 + 1] = halve(k3, 3, 0, n4, cy3, cz3, held).reshape(g4.shape)
    shifts3 = Closed((rows, lanes), (rows, 16 * nz))
    shifts4 = Closed((k4.shape[1], lanes), (k4.shape[1], 8 * nz))
    w3, w4 = three(w3), three(w4)
    weigh(k3, *w3, 3, n3 + 3, 0.25**3, shifts3, d3, inside, b3, U3)
    weigh(k4, *w4, 1, n4 + 1, 0.25**4, shifts4, d4, inside, b4, U3)
    first_sweep(g3, d3, v3, 3, n3 + 3, U3)
    residual_of(v3, g3, r3, w3, 3, n3 + 3, shifts3, b=b3, unroll=U3)
    ry3, rz3 = restriction(tall, rows4, rows3), restriction(wide, lanes3, lanes4, True)
    g4[...] = restrict(r3, 3, 0, n4, ry3, rz3, held).reshape(g4.shape)
    first_sweep(g4, d4, v4, 1, n4 + 1, U3, by=-1)

    def turn(j, carry):
        smooth(v4, g4, d4, w4, 1, n4 + 1, shifts4, b4, n4, by=-1)
        return carry

    lax.fori_loop(0, CSWEEPS - 1, turn, 0)

    def use(i, value):
        return v3[i + 3] + value

    py3, pz3 = prolongation(tall[::-1], rows3, rows4), prolongation(wide, lanes4, lanes3, True)
    prolong(v4, 0, n4 + 2, py3, pz3, fine4, use, into(v3, 3))
    smooth(v3, g3, d3, w3, 3, n3 + 3, shifts3, b3, U3)
    return v3


def spread_matrix(shape, dim_fine, coarse_start, block_fine):
    fine = lax.broadcasted_iota(jnp.int32, shape, dim_fine)
    size = shape[dim_fine]
    fine = jnp.where(fine < (size + block_fine) // 2, fine, fine - size)
    whole = lax.broadcasted_iota(jnp.int32, shape, 1 - dim_fine)
    near = (fine >> 1) + coarse_start
    far = near + 2 * (fine & 1) - 1
    return jnp.where(whole == near, 0.75, jnp.where(whole == far, 0.25, 0.0))


def upward(index, e3, g2, k2, g1, k1, ends, scratch):
    v2, w2, d2, v1, w1, d1, fine2, fine1 = scratch
    shifts, w2, w1 = Open(), three(w2), three(w1)
    weigh(k2, *w2, 1, 11, 0.25**2, shifts, d2, inside, unroll=U2)
    weigh(k1, *w1, 5, 21, 0.25, shifts, d1, inside, unroll=U1)
    first_sweep(g2, d2, v2, 1, 11, U2)
    first_sweep(g1, d1, v1, 5, 21, U1)
    zero = jnp.zeros(d2.shape[1:], F32)
    for i, n in ((0, 0), (11, 1)):
        v2[i] = zero if ends is None else ends[n][0] * ends[n][1]
        d2[i] = zero if ends is None else ends[n][1]

    def use2(i, value):
        return jnp.where(d2[i] > 0.0, v2[i] + value, 0.0)

    py2 = spread_matrix((g2.shape[1], e3.shape[1]), 0, index[1] * 4, 8)
    pz2 = spread_matrix((e3.shape[2], g2.shape[2]), 1, index[2] * 16, 32)
    prolong(e3, index[0] * 2, 8, py2, pz2, fine2, use2, into(v2))
    smooth(v2, g2, d2, w2, 1, 11, shifts, unroll=U2)

    def use1(i, value):
        return jnp.where(d1[i + 5] > 0.0, v1[i + 5] + value, 0.0)

    py1, pz1 = prolongation((40, 24), Y1, Y2), prolongation((128, 128), Z2, Z1, True)
    prolong(v2, 1, 10, py1, pz1, fine1, use1, into(v1, 5))
    smooth(v1, g1, d1, w1, 6, 20, shifts, unroll=U1)
    return v1


BOTTOM = 14
UP = 8


def middle(nz, index, f, k, s, g2, k2, g1, k1, *refs):
    ends, (v, gn, turned, k3) = refs[:2], refs[2:6]
    low, mid, (fine0, r, held0, wx, wy, wz, d) = refs[6:20], refs[20:28], refs[28:]
    weigh(k, wx, wy, wz, 1, 25, 1.0, Open(), d, inside, unroll=U0)
    e3 = bottom(nz, s, k3, low)
    e1 = upward(index, e3, g2, k2, g1, k1, ends, mid)
    w, shifts = (wx, wy, wz), Open()

    def use(i, value):
        return inside(k[i + 1], f[i + 1] * d[i + 1] + value)

    py0, pz0 = prolongation((48, 40), Y0, Y1), prolongation((128, 256), Z1, Z0, True)
    prolong(e1, 6, 14, py0, pz0, fine0, use, into(v, 1))
    smooth(v, f, d, w, 2, 24, shifts, unroll=U0)
    smooth(v, f, d, w, 3, 23, shifts, unroll=U0)
    residual_of(v, f, r, w, 4, 22, shifts, k, unroll=U0)
    ry, rz = restriction((16, 48), span(16), Y0), restriction((256, 128), Z0, Z1, True)
    value = restrict(r, 5, 0, 8, ry, rz, held0)
    gn[...] = value.reshape(gn.shape)
    turned[...] = pltpu.roll(value, 64, 1).reshape(gn.shape)


def final(nz, index, f, k, v0, s, g2, k2, g1, k1, *refs):
    k3, (solution_, residual_) = refs[0], refs[1:3]
    low, mid, (fine0, wx, wy, wz, d, v) = refs[3:17], refs[17:25], refs[25:]
    weigh(k, wx, wy, wz, 3, 22, 1.0, Open(), d, inside, unroll=U0)
    e3 = bottom(nz, s, k3, low)
    e1 = upward(index, e3, g2, k2, g1, k1, None, mid)
    w, shifts = (wx, wy, wz), Open()

    def use(i, value):
        return inside(k[i + 3], v0[i + 3] + value)

    py0, pz0 = prolongation((48, 40), Y0, Y1), prolongation((128, 256), Z1, Z0, True)
    prolong(e1, 7, 12, py0, pz0, fine0, use, into(v, 3))
    smooth(v, f, d, w, 4, 22, shifts, unroll=U0)

    def last(i, here, im):
        return here[:32, :128], (f[i] - im)[:32, :128]

    def out(i, values):
        solution_[i - 5], residual_[i - 5] = values

    image(v, *w, 5, 21, last, out, shifts, unroll=U0)


def call(kernel, outs, scratch, *args, name, scalars=0, room=4):
    vmem = pl.BlockSpec(memory_space=pltpu.VMEM)
    smem = pl.BlockSpec(memory_space=pltpu.SMEM)
    return pl.pallas_call(
        kernel,
        out_shape=[jax.ShapeDtypeStruct(o, F32) for o in outs],
        in_specs=[smem] * scalars + [vmem] * (len(args) - scalars),
        out_specs=[vmem] * len(outs),
        scratch_shapes=[pltpu.VMEM(s, F32) for s in scratch],
        compiler_params=pltpu.CompilerParams(vmem_limit_bytes=room << 20),
        name=name,
    )(*args)


def neighbours(last, initial, axis):
    count = lax.axis_size(axis)
    if axis == "gz":
        up = [(i, (i + 1) % count) for i in range(count)]
    else:
        up = [(i, i + 1) for i in range(count - 1)]
    down = [(j, i) for i, j in up]
    before = lax.ppermute(last, axis, up)
    after = lax.ppermute(initial, axis, down)
    if axis == "gz":
        at = lax.axis_index(axis)
        before = jnp.where(at == 0, 0.0, before)
        after = jnp.where(at == count - 1, 0.0, after)
    return before, after


def finest(fields):
    for axis, dim, size, count, width in (("gz", 2, 128, 256, 25), ("gy", 1, 32, 48, 5)):
        along = 2 if dim == 2 else 0
        last = [lax.slice_in_dim(v, size - width, size, axis=dim) for v in fields]
        initial = [lax.slice_in_dim(v, 0, width, axis=dim) for v in fields]
        before, after = neighbours(
            jnp.concatenate(last, along), jnp.concatenate(initial, along), axis
        )
        before, after = jnp.split(before, 2, along), jnp.split(after, 2, along)
        gap = list(fields[0].shape)
        gap[dim] = count - size - 2 * width
        gap = jnp.zeros(gap, F32)
        fields = [
            jnp.concatenate([v, a, gap, b], dim) for b, v, a in zip(before, fields, after)
        ]
    f, k = fields
    lane = jnp.arange(128)
    ours = (lane < 25) | (lane >= 103)

    def packed(at, shift):
        start = at + shift
        tail = jnp.pad(f[start : start + 4, :, 128:], ((shift, 1 - shift), (0, 0), (0, 0)))
        tail = jnp.where(ours, tail, jnp.roll(k[at : at + 5, :, 128:], 50, 2))
        return jnp.concatenate([f[start : start + 4, :, :128], k[at : at + 5, :, :128], tail])

    before, after = neighbours(packed(11, 1), packed(0, 0), "gx")
    return before, f, k, after


def rows1(values):
    before, after = neighbours(values, values, "gy")
    gap = jnp.zeros((values.shape[0], 2, 128), F32)
    return jnp.concatenate([values, after[:, :11], gap, before[:, 5:]], 1)


def lanes1(values, turned):
    before, after = neighbours(turned, turned, "gz")
    lane = jnp.arange(128)
    zero = jnp.where(lane >= 117, before, 0.0)
    return jnp.where(lane < 64, values, jnp.where(lane < 75, after, zero))


def everyone(pieces, axes):
    return lax.all_to_all(pieces, axes, 0, 0)


def body(right_side, conductivity):
    nx, ny, nz = (lax.axis_size(axis) for axis in ("gx", "gy", "gz"))
    index = jnp.stack([lax.axis_index(axis) for axis in ("gx", "gy", "gz")]).astype(jnp.int32)

    wide, l1, l2 = (26, 48, 256), (26, 40, 128), (12, 24, 128)
    n3, n4 = (2 * nx + 6, 4 * ny, 128), (nx + 2, 2 * ny, 128)
    low = [
        n3, n3, n3, (3,) + n3, n3, n3,
        n4, (nx, 2 * ny, 128), n4, (3,) + n4, n4, n4,
        (nx * 2 * ny, 128), (nx + 2, 4 * ny, 128),
    ]
    mid = [l2, (3,) + l2, l2, l1, (3,) + l1, l1, (8, 24, 128), (10, 40, 128)]
    tiles = nx // 8

    right_side, conductivity, index = lax.optimization_barrier((right_side, conductivity, index))
    f, k, both1 = call(
        down0, [wide] * 2 + [(20, 16, 128)], [wide] * 6 + [(160, 256)],
        *finest([right_side, conductivity]), name="down0", room=14,
    )
    own = rows1(both1)
    last = jnp.concatenate([own[0:9], own[10:19]])
    initial = jnp.concatenate([own[1:10], own[11:20]])
    before, after = neighbours(last, initial, "gx")
    inner = [l1, l1, (288, 128), (3,) + l1, l1, l2, l2, (3,) + l2, l2]
    pair = (2, 24, 128)
    pieces, g1, k1, g2, k2, below, above = call(
        functools.partial(descend, True), [(nx, 8, 128), l1, l1, l2, l2, pair, pair], inner,
        before, own, after, name="descend", room=10,
    )
    pieces = everyone(pieces, "gx")
    (pieces,) = call(repack, [(ny * nz, 2 * tiles, 8, 128)], [], pieces, name="repack")
    outer = neighbours(below, above, "gx")
    s = everyone(pieces, ("gy", "gz"))
    v, value, turned, k3 = call(
        functools.partial(middle, nz), [wide, (8, 16, 128), (8, 16, 128), n3],
        low + mid + [(14, 48, 256), wide, (128, 256)] + [wide] * 4,
        index, f, k, s, g2, k2, g1, k1, *outer, name="middle", room=20, scalars=1,
    )
    own = rows1(lanes1(value, turned))
    before, after = neighbours(own, own, "gx")
    pieces, g1, g2 = call(
        functools.partial(descend, False), [(nx, 8, 128), l1, l2], inner,
        before, own, after, k1, k2, name="again", room=10,
    )
    pieces = everyone(pieces, "gx")
    (pieces,) = call(repack, [(ny * nz, tiles, 8, 128)], [], pieces, name="repack2")
    s = everyone(pieces, ("gy", "gz"))
    return tuple(call(
        functools.partial(final, nz), [(16, 32, 128)] * 2,
        low + mid + [(12, 48, 256)] + [wide] * 5,
        index, f, k, v, s, g2, k2, g1, k1, k3, name="final", room=20, scalars=1,
    ))


def solution(mesh):
    placed = P("gx", "gy", "gz")
    return jax.shard_map(
        body, mesh=mesh, in_specs=(placed, placed), out_specs=(placed, placed), check_vma=False
    )
```

```python
import functools

import jax
import jax.numpy as jnp
from jax import lax
from jax.experimental import pallas as pl
from jax.experimental.pallas import tpu as pltpu
from jax.sharding import PartitionSpec as P

LEVELS = 4
CSWEEPS = 6
absorption = 0.01
relaxation = 0.8
F32 = jnp.float32


def ring(n, b):
    return lambda at: jnp.where(at < (n + b) // 2, at, at - n)


def span(count, away=-1000, start=0):
    return lambda at: jnp.where((at >= start) & (at < start + count), at - start, away)


def matrix(shape, rows, columns, turned, values):
    a = rows(lax.broadcasted_iota(jnp.int32, shape, 0))
    b = columns(lax.broadcasted_iota(jnp.int32, shape, 1))
    return values(b, a) if turned else values(a, b)


def restriction(shape, rows, columns, turned=False):
    def values(coarse, fine):
        gap = fine - 2 * coarse
        outer, inner = (gap == -1) | (gap == 2), (gap == 0) | (gap == 1)
        return jnp.where(outer, 0.125, jnp.where(inner, 0.375, 0.0))

    return matrix(shape, rows, columns, turned, values)


def halving(shape, rows, columns, turned=False):
    def values(coarse, fine):
        return jnp.where((fine >> 1) == coarse, 0.5, 0.0)

    return matrix(shape, rows, columns, turned, values)


def prolongation(shape, rows, columns, turned=False):
    def values(fine, coarse):
        near = (fine >> 1) == coarse
        far = (fine >> 1) + 2 * (fine & 1) - 1 == coarse
        return jnp.where(near, 0.75, jnp.where(far, 0.25, 0.0))

    return matrix(shape, rows, columns, turned, values)


Y0, Z0, Y1, Z1, Y2, Z2 = ring(48, 32), ring(256, 128), ring(40, 16), ring(128, 64), ring(24, 8), ring(128, 32)


def parts(v):
    high = v.astype(jnp.bfloat16)
    rest = v - high.astype(F32)
    middle = rest.astype(jnp.bfloat16)
    return high, middle, (rest - middle.astype(F32)).astype(jnp.bfloat16)


def product(a, b):
    return lax.dot_general(a, b, (((1,), (0,)), ((), ())), preferred_element_type=F32)


def dot_left(m, v):
    m = m.astype(jnp.bfloat16)
    high, middle, low = (product(m, part) for part in parts(v))
    return high + (middle + low)


def dot_right(v, m):
    m = m.astype(jnp.bfloat16)
    high, middle, low = (product(part, m) for part in parts(v))
    return high + (middle + low)


def planes(lo, hi, step, carry=0, unroll=1):
    whole = (hi - lo) // unroll
    if whole > 1:
        carry = lax.fori_loop(0, whole, lambda t, c: step(lo + t * unroll, unroll, c), carry)
    elif whole == 1:
        carry = step(lo, unroll, carry)
    rest = (hi - lo) % unroll
    return step(hi - rest, rest, carry) if rest else carry


class Open:
    def above(self, v, dim):
        return pltpu.roll(v, v.shape[dim] - 1, dim)

    def below(self, v, dim):
        return pltpu.roll(v, 1, dim)

    def closed(self, k):
        return None


class Closed(Open):
    def __init__(self, shape, counts):
        self.last, self.first = [], []
        for dim in range(2):
            at = lax.broadcasted_iota(jnp.int32, shape, dim)
            self.last.append(jnp.where(at == counts[dim] - 1, 0.0, 1.0))
            self.first.append(jnp.where(at == 0, 0.0, 1.0))

    def above(self, v, dim):
        return super().above(v, dim) * self.last[dim]

    def below(self, v, dim):
        return super().below(v, dim) * self.first[dim]

    def closed(self, k):
        return k * ((1.0 - self.first[0]) + (1.0 - self.first[1]))


def weigh(k, wx, wy, wz, lo, hi, factor, shifts, d=None, mask=None, b=None, unroll=1):
    half = 0.5 * factor
    first = half * (k[lo - 1] + k[lo])
    wx[lo - 1] = first

    def step(i, n, below):
        here = [k[i + j] for j in range(n + 1)]
        outs = []
        for j in range(n):
            x = half * (here[j] + here[j + 1])
            y = half * (here[j] + shifts.above(here[j], 0))
            z = half * (here[j] + shifts.above(here[j], 1))
            ends, value = shifts.closed(half * here[j]), None
            if d is not None:
                value = (x + below) + (y + shifts.below(y, 0)) + (z + shifts.below(z, 1))
                if ends is not None:
                    value = value + ends
                value = relaxation / (value + absorption)
                if mask is not None:
                    value = mask(here[j], value)
            outs.append((x, y, z, ends, value))
            below = x
        for j, (x, y, z, ends, value) in enumerate(outs):
            wx[i + j], wy[i + j], wz[i + j] = x, y, z
            if ends is not None:
                b[i + j] = ends
            if value is not None:
                d[i + j] = value
        return below

    planes(lo, hi, step, first, unroll)


def image(v, wx, wy, wz, lo, hi, use, put, shifts, b=None, unroll=1):
    def step(i, n, below):
        here = [v[i + j] for j in range(n + 1)]
        outs = []
        for j in range(n):
            x = wx[i + j] * (here[j] - here[j + 1])
            y = wy[i + j] * (here[j] - shifts.above(here[j], 0))
            z = wz[i + j] * (here[j] - shifts.above(here[j], 1))
            total = (x - below) + (y - shifts.below(y, 0)) + (z - shifts.below(z, 1))
            if b is not None:
                total = total + b[i + j] * here[j]
            outs.append(use(i + j, here[j], total + absorption * here[j]))
            below = x
        for j, value in enumerate(outs):
            put(i + j, value)
        return below

    planes(lo, hi, step, wx[lo - 1] * (v[lo - 1] - v[lo]), unroll)


def into(ref, by=0):
    def put(i, value):
        ref[i + by] = value

    return put


def smooth(v, f, d, w, lo, hi, shifts, b=None, unroll=1, by=0):
    def use(i, here, im):
        return here + d[i] * (f[i + by] - im)

    image(v, *w, lo, hi, use, into(v), shifts, b, unroll)


def residual_of(v, f, r, w, lo, hi, shifts, mask=None, b=None, unroll=1):
    def use(i, here, im):
        value = f[i] - im
        return value if mask is None else jnp.where(mask[i] > 0.0, value, 0.0)

    image(v, *w, lo, hi, use, into(r), shifts, b, unroll)


def first_sweep(g, d, v, lo, hi, unroll, by=0):
    def step(i, n, carry):
        values = [g[i + j + by] * d[i + j] for j in range(n)]
        for j, value in enumerate(values):
            v[i + j] = value
        return carry

    planes(lo, hi, step, unroll=unroll)


def restrict(r, offset, lo, hi, ry, rz, held):
    size = ry.shape[0]
    for i in range(lo, hi):
        at = 2 * i + offset
        plane = 0.125 * (r[at - 1] + r[at + 2]) + 0.375 * (r[at] + r[at + 1])
        held[(i - lo) * size : (i - lo + 1) * size, :] = dot_left(ry, plane)
    return dot_right(held[: (hi - lo) * size, :], rz)


def halve(k, offset, lo, hi, cy, cz, held):
    size = cy.shape[0]
    for i in range(lo, hi):
        plane = 0.5 * (k[2 * i + offset] + k[2 * i + 1 + offset])
        held[(i - lo) * size : (i - lo + 1) * size, :] = dot_left(cy, plane)
    return dot_right(held[: (hi - lo) * size, :], cz)


def prolong(e, first, count, py, pz, finer, use, put):
    rows = e.shape[1]
    spread = dot_right(e[pl.ds(first, count)].reshape(count * rows, e.shape[2]), pz)
    for i in range(count):
        finer[i] = dot_left(py, spread[i * rows : (i + 1) * rows])

    def step(i, n, carry):
        held = [finer[i - 1 + j] for j in range(n + 2)]
        outs = []
        for j in range(n):
            here = 0.75 * held[j + 1]
            outs.append(use(2 * (i + j - 1), here + 0.25 * held[j]))
            outs.append(use(2 * (i + j - 1) + 1, here + 0.25 * held[j + 2]))
        for j, value in enumerate(outs):
            put(2 * (i - 1) + j, value)
        return carry

    planes(1, count - 1, step, unroll=max(1, 36 // (finer.shape[1] * finer.shape[2] // 1024)))


def three(w):
    return tuple(w.at[i] for i in range(3))


def inside(k, value):
    return jnp.where(k > 0.0, value, 0.0)


U0, U1, U2, U3 = 6, 12, 10, 32


def place(target, at, source, start, count, unroll=4):
    def step(i, n, carry):
        values = [source[start + i + j] for j in range(n)]
        for j, value in enumerate(values):
            target[at + i + j] = value
        return carry

    planes(0, count, step, unroll=unroll)


def down0(before, fo, ko, after, f, k, out, wx, wy, wz, d, v, r, held):
    shifts = Open()
    place(f, 5, fo, 0, 16)
    place(k, 5, ko, 0, 16)
    lane = lax.broadcasted_iota(jnp.int32, (48, 128), 1)
    ours = (lane < 25) | (lane >= 103)
    f[0] = f[25] = jnp.zeros((48, 256), F32)
    for ref, at, shift in ((before, 0, 1), (after, 21, 0)):
        for j in range(5):
            tail = ref[9 + j]
            k[at + j, :, :128] = ref[4 + j]
            k[at + j, :, 128:] = jnp.where(ours, pltpu.roll(tail, 78, 1), 0.0)
            if 0 <= j - shift < 4:
                f[at + j, :, :128] = ref[j - shift]
                f[at + j, :, 128:] = jnp.where(ours, tail, 0.0)
    weigh(k, wx, wy, wz, 1, 25, 1.0, shifts, d, inside, unroll=U0)
    first_sweep(f, d, v, 1, 25, U0)
    residual_of(v, f, r, (wx, wy, wz), 2, 24, shifts, k, unroll=U0)
    ry, rz = restriction((16, 48), span(16), Y0), restriction((256, 128), Z0, Z1, True)
    out[:10] = restrict(r, 5, -1, 9, ry, rz, held).reshape(10, 16, 128)
    cy, cz = halving((16, 48), span(16), Y0), halving((256, 128), Z0, Z1, True)
    out[10:] = halve(k, 5, -1, 9, cy, cz, held).reshape(10, 16, 128)


def descend(first, *refs):
    shifts = Open()
    before, own, after = refs[:3]
    if first:
        out, g1, k1, g2, k2, below, above = refs[3:10]
        for ref, at in ((g1, 0), (k1, 1)):
            place(ref, 0, before, 9 * at, 9, 9)
            place(ref, 9, own, 10 * at + 1, 8, 8)
            place(ref, 17, after, 9 * at, 9, 9)
    else:
        k1, k2, out, g1, g2 = refs[3:8]
        zero = jnp.zeros(g1.shape[1:], F32)
        g1[0], g1[25] = zero, zero
        for ref, at in ((before, 1), (own, 9), (after, 17)):
            place(g1, at, ref, 0, 8, 8)
    v1, r1, held, w1, d1, v2, r2, w2, d2 = refs[-9:]
    w1, w2 = three(w1), three(w2)
    rows = g2.shape[1]
    weigh(k1, *w1, 1, 25, 0.25, shifts, d1, inside, unroll=U1)
    first_sweep(g1, d1, v1, 1, 25, U1)
    residual_of(v1, g1, r1, w1, 2, 24, shifts, d1, unroll=U1)
    zero = jnp.zeros(g2.shape[1:], F32)
    g2[0], g2[11] = zero, zero
    ry1, rz1 = restriction((24, 40), Y2, Y1), restriction((128, 128), Z1, Z2, True)
    g2[1:11] = restrict(r1, 9, -3, 7, ry1, rz1, held).reshape(10, rows, 128)
    if first:
        cy1, cz1 = halving((24, 40), Y2, Y1), halving((128, 128), Z1, Z2, True)
        k2[...] = halve(k1, 9, -4, 8, cy1, cz1, held).reshape(k2.shape)
    weigh(k2, *w2, 1, 11, 0.25**2, shifts, d2, inside, unroll=U2)
    if first:
        below[0], below[1], above[0], above[1] = g2[4], d2[4], g2[7], d2[7]
    first_sweep(g2, d2, v2, 1, 11, U2)
    residual_of(v2, g2, r2, w2, 3, 9, shifts, d2, unroll=U2)
    total = None
    for i in range(2):
        at = 2 * i + 4
        plane = 0.125 * (r2[at - 1] + r2[at + 2]) + 0.375 * (r2[at] + r2[at + 1])
        value = dot_left(restriction((8, 24), span(4, start=4 * i), Y2), plane)
        total = value if total is None else total + value
    tile = dot_right(total, restriction((128, 128), Z2, span(16), True))
    if first:
        part = [
            dot_left(halving((8, 24), span(4, start=4 * i), Y2), 0.5 * (k2[2 * i + 4] + k2[2 * i + 5]))
            for i in range(2)
        ]
        tile = tile + dot_right(part[0] + part[1], halving((128, 128), Z2, span(16, start=16), True))
    for i in range(out.shape[0]):
        out[i] = tile


def repack(s, out):
    tiles = 2 * s.shape[0] // 16
    lane = lax.broadcasted_iota(jnp.int32, (8, 128), 1) // 16
    row = lax.broadcasted_iota(jnp.int32, (8, 128), 0) // 4
    for field in range(out.shape[1] // tiles):
        for t in range(tiles):
            total = jnp.zeros((8, 128), F32)
            for half in range(2):
                for p in range(8):
                    plane = 16 * t + 8 * half + p
                    part = s[plane // 2]
                    if plane % 2 != half:
                        part = pltpu.roll(part, 4, 0)
                    if p != field:
                        part = pltpu.roll(part, (16 * (p - field)) % 128, 1)
                    total = jnp.where((lane == p) & (row == half), part, total)
            for i in range(out.shape[0]):
                out[i, field * tiles + t] = total


def unpack(s, first, tiles, nz, whole):
    lane = lax.broadcasted_iota(jnp.int32, (8, 128), 1) // 16
    for j in range(s.shape[0] // nz):
        for t in range(tiles):
            for p in range(8):
                total = jnp.zeros((8, 128), F32)
                for q in range(nz):
                    part = s[j * nz + q, first + t]
                    if p != q:
                        part = pltpu.roll(part, (16 * (q - p)) % 128, 1)
                    total = jnp.where(lane == q, part, total)
                whole[16 * t + p + 3, 4 * j : 4 * j + 4] = total[:4]
                whole[16 * t + p + 11, 4 * j : 4 * j + 4] = total[4:]


def bottom(nz, s, k3, scratch):
    g3, v3, r3, w3, d3, b3, k4, g4, v4, w4, d4, b4, held, fine4 = scratch
    n4 = g4.shape[0]
    lanes3, lanes4 = span(16 * nz, -3000), span(8 * nz, -9000)
    rows3, rows4 = span(g3.shape[1]), span(g4.shape[1])
    tall, wide = (g4.shape[1], g3.shape[1]), (128, 128)
    n3, two = 2 * n4, s.shape[1] == n4 // 4
    rows, lanes = g3.shape[1], g3.shape[2]
    zero = jnp.zeros((rows, lanes), F32)
    for i in (0, 1, 2, n3 + 3, n3 + 4, n3 + 5):
        v3[i], r3[i] = zero, zero
        if two:
            k3[i] = zero
    for ref in (k4, v4):
        for i in (0, n4 + 1):
            ref[i] = jnp.zeros(ref.shape[1:], F32)
    unpack(s, 0, n3 // 16, nz, g3)
    if two:
        unpack(s, n3 // 16, n3 // 16, nz, k3)
    cy3, cz3 = halving(tall, rows4, rows3), halving(wide, lanes3, lanes4, True)
    k4[1 : n4 + 1] = halve(k3, 3, 0, n4, cy3, cz3, held).reshape(g4.shape)
    shifts3 = Closed((rows, lanes), (rows, 16 * nz))
    shifts4 = Closed((k4.shape[1], lanes), (k4.shape[1], 8 * nz))
    w3, w4 = three(w3), three(w4)
    weigh(k3, *w3, 3, n3 + 3, 0.25**3, shifts3, d3, inside, b3, U3)
    weigh(k4, *w4, 1, n4 + 1, 0.25**4, shifts4, d4, inside, b4, U3)
    first_sweep(g3, d3, v3, 3, n3 + 3, U3)
    residual_of(v3, g3, r3, w3, 3, n3 + 3, shifts3, b=b3, unroll=U3)
    ry3, rz3 = restriction(tall, rows4, rows3), restriction(wide, lanes3, lanes4, True)
    g4[...] = restrict(r3, 3, 0, n4, ry3, rz3, held).reshape(g4.shape)
    first_sweep(g4, d4, v4, 1, n4 + 1, U3, by=-1)

    def turn(j, carry):
        smooth(v4, g4, d4, w4, 1, n4 + 1, shifts4, b4, n4, by=-1)
        return carry

    lax.fori_loop(0, CSWEEPS - 1, turn, 0)

    def use(i, value):
        return v3[i + 3] + value

    py3, pz3 = prolongation(tall[::-1], rows3, rows4), prolongation(wide, lanes4, lanes3, True)
    prolong(v4, 0, n4 + 2, py3, pz3, fine4, use, into(v3, 3))
    smooth(v3, g3, d3, w3, 3, n3 + 3, shifts3, b3, U3)
    return v3


def spread_matrix(shape, dim_fine, coarse_start, block_fine):
    fine = lax.broadcasted_iota(jnp.int32, shape, dim_fine)
    size = shape[dim_fine]
    fine = jnp.where(fine < (size + block_fine) // 2, fine, fine - size)
    whole = lax.broadcasted_iota(jnp.int32, shape, 1 - dim_fine)
    near = (fine >> 1) + coarse_start
    far = near + 2 * (fine & 1) - 1
    return jnp.where(whole == near, 0.75, jnp.where(whole == far, 0.25, 0.0))


def upward(index, e3, g2, k2, g1, k1, ends, scratch):
    v2, w2, d2, v1, w1, d1, fine2, fine1 = scratch
    shifts, w2, w1 = Open(), three(w2), three(w1)
    weigh(k2, *w2, 1, 11, 0.25**2, shifts, d2, inside, unroll=U2)
    weigh(k1, *w1, 5, 21, 0.25, shifts, d1, inside, unroll=U1)
    first_sweep(g2, d2, v2, 1, 11, U2)
    first_sweep(g1, d1, v1, 5, 21, U1)
    zero = jnp.zeros(d2.shape[1:], F32)
    for i, n in ((0, 0), (11, 1)):
        v2[i] = zero if ends is None else ends[n][0] * ends[n][1]
        d2[i] = zero if ends is None else ends[n][1]

    def use2(i, value):
        return jnp.where(d2[i] > 0.0, v2[i] + value, 0.0)

    py2 = spread_matrix((g2.shape[1], e3.shape[1]), 0, index[1] * 4, 8)
    pz2 = spread_matrix((e3.shape[2], g2.shape[2]), 1, index[2] * 16, 32)
    prolong(e3, index[0] * 2, 8, py2, pz2, fine2, use2, into(v2))
    smooth(v2, g2, d2, w2, 1, 11, shifts, unroll=U2)

    def use1(i, value):
        return jnp.where(d1[i + 5] > 0.0, v1[i + 5] + value, 0.0)

    py1, pz1 = prolongation((40, 24), Y1, Y2), prolongation((128, 128), Z2, Z1, True)
    prolong(v2, 1, 10, py1, pz1, fine1, use1, into(v1, 5))
    smooth(v1, g1, d1, w1, 6, 20, shifts, unroll=U1)
    return v1


BOTTOM = 14
UP = 8


def middle(nz, index, f, k, s, g2, k2, g1, k1, *refs):
    ends, (v, gn, turned, k3) = refs[:2], refs[2:6]
    low, mid, (fine0, r, held0, wx, wy, wz, d) = refs[6:20], refs[20:28], refs[28:]
    weigh(k, wx, wy, wz, 1, 25, 1.0, Open(), d, inside, unroll=U0)
    e3 = bottom(nz, s, k3, low)
    e1 = upward(index, e3, g2, k2, g1, k1, ends, mid)
    w, shifts = (wx, wy, wz), Open()

    def use(i, value):
        return inside(k[i + 1], f[i + 1] * d[i + 1] + value)

    py0, pz0 = prolongation((48, 40), Y0, Y1), prolongation((128, 256), Z1, Z0, True)
    prolong(e1, 6, 14, py0, pz0, fine0, use, into(v, 1))
    smooth(v, f, d, w, 2, 24, shifts, unroll=U0)
    smooth(v, f, d, w, 3, 23, shifts, unroll=U0)
    residual_of(v, f, r, w, 4, 22, shifts, k, unroll=U0)
    ry, rz = restriction((16, 48), span(16), Y0), restriction((256, 128), Z0, Z1, True)
    value = restrict(r, 5, 0, 8, ry, rz, held0)
    gn[...] = value.reshape(gn.shape)
    turned[...] = pltpu.roll(value, 64, 1).reshape(gn.shape)


def final(nz, index, f, k, v0, s, g2, k2, g1, k1, *refs):
    k3, (solution_, residual_) = refs[0], refs[1:3]
    low, mid, (fine0, wx, wy, wz, d, v) = refs[3:17], refs[17:25], refs[25:]
    weigh(k, wx, wy, wz, 3, 22, 1.0, Open(), d, inside, unroll=U0)
    e3 = bottom(nz, s, k3, low)
    e1 = upward(index, e3, g2, k2, g1, k1, None, mid)
    w, shifts = (wx, wy, wz), Open()

    def use(i, value):
        return inside(k[i + 3], v0[i + 3] + value)

    py0, pz0 = prolongation((48, 40), Y0, Y1), prolongation((128, 256), Z1, Z0, True)
    prolong(e1, 7, 12, py0, pz0, fine0, use, into(v, 3))
    smooth(v, f, d, w, 4, 22, shifts, unroll=U0)

    def last(i, here, im):
        return here[:32, :128], (f[i] - im)[:32, :128]

    def out(i, values):
        solution_[i - 5], residual_[i - 5] = values

    image(v, *w, 5, 21, last, out, shifts, unroll=U0)


def call(kernel, outs, scratch, *args, name, scalars=0, room=4):
    vmem = pl.BlockSpec(memory_space=pltpu.VMEM)
    smem = pl.BlockSpec(memory_space=pltpu.SMEM)
    return pl.pallas_call(
        kernel,
        out_shape=[jax.ShapeDtypeStruct(o, F32) for o in outs],
        in_specs=[smem] * scalars + [vmem] * (len(args) - scalars),
        out_specs=[vmem] * len(outs),
        scratch_shapes=[pltpu.VMEM(s, F32) for s in scratch],
        compiler_params=pltpu.CompilerParams(vmem_limit_bytes=room << 20),
        name=name,
    )(*args)


def neighbours(last, initial, axis):
    count = lax.axis_size(axis)
    if axis == "gz":
        up = [(i, (i + 1) % count) for i in range(count)]
    else:
        up = [(i, i + 1) for i in range(count - 1)]
    down = [(j, i) for i, j in up]
    before = lax.ppermute(last, axis, up)
    after = lax.ppermute(initial, axis, down)
    if axis == "gz":
        at = lax.axis_index(axis)
        before = jnp.where(at == 0, 0.0, before)
        after = jnp.where(at == count - 1, 0.0, after)
    return before, after


def finest(fields):
    for axis, dim, size, count, width in (("gz", 2, 128, 256, 25), ("gy", 1, 32, 48, 5)):
        along = 2 if dim == 2 else 0
        last = [lax.slice_in_dim(v, size - width, size, axis=dim) for v in fields]
        initial = [lax.slice_in_dim(v, 0, width, axis=dim) for v in fields]
        before, after = neighbours(
            jnp.concatenate(last, along), jnp.concatenate(initial, along), axis
        )
        before, after = jnp.split(before, 2, along), jnp.split(after, 2, along)
        gap = list(fields[0].shape)
        gap[dim] = count - size - 2 * width
        gap = jnp.zeros(gap, F32)
        fields = [
            jnp.concatenate([v, a, gap, b], dim) for b, v, a in zip(before, fields, after)
        ]
    f, k = fields
    lane = jnp.arange(128)
    ours = (lane < 25) | (lane >= 103)

    def packed(at, shift):
        start = at + shift
        tail = jnp.pad(f[start : start + 4, :, 128:], ((shift, 1 - shift), (0, 0), (0, 0)))
        tail = jnp.where(ours, tail, jnp.roll(k[at : at + 5, :, 128:], 50, 2))
        return jnp.concatenate([f[start : start + 4, :, :128], k[at : at + 5, :, :128], tail])

    before, after = neighbours(packed(11, 1), packed(0, 0), "gx")
    return before, f, k, after


def rows1(values):
    before, after = neighbours(values, values, "gy")
    gap = jnp.zeros((values.shape[0], 2, 128), F32)
    return jnp.concatenate([values, after[:, :11], gap, before[:, 5:]], 1)


def lanes1(values, turned):
    before, after = neighbours(turned, turned, "gz")
    lane = jnp.arange(128)
    zero = jnp.where(lane >= 117, before, 0.0)
    return jnp.where(lane < 64, values, jnp.where(lane < 75, after, zero))


def everyone(pieces, axes):
    return lax.all_to_all(pieces, axes, 0, 0)


def body(right_side, conductivity):
    nx, ny, nz = (lax.axis_size(axis) for axis in ("gx", "gy", "gz"))
    index = jnp.stack([lax.axis_index(axis) for axis in ("gx", "gy", "gz")]).astype(jnp.int32)

    wide, l1, l2 = (26, 48, 256), (26, 40, 128), (12, 24, 128)
    n3, n4 = (2 * nx + 6, 4 * ny, 128), (nx + 2, 2 * ny, 128)
    low = [
        n3, n3, n3, (3,) + n3, n3, n3,
        n4, (nx, 2 * ny, 128), n4, (3,) + n4, n4, n4,
        (nx * 2 * ny, 128), (nx + 2, 4 * ny, 128),
    ]
    mid = [l2, (3,) + l2, l2, l1, (3,) + l1, l1, (8, 24, 128), (10, 40, 128)]
    tiles = nx // 8

    right_side, conductivity, index = lax.optimization_barrier((right_side, conductivity, index))
    f, k, both1 = call(
        down0, [wide] * 2 + [(20, 16, 128)], [wide] * 6 + [(160, 256)],
        *finest([right_side, conductivity]), name="down0", room=14,
    )
    own = rows1(both1)
    last = jnp.concatenate([own[0:9], own[10:19]])
    initial = jnp.concatenate([own[1:10], own[11:20]])
    before, after = neighbours(last, initial, "gx")
    inner = [l1, l1, (288, 128), (3,) + l1, l1, l2, l2, (3,) + l2, l2]
    pair = (2, 24, 128)
    pieces, g1, k1, g2, k2, below, above = call(
        functools.partial(descend, True), [(nx, 8, 128), l1, l1, l2, l2, pair, pair], inner,
        before, own, after, name="descend", room=10,
    )
    pieces = everyone(pieces, "gx")
    (pieces,) = call(repack, [(ny * nz, 2 * tiles, 8, 128)], [], pieces, name="repack")
    outer = neighbours(below, above, "gx")
    s = everyone(pieces, ("gy", "gz"))
    v, value, turned, k3 = call(
        functools.partial(middle, nz), [wide, (8, 16, 128), (8, 16, 128), n3],
        low + mid + [(14, 48, 256), wide, (128, 256)] + [wide] * 4,
        index, f, k, s, g2, k2, g1, k1, *outer, name="middle", room=20, scalars=1,
    )
    own = rows1(lanes1(value, turned))
    before, after = neighbours(own, own, "gx")
    pieces, g1, g2 = call(
        functools.partial(descend, False), [(nx, 8, 128), l1, l2], inner,
        before, own, after, k1, k2, name="again", room=10,
    )
    pieces = everyone(pieces, "gx")
    (pieces,) = call(repack, [(ny * nz, tiles, 8, 128)], [], pieces, name="repack2")
    s = everyone(pieces, ("gy", "gz"))
    return tuple(call(
        functools.partial(final, nz), [(16, 32, 128)] * 2,
        low + mid + [(12, 48, 256)] + [wide] * 5,
        index, f, k, v, s, g2, k2, g1, k1, k3, name="final", room=20, scalars=1,
    ))


def solution(mesh):
    placed = P("gx", "gy", "gz")
    return jax.shard_map(
        body, mesh=mesh, in_specs=(placed, placed), out_specs=(placed, placed), check_vma=False
    )
```

```python
import functools

import jax
import jax.numpy as jnp
from jax import lax
from jax.experimental import pallas as pl
from jax.experimental.pallas import tpu as pltpu
from jax.sharding import PartitionSpec as P

LEVELS = 4
CSWEEPS = 6
absorption = 0.01
relaxation = 0.8
F32 = jnp.float32


def ring(n, b):
    return lambda at: jnp.where(at < (n + b) // 2, at, at - n)


def span(count, away=-1000, start=0):
    return lambda at: jnp.where((at >= start) & (at < start + count), at - start, away)


def matrix(shape, rows, columns, turned, values):
    a = rows(lax.broadcasted_iota(jnp.int32, shape, 0))
    b = columns(lax.broadcasted_iota(jnp.int32, shape, 1))
    return values(b, a) if turned else values(a, b)


def restriction(shape, rows, columns, turned=False):
    def values(coarse, fine):
        gap = fine - 2 * coarse
        outer, inner = (gap == -1) | (gap == 2), (gap == 0) | (gap == 1)
        return jnp.where(outer, 0.125, jnp.where(inner, 0.375, 0.0))

    return matrix(shape, rows, columns, turned, values)


def halving(shape, rows, columns, turned=False):
    def values(coarse, fine):
        return jnp.where((fine >> 1) == coarse, 0.5, 0.0)

    return matrix(shape, rows, columns, turned, values)


def prolongation(shape, rows, columns, turned=False):
    def values(fine, coarse):
        near = (fine >> 1) == coarse
        far = (fine >> 1) + 2 * (fine & 1) - 1 == coarse
        return jnp.where(near, 0.75, jnp.where(far, 0.25, 0.0))

    return matrix(shape, rows, columns, turned, values)


Y0, Z0, Y1, Z1, Y2, Z2 = ring(48, 32), ring(256, 128), ring(40, 16), ring(128, 64), ring(24, 8), ring(128, 32)


def parts(v):
    high = v.astype(jnp.bfloat16)
    rest = v - high.astype(F32)
    middle = rest.astype(jnp.bfloat16)
    return high, middle, (rest - middle.astype(F32)).astype(jnp.bfloat16)


def product(a, b):
    return lax.dot_general(a, b, (((1,), (0,)), ((), ())), preferred_element_type=F32)


def dot_left(m, v):
    m = m.astype(jnp.bfloat16)
    high, middle, low = (product(m, part) for part in parts(v))
    return high + (middle + low)


def dot_right(v, m):
    m = m.astype(jnp.bfloat16)
    high, middle, low = (product(part, m) for part in parts(v))
    return high + (middle + low)


def planes(lo, hi, step, carry=0, unroll=1):
    whole = (hi - lo) // unroll
    if whole > 1:
        carry = lax.fori_loop(0, whole, lambda t, c: step(lo + t * unroll, unroll, c), carry)
    elif whole == 1:
        carry = step(lo, unroll, carry)
    rest = (hi - lo) % unroll
    return step(hi - rest, rest, carry) if rest else carry


class Open:
    def above(self, v, dim):
        return pltpu.roll(v, v.shape[dim] - 1, dim)

    def below(self, v, dim):
        return pltpu.roll(v, 1, dim)

    def closed(self, k):
        return None


class Closed(Open):
    def __init__(self, shape, counts):
        self.last, self.first = [], []
        for dim in range(2):
            at = lax.broadcasted_iota(jnp.int32, shape, dim)
            self.last.append(jnp.where(at == counts[dim] - 1, 0.0, 1.0))
            self.first.append(jnp.where(at == 0, 0.0, 1.0))

    def above(self, v, dim):
        return super().above(v, dim) * self.last[dim]

    def below(self, v, dim):
        return super().below(v, dim) * self.first[dim]

    def closed(self, k):
        return k * ((1.0 - self.first[0]) + (1.0 - self.first[1]))


def weigh(k, wx, wy, wz, lo, hi, factor, shifts, d=None, mask=None, b=None, unroll=1):
    half = 0.5 * factor
    first = half * (k[lo - 1] + k[lo])
    wx[lo - 1] = first

    def step(i, n, below):
        here = [k[i + j] for j in range(n + 1)]
        outs = []
        for j in range(n):
            x = half * (here[j] + here[j + 1])
            y = half * (here[j] + shifts.above(here[j], 0))
            z = half * (here[j] + shifts.above(here[j], 1))
            ends, value = shifts.closed(half * here[j]), None
            if d is not None:
                value = (x + below) + (y + shifts.below(y, 0)) + (z + shifts.below(z, 1))
                if ends is not None:
                    value = value + ends
                value = relaxation / (value + absorption)
                if mask is not None:
                    value = mask(here[j], value)
            outs.append((x, y, z, ends, value))
            below = x
        for j, (x, y, z, ends, value) in enumerate(outs):
            wx[i + j], wy[i + j], wz[i + j] = x, y, z
            if ends is not None:
                b[i + j] = ends
            if value is not None:
                d[i + j] = value
        return below

    planes(lo, hi, step, first, unroll)


def image(v, wx, wy, wz, lo, hi, use, put, shifts, b=None, unroll=1):
    def step(i, n, below):
        here = [v[i + j] for j in range(n + 1)]
        outs = []
        for j in range(n):
            x = wx[i + j] * (here[j] - here[j + 1])
            y = wy[i + j] * (here[j] - shifts.above(here[j], 0))
            z = wz[i + j] * (here[j] - shifts.above(here[j], 1))
            total = (x - below) + (y - shifts.below(y, 0)) + (z - shifts.below(z, 1))
            if b is not None:
                total = total + b[i + j] * here[j]
            outs.append(use(i + j, here[j], total + absorption * here[j]))
            below = x
        for j, value in enumerate(outs):
            put(i + j, value)
        return below

    planes(lo, hi, step, wx[lo - 1] * (v[lo - 1] - v[lo]), unroll)


def into(ref, by=0):
    def put(i, value):
        ref[i + by] = value

    return put


def smooth(v, f, d, w, lo, hi, shifts, b=None, unroll=1, by=0):
    def use(i, here, im):
        return here + d[i] * (f[i + by] - im)

    image(v, *w, lo, hi, use, into(v), shifts, b, unroll)


def residual_of(v, f, r, w, lo, hi, shifts, mask=None, b=None, unroll=1):
    def use(i, here, im):
        value = f[i] - im
        return value if mask is None else jnp.where(mask[i] > 0.0, value, 0.0)

    image(v, *w, lo, hi, use, into(r), shifts, b, unroll)


def first_sweep(g, d, v, lo, hi, unroll, by=0):
    def step(i, n, carry):
        values = [g[i + j + by] * d[i + j] for j in range(n)]
        for j, value in enumerate(values):
            v[i + j] = value
        return carry

    planes(lo, hi, step, unroll=unroll)


def restrict(r, offset, lo, hi, ry, rz, held):
    size = ry.shape[0]
    for i in range(lo, hi):
        at = 2 * i + offset
        plane = 0.125 * (r[at - 1] + r[at + 2]) + 0.375 * (r[at] + r[at + 1])
        held[(i - lo) * size : (i - lo + 1) * size, :] = dot_left(ry, plane)
    return dot_right(held[: (hi - lo) * size, :], rz)


def halve(k, offset, lo, hi, cy, cz, held):
    size = cy.shape[0]
    for i in range(lo, hi):
        plane = 0.5 * (k[2 * i + offset] + k[2 * i + 1 + offset])
        held[(i - lo) * size : (i - lo + 1) * size, :] = dot_left(cy, plane)
    return dot_right(held[: (hi - lo) * size, :], cz)


def prolong(e, first, count, py, pz, finer, use, put):
    rows = e.shape[1]
    spread = dot_right(e[pl.ds(first, count)].reshape(count * rows, e.shape[2]), pz)
    for i in range(count):
        finer[i] = dot_left(py, spread[i * rows : (i + 1) * rows])

    def step(i, n, carry):
        held = [finer[i - 1 + j] for j in range(n + 2)]
        outs = []
        for j in range(n):
            here = 0.75 * held[j + 1]
            outs.append(use(2 * (i + j - 1), here + 0.25 * held[j]))
            outs.append(use(2 * (i + j - 1) + 1, here + 0.25 * held[j + 2]))
        for j, value in enumerate(outs):
            put(2 * (i - 1) + j, value)
        return carry

    planes(1, count - 1, step, unroll=max(1, 60 // (finer.shape[1] * finer.shape[2] // 1024)))


def three(w):
    return tuple(w.at[i] for i in range(3))


def inside(k, value):
    return jnp.where(k > 0.0, value, 0.0)


U0, U1, U2, U3 = 6, 12, 10, 32


def place(target, at, source, start, count, unroll=4):
    def step(i, n, carry):
        values = [source[start + i + j] for j in range(n)]
        for j, value in enumerate(values):
            target[at + i + j] = value
        return carry

    planes(0, count, step, unroll=unroll)


def down0(before, fo, ko, after, f, k, out, wx, wy, wz, d, v, r, held):
    shifts = Open()
    place(f, 5, fo, 0, 16)
    place(k, 5, ko, 0, 16)
    lane = lax.broadcasted_iota(jnp.int32, (48, 128), 1)
    ours = (lane < 25) | (lane >= 103)
    f[0] = f[25] = jnp.zeros((48, 256), F32)
    for ref, at, shift in ((before, 0, 1), (after, 21, 0)):
        for j in range(5):
            tail = ref[9 + j]
            k[at + j, :, :128] = ref[4 + j]
            k[at + j, :, 128:] = jnp.where(ours, pltpu.roll(tail, 78, 1), 0.0)
            if 0 <= j - shift < 4:
                f[at + j, :, :128] = ref[j - shift]
                f[at + j, :, 128:] = jnp.where(ours, tail, 0.0)
    weigh(k, wx, wy, wz, 1, 25, 1.0, shifts, d, inside, unroll=U0)
    first_sweep(f, d, v, 1, 25, U0)
    residual_of(v, f, r, (wx, wy, wz), 2, 24, shifts, k, unroll=U0)
    ry, rz = restriction((16, 48), span(16), Y0), restriction((256, 128), Z0, Z1, True)
    out[:10] = restrict(r, 5, -1, 9, ry, rz, held).reshape(10, 16, 128)
    cy, cz = halving((16, 48), span(16), Y0), halving((256, 128), Z0, Z1, True)
    out[10:] = halve(k, 5, -1, 9, cy, cz, held).reshape(10, 16, 128)


def descend(first, *refs):
    shifts = Open()
    before, own, after = refs[:3]
    if first:
        out, g1, k1, g2, k2, below, above = refs[3:10]
        for ref, at in ((g1, 0), (k1, 1)):
            place(ref, 0, before, 9 * at, 9, 9)
            place(ref, 9, own, 10 * at + 1, 8, 8)
            place(ref, 17, after, 9 * at, 9, 9)
    else:
        k1, k2, out, g1, g2 = refs[3:8]
        zero = jnp.zeros(g1.shape[1:], F32)
        g1[0], g1[25] = zero, zero
        for ref, at in ((before, 1), (own, 9), (after, 17)):
            place(g1, at, ref, 0, 8, 8)
    v1, r1, held, w1, d1, v2, r2, w2, d2 = refs[-9:]
    w1, w2 = three(w1), three(w2)
    rows = g2.shape[1]
    weigh(k1, *w1, 1, 25, 0.25, shifts, d1, inside, unroll=U1)
    first_sweep(g1, d1, v1, 1, 25, U1)
    residual_of(v1, g1, r1, w1, 2, 24, shifts, d1, unroll=U1)
    zero = jnp.zeros(g2.shape[1:], F32)
    g2[0], g2[11] = zero, zero
    ry1, rz1 = restriction((24, 40), Y2, Y1), restriction((128, 128), Z1, Z2, True)
    g2[1:11] = restrict(r1, 9, -3, 7, ry1, rz1, held).reshape(10, rows, 128)
    if first:
        cy1, cz1 = halving((24, 40), Y2, Y1), halving((128, 128), Z1, Z2, True)
        k2[...] = halve(k1, 9, -4, 8, cy1, cz1, held).reshape(k2.shape)
    weigh(k2, *w2, 1, 11, 0.25**2, shifts, d2, inside, unroll=U2)
    if first:
        below[0], below[1], above[0], above[1] = g2[4], d2[4], g2[7], d2[7]
    first_sweep(g2, d2, v2, 1, 11, U2)
    residual_of(v2, g2, r2, w2, 3, 9, shifts, d2, unroll=U2)
    total = None
    for i in range(2):
        at = 2 * i + 4
        plane = 0.125 * (r2[at - 1] + r2[at + 2]) + 0.375 * (r2[at] + r2[at + 1])
        value = dot_left(restriction((8, 24), span(4, start=4 * i), Y2), plane)
        total = value if total is None else total + value
    tile = dot_right(total, restriction((128, 128), Z2, span(16), True))
    if first:
        part = [
            dot_left(halving((8, 24), span(4, start=4 * i), Y2), 0.5 * (k2[2 * i + 4] + k2[2 * i + 5]))
            for i in range(2)
        ]
        tile = tile + dot_right(part[0] + part[1], halving((128, 128), Z2, span(16, start=16), True))
    for i in range(out.shape[0]):
        out[i] = tile


def repack(s, out):
    tiles = 2 * s.shape[0] // 16
    lane = lax.broadcasted_iota(jnp.int32, (8, 128), 1) // 16
    row = lax.broadcasted_iota(jnp.int32, (8, 128), 0) // 4
    for field in range(out.shape[1] // tiles):
        for t in range(tiles):
            total = jnp.zeros((8, 128), F32)
            for half in range(2):
                for p in range(8):
                    plane = 16 * t + 8 * half + p
                    part = s[plane // 2]
                    if plane % 2 != half:
                        part = pltpu.roll(part, 4, 0)
                    if p != field:
                        part = pltpu.roll(part, (16 * (p - field)) % 128, 1)
                    total = jnp.where((lane == p) & (row == half), part, total)
            for i in range(out.shape[0]):
                out[i, field * tiles + t] = total


def unpack(s, first, tiles, nz, whole):
    lane = lax.broadcasted_iota(jnp.int32, (8, 128), 1) // 16
    for j in range(s.shape[0] // nz):
        for t in range(tiles):
            for p in range(8):
                total = jnp.zeros((8, 128), F32)
                for q in range(nz):
                    part = s[j * nz + q, first + t]
                    if p != q:
                        part = pltpu.roll(part, (16 * (q - p)) % 128, 1)
                    total = jnp.where(lane == q, part, total)
                whole[16 * t + p + 3, 4 * j : 4 * j + 4] = total[:4]
                whole[16 * t + p + 11, 4 * j : 4 * j + 4] = total[4:]


def bottom(nz, s, k3, scratch):
    g3, v3, r3, w3, d3, b3, k4, g4, v4, w4, d4, b4, held, fine4 = scratch
    n4 = g4.shape[0]
    lanes3, lanes4 = span(16 * nz, -3000), span(8 * nz, -9000)
    rows3, rows4 = span(g3.shape[1]), span(g4.shape[1])
    tall, wide = (g4.shape[1], g3.shape[1]), (128, 128)
    n3, two = 2 * n4, s.shape[1] == n4 // 4
    rows, lanes = g3.shape[1], g3.shape[2]
    zero = jnp.zeros((rows, lanes), F32)
    for i in (0, 1, 2, n3 + 3, n3 + 4, n3 + 5):
        v3[i], r3[i] = zero, zero
        if two:
            k3[i] = zero
    for ref in (k4, v4):
        for i in (0, n4 + 1):
            ref[i] = jnp.zeros(ref.shape[1:], F32)
    unpack(s, 0, n3 // 16, nz, g3)
    if two:
        unpack(s, n3 // 16, n3 // 16, nz, k3)
    cy3, cz3 = halving(tall, rows4, rows3), halving(wide, lanes3, lanes4, True)
    k4[1 : n4 + 1] = halve(k3, 3, 0, n4, cy3, cz3, held).reshape(g4.shape)
    shifts3 = Closed((rows, lanes), (rows, 16 * nz))
    shifts4 = Closed((k4.shape[1], lanes), (k4.shape[1], 8 * nz))
    w3, w4 = three(w3), three(w4)
    weigh(k3, *w3, 3, n3 + 3, 0.25**3, shifts3, d3, inside, b3, U3)
    weigh(k4, *w4, 1, n4 + 1, 0.25**4, shifts4, d4, inside, b4, U3)
    first_sweep(g3, d3, v3, 3, n3 + 3, U3)
    residual_of(v3, g3, r3, w3, 3, n3 + 3, shifts3, b=b3, unroll=U3)
    ry3, rz3 = restriction(tall, rows4, rows3), restriction(wide, lanes3, lanes4, True)
    g4[...] = restrict(r3, 3, 0, n4, ry3, rz3, held).reshape(g4.shape)
    first_sweep(g4, d4, v4, 1, n4 + 1, U3, by=-1)

    def turn(j, carry):
        smooth(v4, g4, d4, w4, 1, n4 + 1, shifts4, b4, n4, by=-1)
        return carry

    lax.fori_loop(0, CSWEEPS - 1, turn, 0)

    def use(i, value):
        return v3[i + 3] + value

    py3, pz3 = prolongation(tall[::-1], rows3, rows4), prolongation(wide, lanes4, lanes3, True)
    prolong(v4, 0, n4 + 2, py3, pz3, fine4, use, into(v3, 3))
    smooth(v3, g3, d3, w3, 3, n3 + 3, shifts3, b3, U3)
    return v3


def spread_matrix(shape, dim_fine, coarse_start, block_fine):
    fine = lax.broadcasted_iota(jnp.int32, shape, dim_fine)
    size = shape[dim_fine]
    fine = jnp.where(fine < (size + block_fine) // 2, fine, fine - size)
    whole = lax.broadcasted_iota(jnp.int32, shape, 1 - dim_fine)
    near = (fine >> 1) + coarse_start
    far = near + 2 * (fine & 1) - 1
    return jnp.where(whole == near, 0.75, jnp.where(whole == far, 0.25, 0.0))


def upward(index, e3, g2, k2, g1, k1, ends, scratch):
    v2, w2, d2, v1, w1, d1, fine2, fine1 = scratch
    shifts, w2, w1 = Open(), three(w2), three(w1)
    weigh(k2, *w2, 1, 11, 0.25**2, shifts, d2, inside, unroll=U2)
    weigh(k1, *w1, 5, 21, 0.25, shifts, d1, inside, unroll=U1)
    first_sweep(g2, d2, v2, 1, 11, U2)
    first_sweep(g1, d1, v1, 5, 21, U1)
    zero = jnp.zeros(d2.shape[1:], F32)
    for i, n in ((0, 0), (11, 1)):
        v2[i] = zero if ends is None else ends[n][0] * ends[n][1]
        d2[i] = zero if ends is None else ends[n][1]

    def use2(i, value):
        return jnp.where(d2[i] > 0.0, v2[i] + value, 0.0)

    py2 = spread_matrix((g2.shape[1], e3.shape[1]), 0, index[1] * 4, 8)
    pz2 = spread_matrix((e3.shape[2], g2.shape[2]), 1, index[2] * 16, 32)
    prolong(e3, index[0] * 2, 8, py2, pz2, fine2, use2, into(v2))
    smooth(v2, g2, d2, w2, 1, 11, shifts, unroll=U2)

    def use1(i, value):
        return jnp.where(d1[i + 5] > 0.0, v1[i + 5] + value, 0.0)

    py1, pz1 = prolongation((40, 24), Y1, Y2), prolongation((128, 128), Z2, Z1, True)
    prolong(v2, 1, 10, py1, pz1, fine1, use1, into(v1, 5))
    smooth(v1, g1, d1, w1, 6, 20, shifts, unroll=U1)
    return v1


BOTTOM = 14
UP = 8


def middle(nz, index, f, k, s, g2, k2, g1, k1, *refs):
    ends, (v, gn, turned, k3) = refs[:2], refs[2:6]
    low, mid, (fine0, r, held0, wx, wy, wz, d) = refs[6:20], refs[20:28], refs[28:]
    weigh(k, wx, wy, wz, 1, 25, 1.0, Open(), d, inside, unroll=U0)
    e3 = bottom(nz, s, k3, low)
    e1 = upward(index, e3, g2, k2, g1, k1, ends, mid)
    w, shifts = (wx, wy, wz), Open()

    def use(i, value):
        return inside(k[i + 1], f[i + 1] * d[i + 1] + value)

    py0, pz0 = prolongation((48, 40), Y0, Y1), prolongation((128, 256), Z1, Z0, True)
    prolong(e1, 6, 14, py0, pz0, fine0, use, into(v, 1))
    smooth(v, f, d, w, 2, 24, shifts, unroll=U0)
    smooth(v, f, d, w, 3, 23, shifts, unroll=U0)
    residual_of(v, f, r, w, 4, 22, shifts, k, unroll=U0)
    ry, rz = restriction((16, 48), span(16), Y0), restriction((256, 128), Z0, Z1, True)
    value = restrict(r, 5, 0, 8, ry, rz, held0)
    gn[...] = value.reshape(gn.shape)
    turned[...] = pltpu.roll(value, 64, 1).reshape(gn.shape)


def final(nz, index, f, k, v0, s, g2, k2, g1, k1, *refs):
    k3, (solution_, residual_) = refs[0], refs[1:3]
    low, mid, (fine0, wx, wy, wz, d, v) = refs[3:17], refs[17:25], refs[25:]
    weigh(k, wx, wy, wz, 3, 22, 1.0, Open(), d, inside, unroll=U0)
    e3 = bottom(nz, s, k3, low)
    e1 = upward(index, e3, g2, k2, g1, k1, None, mid)
    w, shifts = (wx, wy, wz), Open()

    def use(i, value):
        return inside(k[i + 3], v0[i + 3] + value)

    py0, pz0 = prolongation((48, 40), Y0, Y1), prolongation((128, 256), Z1, Z0, True)
    prolong(e1, 7, 12, py0, pz0, fine0, use, into(v, 3))
    smooth(v, f, d, w, 4, 22, shifts, unroll=U0)

    def last(i, here, im):
        return here[:32, :128], (f[i] - im)[:32, :128]

    def out(i, values):
        solution_[i - 5], residual_[i - 5] = values

    image(v, *w, 5, 21, last, out, shifts, unroll=U0)


def call(kernel, outs, scratch, *args, name, scalars=0, room=4):
    vmem = pl.BlockSpec(memory_space=pltpu.VMEM)
    smem = pl.BlockSpec(memory_space=pltpu.SMEM)
    return pl.pallas_call(
        kernel,
        out_shape=[jax.ShapeDtypeStruct(o, F32) for o in outs],
        in_specs=[smem] * scalars + [vmem] * (len(args) - scalars),
        out_specs=[vmem] * len(outs),
        scratch_shapes=[pltpu.VMEM(s, F32) for s in scratch],
        compiler_params=pltpu.CompilerParams(vmem_limit_bytes=room << 20),
        name=name,
    )(*args)


def neighbours(last, initial, axis):
    count = lax.axis_size(axis)
    if axis == "gz":
        up = [(i, (i + 1) % count) for i in range(count)]
    else:
        up = [(i, i + 1) for i in range(count - 1)]
    down = [(j, i) for i, j in up]
    before = lax.ppermute(last, axis, up)
    after = lax.ppermute(initial, axis, down)
    if axis == "gz":
        at = lax.axis_index(axis)
        before = jnp.where(at == 0, 0.0, before)
        after = jnp.where(at == count - 1, 0.0, after)
    return before, after


def finest(fields):
    for axis, dim, size, count, width in (("gz", 2, 128, 256, 25), ("gy", 1, 32, 48, 5)):
        along = 2 if dim == 2 else 0
        last = [lax.slice_in_dim(v, size - width, size, axis=dim) for v in fields]
        initial = [lax.slice_in_dim(v, 0, width, axis=dim) for v in fields]
        before, after = neighbours(
            jnp.concatenate(last, along), jnp.concatenate(initial, along), axis
        )
        before, after = jnp.split(before, 2, along), jnp.split(after, 2, along)
        gap = list(fields[0].shape)
        gap[dim] = count - size - 2 * width
        gap = jnp.zeros(gap, F32)
        fields = [
            jnp.concatenate([v, a, gap, b], dim) for b, v, a in zip(before, fields, after)
        ]
    f, k = fields
    lane = jnp.arange(128)
    ours = (lane < 25) | (lane >= 103)

    def packed(at, shift):
        start = at + shift
        tail = jnp.pad(f[start : start + 4, :, 128:], ((shift, 1 - shift), (0, 0), (0, 0)))
        tail = jnp.where(ours, tail, jnp.roll(k[at : at + 5, :, 128:], 50, 2))
        return jnp.concatenate([f[start : start + 4, :, :128], k[at : at + 5, :, :128], tail])

    before, after = neighbours(packed(11, 1), packed(0, 0), "gx")
    return before, f, k, after


def rows1(values):
    before, after = neighbours(values, values, "gy")
    gap = jnp.zeros((values.shape[0], 2, 128), F32)
    return jnp.concatenate([values, after[:, :11], gap, before[:, 5:]], 1)


def lanes1(values, turned):
    before, after = neighbours(turned, turned, "gz")
    lane = jnp.arange(128)
    zero = jnp.where(lane >= 117, before, 0.0)
    return jnp.where(lane < 64, values, jnp.where(lane < 75, after, zero))


def everyone(pieces, axes):
    return lax.all_to_all(pieces, axes, 0, 0)


def body(right_side, conductivity):
    nx, ny, nz = (lax.axis_size(axis) for axis in ("gx", "gy", "gz"))
    index = jnp.stack([lax.axis_index(axis) for axis in ("gx", "gy", "gz")]).astype(jnp.int32)

    wide, l1, l2 = (26, 48, 256), (26, 40, 128), (12, 24, 128)
    n3, n4 = (2 * nx + 6, 4 * ny, 128), (nx + 2, 2 * ny, 128)
    low = [
        n3, n3, n3, (3,) + n3, n3, n3,
        n4, (nx, 2 * ny, 128), n4, (3,) + n4, n4, n4,
        (nx * 2 * ny, 128), (nx + 2, 4 * ny, 128),
    ]
    mid = [l2, (3,) + l2, l2, l1, (3,) + l1, l1, (8, 24, 128), (10, 40, 128)]
    tiles = nx // 8

    right_side, conductivity, index = lax.optimization_barrier((right_side, conductivity, index))
    f, k, both1 = call(
        down0, [wide] * 2 + [(20, 16, 128)], [wide] * 6 + [(160, 256)],
        *finest([right_side, conductivity]), name="down0", room=14,
    )
    own = rows1(both1)
    last = jnp.concatenate([own[0:9], own[10:19]])
    initial = jnp.concatenate([own[1:10], own[11:20]])
    before, after = neighbours(last, initial, "gx")
    inner = [l1, l1, (288, 128), (3,) + l1, l1, l2, l2, (3,) + l2, l2]
    pair = (2, 24, 128)
    pieces, g1, k1, g2, k2, below, above = call(
        functools.partial(descend, True), [(nx, 8, 128), l1, l1, l2, l2, pair, pair], inner,
        before, own, after, name="descend", room=10,
    )
    pieces = everyone(pieces, "gx")
    (pieces,) = call(repack, [(ny * nz, 2 * tiles, 8, 128)], [], pieces, name="repack")
    outer = neighbours(below, above, "gx")
    s = everyone(pieces, ("gy", "gz"))
    v, value, turned, k3 = call(
        functools.partial(middle, nz), [wide, (8, 16, 128), (8, 16, 128), n3],
        low + mid + [(14, 48, 256), wide, (128, 256)] + [wide] * 4,
        index, f, k, s, g2, k2, g1, k1, *outer, name="middle", room=20, scalars=1,
    )
    own = rows1(lanes1(value, turned))
    before, after = neighbours(own, own, "gx")
    pieces, g1, g2 = call(
        functools.partial(descend, False), [(nx, 8, 128), l1, l2], inner,
        before, own, after, k1, k2, name="again", room=10,
    )
    pieces = everyone(pieces, "gx")
    (pieces,) = call(repack, [(ny * nz, tiles, 8, 128)], [], pieces, name="repack2")
    s = everyone(pieces, ("gy", "gz"))
    return tuple(call(
        functools.partial(final, nz), [(16, 32, 128)] * 2,
        low + mid + [(12, 48, 256)] + [wide] * 5,
        index, f, k, v, s, g2, k2, g1, k1, k3, name="final", room=20, scalars=1,
    ))


def solution(mesh):
    placed = P("gx", "gy", "gz")
    return jax.shard_map(
        body, mesh=mesh, in_specs=(placed, placed), out_specs=(placed, placed), check_vma=False
    )
```
